32 devices in a mesh: grp: 2 (over y), hh: 4 (over z), per: 2 (over x), st: 2 (over core).
Axes of the slice: x: 2, y: 2, z: 4, core: 2. Of those that a mesh axis runs over, the one named last changes fastest.
Arguments:
- earnings: float32 [3072, 16], P(('hh', 'per')), may hold values from -5.4 to 5.4
- starts: int32 [3072], P(('hh', 'per')), may hold values from 0 to 12, as said below
- lengths: int32 [3072], P(('hh', 'per')), may hold values from 4 to 16
- block_count: int32 [8], P(('hh', 'per')), may hold values from 0 to 3, as said below
- trans_logits: bfloat16 [32, 256, 256], P(('grp', 'per', 'st')), parts along dimension 0, may hold values from -4 to 4
- init_logits: float32 [512], P('grp'), parts along dimension 0, may hold values from -4 to 4
- state_mean: float32 [512], P('grp'), parts along dimension 0, may hold values from -4 to 4
- log_sd: float32 [512], P('grp'), parts along dimension 0, may hold values from 0 to 1
Outputs:
- trans_grad: float32 [32, 256, 256], P(('grp', 'per'), 'hh', 'st'), parts along dimension 0
- mean_loglik: float32 [2], P('grp'), parts along dimension 0
The draws below stay inside these ranges and needn't reach their ends.
There are 2 independent parts, one for each index of `grp`. The reference program is written for one: setup_inputs(seed, part) draws one part's arguments, and reference() takes and returns one part's arrays. A program takes and returns all parts, laid end to end along the dimension named above; an argument that names none is the same for every part. Nothing has to cross between parts.
Inputs may be any that keep to these rules, and one draw needn't show every extreme that they name: starts[h] + lengths[h] <= 16. Exactly 1 device hold 3 blocks and as many hold 2; the counts sum to 8. Only the first block_count[d] blocks of device d's 3 slots hold households; the entries of the other slots are to be ignored.
All inputs are finite; a program needn't handle non-finite values.
Results may differ from the reference program's by a relative error of at most 0.00055.
Values may be sent and summed in bfloat16 or wider, within the bound.
A program may use at most 64 MiB of HBM per device.

```python
import jax
import jax.numpy as jnp
from jax import lax

S = 256
NT = 16
HB = 128
CAP = 3
ND = 8


def draw_earnings(key, part):
    row_count = CAP * HB * ND
    slot_ids = jnp.arange(row_count, dtype=jnp.int32)
    device_ids = slot_ids // (CAP * HB)
    cycle_pos = slot_ids % (CAP * HB) % ND
    level_exp = (device_ids + cycle_pos).astype(jnp.float32) / ND
    row_scale = 0.3 * 3.0 ** level_exp
    base_draw = jnp.clip(jax.random.normal(key, (row_count, NT), jnp.float32), -2.0, 2.0)
    return base_draw * row_scale[:, None]


def household_times(key):
    row_count = CAP * HB * ND
    slot_ids = jnp.arange(row_count, dtype=jnp.int32)
    span_len = jax.random.randint(jax.random.fold_in(key, 101), (row_count,), 4, NT + 1)
    span_len = jnp.where(slot_ids == 0, NT, jnp.where(slot_ids == 1, 4, span_len))
    raw_bits = jax.random.randint(jax.random.fold_in(key, 202), (row_count,), 0, 1 << 20)
    begin_at = raw_bits % (NT - span_len + 1)
    begin_at = jnp.where(slot_ids == 1, NT - 4, begin_at)
    return (begin_at.astype(jnp.int32), span_len.astype(jnp.int32))


def draw_starts(key, part):
    return household_times(key)[0]


def draw_lengths(key, part):
    return household_times(key)[1]


def draw_block_count(key, part):
    eighth = ND // 8
    rank_ids = jnp.arange(ND, dtype=jnp.int32)
    count_table = jnp.where(rank_ids < eighth, CAP, jnp.where(rank_ids < CAP * eighth, 0, jnp.where(rank_ids < CAP * eighth + eighth, 2, jnp.where(rank_ids < CAP * eighth + 2 * eighth, 0, 1))))
    shuffle = jax.random.permutation(key, ND)
    return count_table[shuffle].astype(jnp.int32)


def block_levels(rng, shape, split, smallest, largest):
    def one(axis_at, blocks):
        steps = jax.random.uniform(jax.random.fold_in(jax.random.fold_in(rng, 6), axis_at), (blocks,), jnp.float32, smallest / len(split), largest / len(split))
        return jnp.repeat(jnp.exp(steps), shape[axis_at] // blocks).reshape((-1,) + (1,) * (len(shape) - axis_at - 1))

    level = one(*split[0])
    for cut in split[1:]:
        level = level * one(*cut)
    return level


def scatter_about(stream_key, extent, deviation, most, pieces=(), kind=jnp.bfloat16):
    factor_of = block_levels(stream_key, extent, pieces, -0.22, 0.18) if pieces else 1.0
    result = jax.random.normal(stream_key, extent, jnp.float32) * deviation * factor_of
    return jnp.minimum(jnp.maximum(result, -most), most).astype(kind)


def setup_inputs(seed: int = 0, part: int = 0) -> dict:
    streams_of = jax.random.split(jax.random.key(seed), 9)
    part_splits = jax.random.split(jax.random.fold_in(streams_of[8], part), 9)
    return {
        "earnings": draw_earnings(jax.random.fold_in(streams_of[8], 71), part),
        "starts": draw_starts(jax.random.fold_in(streams_of[8], 71), part),
        "lengths": draw_lengths(jax.random.fold_in(streams_of[8], 71), part),
        "block_count": draw_block_count(jax.random.fold_in(streams_of[8], 71), part),
        "trans_logits": scatter_about(part_splits[4], (NT, S, S), 1.0, 4.0, ((0, 4),)),
        "init_logits": scatter_about(part_splits[5], (S,), 1.0, 4.0, (), jnp.float32),
        "state_mean": jnp.clip(jax.random.uniform(part_splits[6], (S,), jnp.float32, -4.0, 4.0), -4.0, 4.0),
        "log_sd": jnp.clip(jax.random.uniform(part_splits[7], (S,), jnp.float32, 0.0, 1.0), 0.0, 1.0),
    }


top_precision = lax.Precision.HIGHEST


def emission(column, state_mean, log_sd):
    z_score = (column[:, None] - state_mean[None, :]) / jnp.exp(log_sd)[None, :]
    return jnp.exp(-0.5 * z_score * z_score - log_sd[None, :])


def reference(earnings, starts, lengths, block_count, trans_logits, init_logits, state_mean, log_sd):
    raised = jnp.exp(trans_logits.astype(jnp.float32))
    probs = raised / jnp.sum(raised, axis=2, keepdims=True)
    raised_first = jnp.exp(init_logits)
    first_probs = raised_first / jnp.sum(raised_first)
    num_states = first_probs.shape[0]
    block_total = ND * CAP
    block_alive = (jnp.arange(block_total, dtype=jnp.int32) % CAP) < jnp.repeat(block_count, CAP)
    earn_blocks = earnings.reshape(block_total, HB, NT)
    start_blocks = starts.reshape(block_total, HB)
    length_blocks = lengths.reshape(block_total, HB)
    period_ids = jnp.arange(NT, dtype=jnp.int32)

    def block_terms(earn_rows, begin_at, span_len):
        def forward(prev_alpha, inputs):
            matrix, column, step_now = inputs
            moved_mass = jnp.dot(prev_alpha, matrix, precision=top_precision, preferred_element_type=jnp.float32)
            joint_mass = jnp.where((step_now <= begin_at)[:, None], first_probs[None, :], moved_mass) * emission(column, state_mean, log_sd)
            seen_now = (step_now >= begin_at) & (step_now < begin_at + span_len)
            scale_now = jnp.where(seen_now, jnp.sum(joint_mass, axis=1), 1.0)
            new_alpha = jnp.where(seen_now[:, None], joint_mass / scale_now[:, None], prev_alpha)
            return new_alpha, (new_alpha, scale_now)

        start_alpha = jnp.broadcast_to(first_probs[None, :], (HB, num_states))
        columns = earn_rows.T
        _, (alphas, scales) = lax.scan(forward, start_alpha, (probs, columns, period_ids))

        def carry_of(back_now, column, scale_now, step_now):
            seen_now = (step_now >= begin_at) & (step_now < begin_at + span_len)
            return jnp.where(seen_now[:, None], emission(column, state_mean, log_sd) * back_now / scale_now[:, None], 0.0)

        def backward(carry_now, inputs):
            matrix, alpha_prev, column_prev, scale_prev, step_now = inputs
            moving = (step_now > begin_at) & (step_now < begin_at + span_len)
            weights = jnp.where(moving[:, None], alpha_prev, 0.0)
            grad_term = jnp.dot(weights.T, carry_now, precision=top_precision, preferred_element_type=jnp.float32)
            back_now = jnp.where(moving[:, None], jnp.dot(carry_now, matrix.T, precision=top_precision, preferred_element_type=jnp.float32), 1.0)
            return carry_of(back_now, column_prev, scale_prev, step_now - 1), grad_term

        last_carry = carry_of(jnp.ones((HB, num_states), jnp.float32), columns[NT - 1], scales[NT - 1], NT - 1)
        _, grad_terms = lax.scan(backward, last_carry, (probs[1:], alphas[:-1], columns[:-1], scales[:-1], period_ids[1:]), reverse=True)
        return grad_terms, jnp.sum(jnp.log(scales)), jnp.sum(span_len).astype(jnp.float32)

    def accumulate(totals, inputs):
        earn_rows, begin_at, span_len, alive_now = inputs

        def take_block(operands):
            counts, loglik, years = totals
            grad_terms, part_loglik, part_years = block_terms(operands[0], operands[1], operands[2])
            return counts.at[1:].add(grad_terms), loglik + part_loglik, years + part_years

        def skip_block(operands):
            return totals

        return lax.cond(alive_now, take_block, skip_block, (earn_rows, begin_at, span_len)), None

    zero_totals = (jnp.zeros((NT, num_states, num_states), jnp.float32), jnp.zeros((), jnp.float32), jnp.zeros((), jnp.float32))
    (counts, loglik, years), _ = lax.scan(accumulate, zero_totals, (earn_blocks, start_blocks, length_blocks, block_alive))
    weighted = probs * counts
    row_total = jnp.sum(weighted, axis=2, keepdims=True)
    factor = float(num_states * num_states * NT) / years
    trans_grad = factor * (weighted - probs * row_total)
    mean_loglik = jnp.reshape(loglik / years, (1,))
    return trans_grad, mean_loglik
```

```python
import functools

import jax
import jax.numpy as jnp
from jax import lax
from jax.sharding import PartitionSpec as P
from jax.experimental import pallas as pl
from jax.experimental.pallas import tpu as pltpu

HB = 128


top_precision = lax.Precision.HIGHEST


def emission(column, state_mean, log_sd):
    z_score = (column[:, None] - state_mean[None, :]) / jnp.exp(log_sd)[None, :]
    return jnp.exp(-0.5 * z_score * z_score - log_sd[None, :])


def per_device(
    earnings, starts, lengths, block_count, trans_logits, init_logits, state_mean, log_sd
):
    num_states = init_logits.shape[0]
    num_periods = earnings.shape[1]
    slot_rows = earnings.shape[0]
    group_size = lax.axis_size(("hh", "per"))
    core_count = lax.axis_size("st")
    half_states = num_states // core_count
    lead_state = lax.axis_index("st") * half_states
    whole_logits = lax.all_gather(trans_logits, ("per", "st"), axis=0, tiled=True)
    raised = jnp.exp(whole_logits.astype(jnp.float32))
    trans_probs = raised / jnp.sum(raised, axis=2, keepdims=True)
    raised_first = jnp.exp(init_logits)
    first_probs = raised_first / jnp.sum(raised_first)
    source_rows = slot_rows // group_size
    count_out = jnp.broadcast_to(block_count.reshape(1, 1), (1, group_size))
    got_earn, got_start, got_len, got_count = (
        lax.all_to_all(
            earnings.reshape(source_rows, group_size, num_periods),
            ("hh", "per"),
            split_axis=1,
            concat_axis=1,
            tiled=True,
        ),
        lax.all_to_all(
            starts.reshape(source_rows, group_size),
            ("hh", "per"),
            split_axis=1,
            concat_axis=1,
            tiled=True,
        ),
        lax.all_to_all(
            lengths.reshape(source_rows, group_size),
            ("hh", "per"),
            split_axis=1,
            concat_axis=1,
            tiled=True,
        ),
        lax.all_to_all(count_out, ("hh", "per"), split_axis=1, concat_axis=1, tiled=True),
    )
    per_source = got_count[0] * (HB // group_size)
    source_order = jnp.arange(group_size, dtype=jnp.int32)
    up_to = source_order[None, :] <= source_order[:, None]
    ends_at = jnp.sum(jnp.where(up_to, per_source[None, :], 0), axis=1)
    target_ids = jnp.arange(HB, dtype=jnp.int32)
    before_mask = ends_at[None, :] <= target_ids[:, None]
    source_ids = jnp.sum(before_mask.astype(jnp.int32), axis=1)
    begins_at = jnp.sum(jnp.where(before_mask, per_source[None, :], 0), axis=1)
    pick_ids = (target_ids - begins_at) * group_size + source_ids
    rows_earn = jnp.take(got_earn.reshape(source_rows * group_size, num_periods), pick_ids, axis=0)
    rows_start = jnp.take(got_start.reshape(source_rows * group_size), pick_ids)
    rows_len = jnp.take(got_len.reshape(source_rows * group_size), pick_ids)
    row_live = jnp.ones((HB,), dtype=bool)
    years_local = jnp.sum(jnp.where(row_live, rows_len, 0)).astype(jnp.float32)
    row_total_count = rows_earn.shape[0]
    columns = rows_earn.T
    period_ids = jnp.arange(num_periods, dtype=jnp.int32)

    def observed(step_now):
        return row_live & (step_now >= rows_start) & (step_now < rows_start + rows_len)

    def forward(prev_alpha, inputs):
        matrix, column, step_now = inputs
        fresh_start = (step_now <= rows_start)[:, None]
        moved_mass = jnp.dot(
            prev_alpha, matrix, precision=top_precision, preferred_element_type=jnp.float32
        )
        joint_mass = jnp.where(fresh_start, first_probs[None, :], moved_mass) * emission(
            column, state_mean, log_sd
        )
        seen_now = observed(step_now)
        scale_now = jnp.where(seen_now, jnp.sum(joint_mass, axis=1), 1.0)
        new_alpha = jnp.where(seen_now[:, None], joint_mass / scale_now[:, None], prev_alpha)
        return (new_alpha, (new_alpha, scale_now))

    start_alpha = jnp.broadcast_to(first_probs[None, :], (row_total_count, num_states))
    _, (alphas, scales) = lax.scan(forward, start_alpha, (trans_probs, columns, period_ids))

    def carry_of(back_now, column, scale_now, step_now):
        seen_now = observed(step_now)
        return jnp.where(
            seen_now[:, None],
            emission(column, state_mean, log_sd) * back_now / scale_now[:, None],
            0.0,
        )

    def backward(carry_now, inputs):
        matrix, alpha_prev, column_prev, scale_prev, step_now = inputs
        moving = row_live & (step_now > rows_start) & (step_now < rows_start + rows_len)
        weights = jnp.where(moving[:, None], alpha_prev, 0.0)
        own_carry = lax.dynamic_slice_in_dim(carry_now, lead_state, half_states, 1)
        grad_term = lax.dot_general(
            weights,
            own_carry,
            (((0,), (0,)), ((), ())),
            precision=top_precision,
            preferred_element_type=jnp.float32,
        )
        pulled = lax.dot_general(
            carry_now,
            matrix,
            (((1,), (1,)), ((), ())),
            precision=top_precision,
            preferred_element_type=jnp.float32,
        )
        back_now = jnp.where(moving[:, None], pulled, 1.0)
        return (carry_of(back_now, column_prev, scale_prev, step_now - 1), grad_term)

    ones_back = jnp.ones((row_total_count, num_states), jnp.float32)
    last_carry = carry_of(
        ones_back, columns[num_periods - 1], scales[num_periods - 1], num_periods - 1
    )
    _, grad_terms = lax.scan(
        backward,
        last_carry,
        (trans_probs[1:], alphas[:-1], columns[:-1], scales[:-1], period_ids[1:]),
        reverse=True,
    )
    zero_first = jnp.zeros((1,) + grad_terms.shape[1:], jnp.float32)
    partial_counts = jnp.concatenate([zero_first, grad_terms], axis=0)
    loglik_local = jnp.sum(jnp.log(scales))
    summed = lax.psum_scatter(partial_counts, "hh", scatter_dimension=1, tiled=True)
    summed = lax.psum_scatter(summed, "per", scatter_dimension=0, tiled=True)
    loglik_share = loglik_local / core_count
    years_share = years_local / core_count
    period_block = summed.shape[0]
    row_block_size = summed.shape[1]
    local_probs = lax.dynamic_slice(
        trans_probs,
        (lax.axis_index("per") * period_block, lax.axis_index("hh") * row_block_size, lead_state),
        (period_block, row_block_size, half_states),
    )
    weighted = local_probs * summed
    row_total, loglik_core, years_core = lax.psum(
        (jnp.sum(weighted, axis=2), loglik_share, years_share), "st"
    )
    loglik_all, years_all = lax.psum((loglik_core, years_core), ("hh", "per"))
    factor = float(num_states * num_states * num_periods) / years_all
    trans_grad = factor * (weighted - local_probs * row_total[:, :, None])
    mean_loglik = jnp.reshape(loglik_all / years_all, (1,))
    return (trans_grad, mean_loglik)


F32 = jnp.float32
BF = jnp.bfloat16
MESH = pl.DeviceIdType.MESH
EXT = 16
LOG2E = 1.4426950408889634
NT_DIMS = (((1,), (1,)), ((), ()))


def dot(p, q):
    return jnp.dot(p, q, preferred_element_type=F32)


def dot_nt(p, q):
    return lax.dot_general(p, q, NT_DIMS, preferred_element_type=F32)


def fused_kernel(cfg, earn, begin, length, count, logits, init_ref, mean_ref, sd_ref, out, llout,
                 pack, got, people, span, lg, mats, cols, alph, back_u, emem, srow, svrow, yrow,
                 cacc, crecv, prb, llbox, ybox, rts, rtr,
                 hs_sem, hr_sem, lr_sem, ls_sem, xs_sem, xr_sem, cs_sem, cr_sem, r_sem, lls_sem, llr_sem, y_sem):
    nz, nt, half_t, own_t, num_states, groups, lanes = cfg
    x = lax.axis_index("per")
    z = lax.axis_index("hh")
    s = lax.axis_index("st")
    half = num_states // 2
    nsrc = nz * 2
    zr = num_states // nz
    tiles = groups * lanes // 128
    per_group = lanes // 128
    chunk = 64

    def rcopy(src, dst, ss, rs, dev):
        return pltpu.make_async_remote_copy(
            src_ref=src, dst_ref=dst, send_sem=ss, recv_sem=rs,
            device_id=dev, device_id_type=MESH)

    partner = {"hh": z, "per": x, "st": 1 - s}
    across = {"hh": z, "per": 1 - x, "st": s}
    corner = {"hh": z, "per": 1 - x, "st": 1 - s}
    peers = []
    for dz in range(nz):
        for dx in range(2):
            if dz or dx:
                px = x if dx == 0 else 1 - x
                peers.append((px, {"hh": lax.rem(z + dz, nz), "per": px, "st": s}))
    barrier = pltpu.get_barrier_semaphore()
    for dev in [d for _, d in peers] + [partner, corner]:
        pl.semaphore_signal(barrier, inc=1, device_id=dev, device_id_type=MESH)

    local = []
    for i in range(own_t):
        c = pltpu.make_async_copy(logits.at[i], lg.at[own_t * s + i], lr_sem.at[i])
        c.start()
        local.append(c)

    low = lax.broadcasted_iota(jnp.int32, (8, 128), 1) < 64
    first_core = s == 0

    def to_low(v):
        return jnp.where(first_core, v, pltpu.roll(v, 64, 1))

    def to_high(v):
        return jnp.where(first_core, pltpu.roll(v, 64, 1), v)

    cnt = count[0].astype(F32)
    about = jnp.concatenate(
        [begin[...].astype(F32), length[...].astype(F32), jnp.full((2, 128), 1.0, F32) * cnt], axis=0)
    about = to_high(about)
    for h in range(2):
        e = [earn[h * half_t:(h + 1) * half_t, b * 128:(b + 1) * 128] for b in range(3)]
        pack[h, :, 0:128] = jnp.where(low, to_low(e[0]), to_high(e[1]))
        pack[h, :, 128:256] = jnp.where(low, to_low(e[2]), about)

    mean = mean_ref[...]
    log_sd = sd_ref[...]
    raised_first = jnp.exp(init_ref[...])
    first = raised_first / jnp.sum(raised_first, axis=1, keepdims=True)
    slope = jnp.exp(-log_sd) * ((0.5 * LOG2E) ** 0.5)
    for i, v in enumerate([slope, slope * mean, log_sd * (-LOG2E), first]):
        cols[i] = jnp.broadcast_to(v, (128, num_states)).T
    ext_row = lax.broadcasted_iota(jnp.int32, (EXT, num_states), 0)
    ext = jnp.where(ext_row == 0, 1.0, jnp.where(ext_row == 1, jnp.broadcast_to(first, (EXT, num_states)), 0.0)).astype(BF)
    eye = jnp.where(lax.broadcasted_iota(jnp.int32, (num_states, num_states), 0)
                    == lax.broadcasted_iota(jnp.int32, (num_states, num_states), 1), 1.0, 0.0).astype(BF)

    pl.semaphore_wait(barrier, len(peers) + 2)
    me_src = z * 2 + x
    hist = []
    for n, (px, dev) in enumerate(peers):
        c = rcopy(pack.at[px], got.at[me_src], hs_sem.at[n], hr_sem.at[n], dev)
        c.start()
        hist.append(c)
    near = []
    for i in range(own_t):
        c = rcopy(logits.at[i], lg.at[own_t * s + i], ls_sem.at[i], lr_sem.at[own_t + i], partner)
        c.start()
        near.append(c)
    got[me_src] = pack[x]

    zrow = pl.ds(pl.multiple_of(z * zr, zr), zr)

    def make_probs(l):
        r = jnp.exp(lg[l].astype(F32))
        p = (r * (1.0 / jnp.sum(r, axis=1, keepdims=True))).astype(BF)
        mats[0, l, 0:EXT] = ext
        mats[1, l, 0:EXT] = ext
        mats[0, l, EXT:] = p
        mats[1, l, EXT:] = dot_nt(eye, p).astype(BF)
        rz = jnp.exp(lg[l, zrow, :].astype(F32))
        prb[l] = rz / jnp.sum(rz, axis=1, keepdims=True)

    for i in range(own_t):
        local[i].wait()

    @pl.loop(0, own_t)
    def _(i):
        make_probs(own_t * s + i)

    for i in range(own_t):
        near[i].wait_recv()

    @pl.loop(0, own_t)
    def _(i):
        make_probs(own_t * (1 - s) + i)

    for n in range(len(peers)):
        hist[n].wait_recv()

    high_bit = jnp.where(lax.broadcasted_iota(jnp.int32, (1, 128), 1) < 64, 0.0, 1.0)
    base = jnp.zeros((1, 128), F32)
    xs = [jnp.zeros((8, 128), F32) for _ in range(tiles)]
    starts = [jnp.zeros((1, 128), F32) for _ in range(tiles)]
    spans = [jnp.zeros((1, 128), F32) for _ in range(tiles)]
    for d in range(nsrc):
        t0, t1 = got[d, :, 0:128], got[d, :, 128:256]
        r0, r1 = pltpu.roll(t0, 64, 1), pltpu.roll(t1, 64, 1)
        held = [jnp.where(low, t0, r0), jnp.where(low, r0, t0), jnp.where(low, t1, r1)]
        about = jnp.where(low, r1, t1)
        live = about[6:7]
        for b in range(3):
            spot = jnp.where(live > float(b), base + float(b), -2.0) - high_bit
            for m in range(tiles):
                hit = spot == float(2 * m)
                xs[m] = jnp.where(hit, held[b], xs[m])
                starts[m] = jnp.where(hit, about[b:b + 1], starts[m])
                spans[m] = jnp.where(hit, about[3 + b:4 + b], spans[m])
        base = base + live
    years_own = jnp.zeros((1, 1), F32)
    for m in range(tiles):
        for t in range(half_t):
            people[t, m:m + 1, :] = xs[m][t:t + 1]
        span[0, m:m + 1, :] = starts[m]
        span[1, m:m + 1, :] = starts[m] + spans[m]
        years_own = years_own + jnp.sum(spans[m], axis=1, keepdims=True)
    ybox[0] = jnp.broadcast_to(years_own, (8, 128))
    yc = rcopy(ybox.at[0], ybox.at[1], y_sem.at[0], y_sem.at[1], partner)
    yc.start()

    def lane(m):
        return pl.ds(m * 128, 128)

    def start_of(m):
        return span[0, m:m + 1, :]

    def stop_of(m):
        return span[1, m:m + 1, :]

    def row(ref, l, m):
        return ref[l, m:m + 1, :]

    def chunks():
        for m in range(tiles):
            for r in range(0, num_states, chunk):
                yield m, m // per_group, pl.ds((m % per_group) * 128, 128), (m % per_group) * 128, r

    def fill_emission(l):
        for m in range(tiles):
            xrow = row(people, l, m)
            for r in range(0, num_states, chunk):
                rr = pl.ds(r, chunk)
                dev = cols[0, rr, :] * xrow - cols[1, rr, :]
                emem[l, rr, lane(m)] = jnp.exp2(cols[2, rr, :] - dev * dev)

    def per_tile(raws, i):
        return [raws[m // per_group][i:i + 1, (m % per_group) * 128:(m % per_group + 1) * 128] for m in range(tiles)]

    def piece(raws, g, c0, r):
        return raws[g][EXT + r:EXT + r + chunk, c0:c0 + 128]

    def store_rows(ref, l, vals):
        for m in range(tiles):
            ref[l, m:m + 1, :] = vals[m]

    def forward_step(l, t, raws, dst):
        sums = per_tile(raws, 0)
        inv = [1.0 / v for v in sums]
        fresh = [t <= start_of(m) for m in range(tiles)]
        for m, g, cc, c0, r in chunks():
            rr = pl.ds(r, chunk)
            moved = jnp.where(fresh[m], cols[3, rr, :], piece(raws, g, c0, r) * inv[m])
            alph[dst, g, rr, cc] = (moved * emem[l, rr, lane(m)]).astype(BF)
        return sums, inv

    def own_counts(l, raws):
        c = raws[0]
        for v in raws[1:]:
            c = c + v
        cacc[l, 0] = c[:, :half]
        cacc[l, 1] = c[:, half:]
        rcopy(cacc.at[l, 1 - s], crecv.at[l], cs_sem.at[l], cr_sem.at[l], partner).start()

    def cross(g):
        return rcopy(alph.at[half_t, g], alph.at[0, g], xs_sem.at[g], xr_sem.at[g], across)

    def junction():
        q = []
        for m in range(tiles):
            g, cc = m // per_group, pl.ds((m % per_group) * 128, 128)
            acc = jnp.zeros((chunk, 128), F32)
            for r in range(0, num_states, chunk):
                rr = pl.ds(r, chunk)
                acc = acc + alph[half_t, g, rr, cc].astype(F32) * alph[0, g, rr, cc].astype(F32)
            q.append(jnp.sum(acc, axis=0, keepdims=True))
        return q

    def put_ll():
        logs = jnp.zeros((tiles, 128), F32)
        for l in range(half_t):
            t = (x * half_t + l).astype(F32)
            seen = (t >= span[0]) & (t < span[1])
            logs = logs + jnp.where(seen, jnp.log(srow[l]), 0.0)
        total = jnp.sum(jnp.sum(logs, axis=0, keepdims=True), axis=1, keepdims=True)
        llbox[x * 2 + s] = jnp.broadcast_to(total, (8, 128))

    @pl.when(x == 0)
    def _early():
        fill_emission(0)
        for m, g, cc, c0, r in chunks():
            rr = pl.ds(r, chunk)
            alph[1, g, rr, cc] = (cols[3, rr, :] * emem[0, rr, lane(m)]).astype(BF)

        @pl.loop(1, half_t)
        def _(l):
            raws = [dot(mats[1, l], alph[l, g]) for g in range(groups)]
            fill_emission(l)
            sums, _ = forward_step(l, l.astype(F32), raws, l + 1)
            store_rows(srow, l - 1, sums)

        for g in range(groups):
            cross(g).start()
        cacc[0] = jnp.zeros(cacc.shape[1:], F32)
        rcopy(cacc.at[0, 1 - s], crecv.at[0], cs_sem.at[0], cr_sem.at[0], partner).start()
        last = [dot(ext, alph[half_t, g]) for g in range(groups)]
        store_rows(srow, half_t - 1, per_tile(last, 0))
        put_ll()
        srow_inv = 1.0 / srow[...]
        svrow[...] = srow_inv
        for g in range(groups):
            cross(g).wait()
        inv_q = [1.0 / v for v in junction()]

        def moving(t, m):
            return (t > start_of(m)) & (t < stop_of(m))

        def put_u(l, t, get):
            for m in range(tiles):
                g, cc, c0 = m // per_group, pl.ds((m % per_group) * 128, 128), (m % per_group) * 128
                on = moving(t + 1.0, m)
                gain = jnp.where(moving(t, m), row(svrow, l - 1, m), 0.0)
                inv_s = row(svrow, l, m)
                for r in range(0, num_states, chunk):
                    rr = pl.ds(r, chunk)
                    y = jnp.where(on, get(m, g, c0, cc, r), inv_s)
                    back_u[l, g, rr, cc] = (emem[l, rr, lane(m)] * y * gain).astype(BF)

        put_u(half_t - 1, float(half_t - 1),
              lambda m, g, c0, cc, r: alph[0, g, pl.ds(r, chunk), cc].astype(F32) * inv_q[m])

        def counts(l):
            own_counts(l, [dot_nt(alph[l, g, zrow, :], back_u[l, g]) for g in range(groups)])

        @pl.loop(0, half_t - 2)
        def _(k):
            l = half_t - 1 - k
            raws = [dot(mats[0, l], back_u[l, g]) for g in range(groups)]
            counts(l)
            put_u(l - 1, (l - 1).astype(F32), lambda m, g, c0, cc, r: piece(raws, g, c0, r))

        counts(1)

    @pl.when(x == 1)
    def _late():
        top = half_t - 1
        fill_emission(top)
        for m, g, cc, c0, r in chunks():
            rr = pl.ds(r, chunk)
            back_u[top, g, rr, cc] = emem[top, rr, lane(m)].astype(BF)

        def back_step(l, put):
            raws = [dot(mats[0, l], back_u[l, g]) for g in range(groups)]
            t = jnp.asarray(l + half_t).astype(F32)
            sums = per_tile(raws, 0)
            store_rows(svrow, l, sums)
            store_rows(yrow, l, per_tile(raws, 1))
            inv = [1.0 / v for v in sums]
            on = [(t > start_of(m)) & (t < stop_of(m)) for m in range(tiles)]
            for m, g, cc, c0, r in chunks():
                put(m, g, cc, r, jnp.where(on[m], piece(raws, g, c0, r) * inv[m], 1.0))

        @pl.loop(0, top)
        def _(k):
            l = top - k
            fill_emission(l - 1)

            def put(m, g, cc, r, v):
                rr = pl.ds(r, chunk)
                back_u[l - 1, g, rr, cc] = (v * emem[l - 1, rr, lane(m)]).astype(BF)

            back_step(l, put)

        def put(m, g, cc, r, v):
            alph[half_t, g, pl.ds(r, chunk), cc] = v.astype(BF)

        back_step(0, put)
        for g in range(groups):
            cross(g).start()
        for g in range(groups):
            cross(g).wait()
        q = junction()
        for m in range(tiles):
            span[2, m:m + 1, :] = q[m]
            span[3, m:m + 1, :] = q[m]

        @pl.loop(0, half_t)
        def _(l):
            raws = [dot(mats[1, l], alph[l, g]) for g in range(groups)]
            t = (l + half_t).astype(F32)
            sums, inv = forward_step(l, t, raws, l + 1)

            @pl.when(l > 0)
            def _():
                store_rows(srow, l - 1, sums)

            parts = []
            scaled = []
            for m in range(tiles):
                g, cc = m // per_group, pl.ds((m % per_group) * 128, 128)
                moving = (t > start_of(m)) & (t < stop_of(m))
                d = jnp.where(start_of(m) == t - 1.0, span[3, m:m + 1, :], span[2, m:m + 1, :])
                d = d * inv[m] * row(svrow, l, m)
                span[2, m:m + 1, :] = d
                span[3, m:m + 1, :] = row(yrow, l, m)
                w = jnp.where(moving, 1.0 / d, 0.0)
                scaled.append((alph[l, g, zrow, cc].astype(F32) * inv[m] * w).astype(BF))
            for g in range(groups):
                a = jnp.concatenate(scaled[g * per_group:(g + 1) * per_group], axis=1)
                parts.append(dot_nt(a, back_u[l, g]))
            own_counts(l, parts)

        last = [dot(ext, alph[half_t, g]) for g in range(groups)]
        store_rows(srow, half_t - 1, per_tile(last, 0))
        put_ll()

    mine = x * 2 + s
    ll_copies = []
    for j, dev in enumerate([partner, across, corner]):
        c = rcopy(llbox.at[mine], llbox.at[mine], lls_sem.at[j], llr_sem.at[j], dev)
        c.start()
        ll_copies.append(c)
    lane_out = lax.broadcasted_iota(jnp.int32, (zr, 128), 1)
    sums = jnp.zeros((zr, 128), F32)
    for k in range(half_t):
        part = jnp.sum(prb[k, :, :half] * cacc[k, 0] + prb[k, :, half:] * cacc[k, 1], axis=1, keepdims=True)
        sums = sums + jnp.where(lane_out == k, part, 0.0)
    rts[...] = sums
    rc = rcopy(rts, rtr, r_sem.at[0], r_sem.at[1], partner)
    rc.start()
    yc.wait()
    years = ybox[0, 0:1, 0:1] + ybox[1, 0:1, 0:1]
    factor = float(num_states * num_states * nt) / years
    rc.wait_recv()
    rtot = rts[...] + rtr[...]
    for k in range(half_t):
        rcopy(cacc.at[k, 1 - s], crecv.at[k], cs_sem.at[k], cr_sem.at[k], partner).wait()
        pr = jnp.where(first_core, prb[k, :, :half], prb[k, :, half:])
        out[k] = factor * (pr * ((cacc[k, s] + crecv[k]) - rtot[:, k:k + 1]))
    for c in ll_copies:
        c.wait_recv()
    ll = (llbox[0, 0:1, :] + llbox[1, 0:1, :]) + (llbox[2, 0:1, :] + llbox[3, 0:1, :])
    llout[...] = ll / years

    for c in hist + near + ll_copies + [rc]:
        c.wait_send()


def fused_device(
    earnings, starts, lengths, block_count, trans_logits, init_logits, state_mean, log_sd
):
    num_states = init_logits.shape[0]
    nt = earnings.shape[1]
    slot_rows = earnings.shape[0]
    cap = slot_rows // HB
    nz = lax.axis_size("hh")
    nsrc = nz * 2
    own_t = trans_logits.shape[0]
    half_t = nt // 2
    half = num_states // 2
    zr = num_states // nz
    lanes = 256
    groups = nsrc * HB // 2 // lanes
    wide = groups * lanes
    cfg = (nz, nt, half_t, own_t, num_states, groups, lanes)
    V = pltpu.VMEM
    D = pltpu.SemaphoreType.DMA
    vm = pl.BlockSpec(memory_space=pltpu.VMEM)
    grad, ll = pl.pallas_call(
        functools.partial(fused_kernel, cfg),
        out_shape=(jax.ShapeDtypeStruct((half_t, zr, half), F32),
                   jax.ShapeDtypeStruct((1, 128), F32)),
        in_specs=[vm, vm, vm, pl.BlockSpec(memory_space=pltpu.SMEM), pl.BlockSpec(memory_space=pl.ANY), vm, vm, vm],
        out_specs=(vm, vm),
        scratch_shapes=[
            V((2, 8, 256), F32),
            V((nsrc, 8, 256), F32),
            V((half_t, wide // 128, 128), F32),
            V((4, wide // 128, 128), F32),
            V((half_t, num_states, num_states), BF),
            V((2, half_t, EXT + num_states, num_states), BF),
            V((4, num_states, 128), F32),
            V((half_t + 1, groups, num_states, lanes), BF),
            V((half_t, groups, num_states, lanes), BF),
            V((half_t, num_states, wide), F32),
            V((half_t, wide // 128, 128), F32),
            V((half_t, wide // 128, 128), F32),
            V((half_t, wide // 128, 128), F32),
            V((half_t, 2, zr, half), F32),
            V((half_t, zr, half), F32),
            V((half_t, zr, num_states), F32),
            V((4, 8, 128), F32),
            V((2, 8, 128), F32),
            V((zr, 128), F32),
            V((zr, 128), F32),
            D((nsrc - 1,)), D((nsrc - 1,)), D((2 * own_t,)), D((own_t,)),
            D((groups,)), D((groups,)), D((half_t,)), D((half_t,)), D((2,)), D((3,)), D((3,)), D((2,)),
        ],
        compiler_params=pltpu.CompilerParams(
            collective_id=0, has_side_effects=True, vmem_limit_bytes=40 * 1024 * 1024),
        name="chain",
    )(earnings.T, starts.reshape(cap, HB), lengths.reshape(cap, HB), block_count, trans_logits,
      init_logits[None], state_mean[None], log_sd[None])
    return grad, ll[0, 0:1]


def solution(mesh):
    fits = mesh.shape["per"] == 2 and mesh.shape["st"] == 2 and mesh.shape["hh"] == 4
    body = fused_device if fits else per_device
    placed = (
        P(("hh", "per"), None),
        P(("hh", "per")),
        P(("hh", "per")),
        P(("hh", "per")),
        P(("grp", "per", "st"), None, None),
        P("grp"),
        P("grp"),
        P("grp"),
    )
    return jax.shard_map(
        body,
        mesh=mesh,
        in_specs=placed,
        out_specs=(P(("grp", "per"), "hh", "st"), P("grp")),
        check_vma=False,
    )
```

```python
import functools

import jax
import jax.numpy as jnp
from jax import lax
from jax.sharding import PartitionSpec as P
from jax.experimental import pallas as pl
from jax.experimental.pallas import tpu as pltpu

HB = 128


top_precision = lax.Precision.HIGHEST


def emission(column, state_mean, log_sd):
    z_score = (column[:, None] - state_mean[None, :]) / jnp.exp(log_sd)[None, :]
    return jnp.exp(-0.5 * z_score * z_score - log_sd[None, :])


def per_device(
    earnings, starts, lengths, block_count, trans_logits, init_logits, state_mean, log_sd
):
    num_states = init_logits.shape[0]
    num_periods = earnings.shape[1]
    slot_rows = earnings.shape[0]
    group_size = lax.axis_size(("hh", "per"))
    core_count = lax.axis_size("st")
    half_states = num_states // core_count
    lead_state = lax.axis_index("st") * half_states
    whole_logits = lax.all_gather(trans_logits, ("per", "st"), axis=0, tiled=True)
    raised = jnp.exp(whole_logits.astype(jnp.float32))
    trans_probs = raised / jnp.sum(raised, axis=2, keepdims=True)
    raised_first = jnp.exp(init_logits)
    first_probs = raised_first / jnp.sum(raised_first)
    source_rows = slot_rows // group_size
    count_out = jnp.broadcast_to(block_count.reshape(1, 1), (1, group_size))
    got_earn, got_start, got_len, got_count = (
        lax.all_to_all(
            earnings.reshape(source_rows, group_size, num_periods),
            ("hh", "per"),
            split_axis=1,
            concat_axis=1,
            tiled=True,
        ),
        lax.all_to_all(
            starts.reshape(source_rows, group_size),
            ("hh", "per"),
            split_axis=1,
            concat_axis=1,
            tiled=True,
        ),
        lax.all_to_all(
            lengths.reshape(source_rows, group_size),
            ("hh", "per"),
            split_axis=1,
            concat_axis=1,
            tiled=True,
        ),
        lax.all_to_all(count_out, ("hh", "per"), split_axis=1, concat_axis=1, tiled=True),
    )
    per_source = got_count[0] * (HB // group_size)
    source_order = jnp.arange(group_size, dtype=jnp.int32)
    up_to = source_order[None, :] <= source_order[:, None]
    ends_at = jnp.sum(jnp.where(up_to, per_source[None, :], 0), axis=1)
    target_ids = jnp.arange(HB, dtype=jnp.int32)
    before_mask = ends_at[None, :] <= target_ids[:, None]
    source_ids = jnp.sum(before_mask.astype(jnp.int32), axis=1)
    begins_at = jnp.sum(jnp.where(before_mask, per_source[None, :], 0), axis=1)
    pick_ids = (target_ids - begins_at) * group_size + source_ids
    rows_earn = jnp.take(got_earn.reshape(source_rows * group_size, num_periods), pick_ids, axis=0)
    rows_start = jnp.take(got_start.reshape(source_rows * group_size), pick_ids)
    rows_len = jnp.take(got_len.reshape(source_rows * group_size), pick_ids)
    row_live = jnp.ones((HB,), dtype=bool)
    years_local = jnp.sum(jnp.where(row_live, rows_len, 0)).astype(jnp.float32)
    row_total_count = rows_earn.shape[0]
    columns = rows_earn.T
    period_ids = jnp.arange(num_periods, dtype=jnp.int32)

    def observed(step_now):
        return row_live & (step_now >= rows_start) & (step_now < rows_start + rows_len)

    def forward(prev_alpha, inputs):
        matrix, column, step_now = inputs
        fresh_start = (step_now <= rows_start)[:, None]
        moved_mass = jnp.dot(
            prev_alpha, matrix, precision=top_precision, preferred_element_type=jnp.float32
        )
        joint_mass = jnp.where(fresh_start, first_probs[None, :], moved_mass) * emission(
            column, state_mean, log_sd
        )
        seen_now = observed(step_now)
        scale_now = jnp.where(seen_now, jnp.sum(joint_mass, axis=1), 1.0)
        new_alpha = jnp.where(seen_now[:, None], joint_mass / scale_now[:, None], prev_alpha)
        return (new_alpha, (new_alpha, scale_now))

    start_alpha = jnp.broadcast_to(first_probs[None, :], (row_total_count, num_states))
    _, (alphas, scales) = lax.scan(forward, start_alpha, (trans_probs, columns, period_ids))

    def carry_of(back_now, column, scale_now, step_now):
        seen_now = observed(step_now)
        return jnp.where(
            seen_now[:, None],
            emission(column, state_mean, log_sd) * back_now / scale_now[:, None],
            0.0,
        )

    def backward(carry_now, inputs):
        matrix, alpha_prev, column_prev, scale_prev, step_now = inputs
        moving = row_live & (step_now > rows_start) & (step_now < rows_start + rows_len)
        weights = jnp.where(moving[:, None], alpha_prev, 0.0)
        own_carry = lax.dynamic_slice_in_dim(carry_now, lead_state, half_states, 1)
        grad_term = lax.dot_general(
            weights,
            own_carry,
            (((0,), (0,)), ((), ())),
            precision=top_precision,
            preferred_element_type=jnp.float32,
        )
        pulled = lax.dot_general(
            carry_now,
            matrix,
            (((1,), (1,)), ((), ())),
            precision=top_precision,
            preferred_element_type=jnp.float32,
        )
        back_now = jnp.where(moving[:, None], pulled, 1.0)
        return (carry_of(back_now, column_prev, scale_prev, step_now - 1), grad_term)

    ones_back = jnp.ones((row_total_count, num_states), jnp.float32)
    last_carry = carry_of(
        ones_back, columns[num_periods - 1], scales[num_periods - 1], num_periods - 1
    )
    _, grad_terms = lax.scan(
        backward,
        last_carry,
        (trans_probs[1:], alphas[:-1], columns[:-1], scales[:-1], period_ids[1:]),
        reverse=True,
    )
    zero_first = jnp.zeros((1,) + grad_terms.shape[1:], jnp.float32)
    partial_counts = jnp.concatenate([zero_first, grad_terms], axis=0)
    loglik_local = jnp.sum(jnp.log(scales))
    summed = lax.psum_scatter(partial_counts, "hh", scatter_dimension=1, tiled=True)
    summed = lax.psum_scatter(summed, "per", scatter_dimension=0, tiled=True)
    loglik_share = loglik_local / core_count
    years_share = years_local / core_count
    period_block = summed.shape[0]
    row_block_size = summed.shape[1]
    local_probs = lax.dynamic_slice(
        trans_probs,
        (lax.axis_index("per") * period_block, lax.axis_index("hh") * row_block_size, lead_state),
        (period_block, row_block_size, half_states),
    )
    weighted = local_probs * summed
    row_total, loglik_core, years_core = lax.psum(
        (jnp.sum(weighted, axis=2), loglik_share, years_share), "st"
    )
    loglik_all, years_all = lax.psum((loglik_core, years_core), ("hh", "per"))
    factor = float(num_states * num_states * num_periods) / years_all
    trans_grad = factor * (weighted - local_probs * row_total[:, :, None])
    mean_loglik = jnp.reshape(loglik_all / years_all, (1,))
    return (trans_grad, mean_loglik)


F32 = jnp.float32
BF = jnp.bfloat16
MESH = pl.DeviceIdType.MESH
EXT = 16
LOG2E = 1.4426950408889634
NT_DIMS = (((1,), (1,)), ((), ()))


def dot(p, q):
    return jnp.dot(p, q, preferred_element_type=F32)


def dot_nt(p, q):
    return lax.dot_general(p, q, NT_DIMS, preferred_element_type=F32)


def fused_kernel(cfg, earn_h, begin_h, length_h, count, logits, init_h, mean_h, sd_h, out, llout,
                 earn, begin, length, params, pack, got, people, span, lg, mats, cols, alph, back_u, emem, srow, svrow, yrow,
                 cacc, crecv, prb, llbox, ybox, rts, rtr,
                 hs_sem, hr_sem, lr_sem, ls_sem, xs_sem, xr_sem, cs_sem, cr_sem, r_sem, lls_sem, llr_sem, y_sem, in_sem):
    nz, nt, half_t, own_t, num_states, groups, lanes = cfg
    x = lax.axis_index("per")
    z = lax.axis_index("hh")
    s = lax.axis_index("st")
    half = num_states // 2
    nsrc = nz * 2
    zr = num_states // nz
    tiles = groups * lanes // 128
    per_group = lanes // 128
    chunk = 64

    def rcopy(src, dst, ss, rs, dev):
        return pltpu.make_async_remote_copy(
            src_ref=src, dst_ref=dst, send_sem=ss, recv_sem=rs,
            device_id=dev, device_id_type=MESH)

    partner = {"hh": z, "per": x, "st": 1 - s}
    across = {"hh": z, "per": 1 - x, "st": s}
    corner = {"hh": z, "per": 1 - x, "st": 1 - s}
    peers = []
    for dz in range(nz):
        for dx in range(2):
            if dz or dx:
                px = x if dx == 0 else 1 - x
                peers.append((px, {"hh": lax.rem(z + dz, nz), "per": px, "st": s}))
    barrier = pltpu.get_barrier_semaphore()
    for dev in [d for _, d in peers] + [partner, corner]:
        pl.semaphore_signal(barrier, inc=1, device_id=dev, device_id_type=MESH)

    loads = [pltpu.make_async_copy(src, dst, in_sem.at[i]) for i, (src, dst) in enumerate([
        (earn_h, earn), (begin_h, begin), (length_h, length),
        (init_h, params.at[0]), (mean_h, params.at[1]), (sd_h, params.at[2])])]
    for c in loads:
        c.start()
    local = []
    for i in range(own_t):
        c = pltpu.make_async_copy(logits.at[i], lg.at[own_t * s + i], lr_sem.at[i])
        c.start()
        local.append(c)

    low = lax.broadcasted_iota(jnp.int32, (8, 128), 1) < 64
    first_core = s == 0

    def to_low(v):
        return jnp.where(first_core, v, pltpu.roll(v, 64, 1))

    def to_high(v):
        return jnp.where(first_core, pltpu.roll(v, 64, 1), v)

    for c in loads[:3]:
        c.wait()
    cnt = count[0].astype(F32)
    about = jnp.concatenate(
        [begin[...].astype(F32), length[...].astype(F32), jnp.full((2, 128), 1.0, F32) * cnt], axis=0)
    about = to_high(about)
    for h in range(2):
        e = [earn[h * half_t:(h + 1) * half_t, b * 128:(b + 1) * 128] for b in range(3)]
        pack[h, :, 0:128] = jnp.where(low, to_low(e[0]), to_high(e[1]))
        pack[h, :, 128:256] = jnp.where(low, to_low(e[2]), about)

    pl.semaphore_wait(barrier, len(peers) + 2)
    me_src = z * 2 + x
    hist = []
    for n, (px, dev) in enumerate(peers):
        c = rcopy(pack.at[px], got.at[me_src], hs_sem.at[n], hr_sem.at[n], dev)
        c.start()
        hist.append(c)
    near = []
    for i in range(own_t):
        c = rcopy(logits.at[i], lg.at[own_t * s + i], ls_sem.at[i], lr_sem.at[own_t + i], partner)
        c.start()
        near.append(c)
    got[me_src] = pack[x]

    for c in loads[3:]:
        c.wait()
    mean = params[1]
    log_sd = params[2]
    raised_first = jnp.exp(params[0])
    first = raised_first / jnp.sum(raised_first, axis=1, keepdims=True)
    slope = jnp.exp(-log_sd) * ((0.5 * LOG2E) ** 0.5)
    for i, v in enumerate([slope, slope * mean, log_sd * (-LOG2E), first]):
        cols[i] = jnp.broadcast_to(v, (128, num_states)).T
    ext_row = lax.broadcasted_iota(jnp.int32, (EXT, num_states), 0)
    ext = jnp.where(ext_row == 0, 1.0, jnp.where(ext_row == 1, jnp.broadcast_to(first, (EXT, num_states)), 0.0)).astype(BF)
    eye = jnp.where(lax.broadcasted_iota(jnp.int32, (num_states, num_states), 0)
                    == lax.broadcasted_iota(jnp.int32, (num_states, num_states), 1), 1.0, 0.0).astype(BF)

    zrow = pl.ds(pl.multiple_of(z * zr, zr), zr)

    def make_probs(l):
        r = jnp.exp(lg[l].astype(F32))
        p = (r * (1.0 / jnp.sum(r, axis=1, keepdims=True))).astype(BF)
        mats[0, l, 0:EXT] = ext
        mats[1, l, 0:EXT] = ext
        mats[0, l, EXT:] = p
        mats[1, l, EXT:] = dot_nt(eye, p).astype(BF)
        rz = jnp.exp(lg[l, zrow, :].astype(F32))
        prb[l] = rz / jnp.sum(rz, axis=1, keepdims=True)

    for i in range(own_t):
        local[i].wait()

    @pl.loop(0, own_t)
    def _(i):
        make_probs(own_t * s + i)

    for i in range(own_t):
        near[i].wait_recv()

    @pl.loop(0, own_t)
    def _(i):
        make_probs(own_t * (1 - s) + i)

    for n in range(len(peers)):
        hist[n].wait_recv()

    high_bit = jnp.where(lax.broadcasted_iota(jnp.int32, (1, 128), 1) < 64, 0.0, 1.0)
    base = jnp.zeros((1, 128), F32)
    xs = [jnp.zeros((8, 128), F32) for _ in range(tiles)]
    starts = [jnp.zeros((1, 128), F32) for _ in range(tiles)]
    spans = [jnp.zeros((1, 128), F32) for _ in range(tiles)]
    for d in range(nsrc):
        t0, t1 = got[d, :, 0:128], got[d, :, 128:256]
        r0, r1 = pltpu.roll(t0, 64, 1), pltpu.roll(t1, 64, 1)
        held = [jnp.where(low, t0, r0), jnp.where(low, r0, t0), jnp.where(low, t1, r1)]
        about = jnp.where(low, r1, t1)
        live = about[6:7]
        for b in range(3):
            spot = jnp.where(live > float(b), base + float(b), -2.0) - high_bit
            for m in range(tiles):
                hit = spot == float(2 * m)
                xs[m] = jnp.where(hit, held[b], xs[m])
                starts[m] = jnp.where(hit, about[b:b + 1], starts[m])
                spans[m] = jnp.where(hit, about[3 + b:4 + b], spans[m])
        base = base + live
    years_own = jnp.zeros((1, 1), F32)
    for m in range(tiles):
        for t in range(half_t):
            people[t, m:m + 1, :] = xs[m][t:t + 1]
        span[0, m:m + 1, :] = starts[m]
        span[1, m:m + 1, :] = starts[m] + spans[m]
        years_own = years_own + jnp.sum(spans[m], axis=1, keepdims=True)
    ybox[0] = jnp.broadcast_to(years_own, (8, 128))
    yc = rcopy(ybox.at[0], ybox.at[1], y_sem.at[0], y_sem.at[1], partner)
    yc.start()

    def lane(m):
        return pl.ds(m * 128, 128)

    def start_of(m):
        return span[0, m:m + 1, :]

    def stop_of(m):
        return span[1, m:m + 1, :]

    def row(ref, l, m):
        return ref[l, m:m + 1, :]

    def chunks():
        for m in range(tiles):
            for r in range(0, num_states, chunk):
                yield m, m // per_group, pl.ds((m % per_group) * 128, 128), (m % per_group) * 128, r

    def fill_emission(l):
        for m in range(tiles):
            xrow = row(people, l, m)
            for r in range(0, num_states, chunk):
                rr = pl.ds(r, chunk)
                dev = cols[0, rr, :] * xrow - cols[1, rr, :]
                emem[l, rr, lane(m)] = jnp.exp2(cols[2, rr, :] - dev * dev)

    def per_tile(raws, i):
        return [raws[m // per_group][i:i + 1, (m % per_group) * 128:(m % per_group + 1) * 128] for m in range(tiles)]

    def piece(raws, g, c0, r):
        return raws[g][EXT + r:EXT + r + chunk, c0:c0 + 128]

    def store_rows(ref, l, vals):
        for m in range(tiles):
            ref[l, m:m + 1, :] = vals[m]

    def forward_step(l, t, raws, dst):
        sums = per_tile(raws, 0)
        inv = [1.0 / v for v in sums]
        fresh = [t <= start_of(m) for m in range(tiles)]
        for m, g, cc, c0, r in chunks():
            rr = pl.ds(r, chunk)
            moved = jnp.where(fresh[m], cols[3, rr, :], piece(raws, g, c0, r) * inv[m])
            alph[dst, g, rr, cc] = (moved * emem[l, rr, lane(m)]).astype(BF)
        return sums, inv

    def own_counts(l, raws):
        c = raws[0]
        for v in raws[1:]:
            c = c + v
        cacc[l, 0] = c[:, :half]
        cacc[l, 1] = c[:, half:]
        rcopy(cacc.at[l, 1 - s], crecv.at[l], cs_sem.at[l], cr_sem.at[l], partner).start()

    def cross(g):
        return rcopy(alph.at[half_t, g], alph.at[0, g], xs_sem.at[g], xr_sem.at[g], across)

    def junction():
        q = []
        for m in range(tiles):
            g, cc = m // per_group, pl.ds((m % per_group) * 128, 128)
            acc = jnp.zeros((chunk, 128), F32)
            for r in range(0, num_states, chunk):
                rr = pl.ds(r, chunk)
                acc = acc + alph[half_t, g, rr, cc].astype(F32) * alph[0, g, rr, cc].astype(F32)
            q.append(jnp.sum(acc, axis=0, keepdims=True))
        return q

    def put_ll():
        logs = jnp.zeros((tiles, 128), F32)
        for l in range(half_t):
            t = (x * half_t + l).astype(F32)
            seen = (t >= span[0]) & (t < span[1])
            logs = logs + jnp.where(seen, jnp.log(srow[l]), 0.0)
        total = jnp.sum(jnp.sum(logs, axis=0, keepdims=True), axis=1, keepdims=True)
        llbox[x * 2 + s] = jnp.broadcast_to(total, (8, 128))

    @pl.when(x == 0)
    def _early():
        fill_emission(0)
        for m, g, cc, c0, r in chunks():
            rr = pl.ds(r, chunk)
            alph[1, g, rr, cc] = (cols[3, rr, :] * emem[0, rr, lane(m)]).astype(BF)

        @pl.loop(1, half_t)
        def _(l):
            raws = [dot(mats[1, l], alph[l, g]) for g in range(groups)]
            fill_emission(l)
            sums, _ = forward_step(l, l.astype(F32), raws, l + 1)
            store_rows(srow, l - 1, sums)

        for g in range(groups):
            cross(g).start()
        cacc[0] = jnp.zeros(cacc.shape[1:], F32)
        rcopy(cacc.at[0, 1 - s], crecv.at[0], cs_sem.at[0], cr_sem.at[0], partner).start()
        last = [dot(ext, alph[half_t, g]) for g in range(groups)]
        store_rows(srow, half_t - 1, per_tile(last, 0))
        put_ll()
        srow_inv = 1.0 / srow[...]
        svrow[...] = srow_inv
        for g in range(groups):
            cross(g).wait()
        inv_q = [1.0 / v for v in junction()]

        def moving(t, m):
            return (t > start_of(m)) & (t < stop_of(m))

        def put_u(l, t, get):
            for m in range(tiles):
                g, cc, c0 = m // per_group, pl.ds((m % per_group) * 128, 128), (m % per_group) * 128
                on = moving(t + 1.0, m)
                gain = jnp.where(moving(t, m), row(svrow, l - 1, m), 0.0)
                inv_s = row(svrow, l, m)
                for r in range(0, num_states, chunk):
                    rr = pl.ds(r, chunk)
                    y = jnp.where(on, get(m, g, c0, cc, r), inv_s)
                    back_u[l, g, rr, cc] = (emem[l, rr, lane(m)] * y * gain).astype(BF)

        put_u(half_t - 1, float(half_t - 1),
              lambda m, g, c0, cc, r: alph[0, g, pl.ds(r, chunk), cc].astype(F32) * inv_q[m])

        def counts(l):
            own_counts(l, [dot_nt(alph[l, g, zrow, :], back_u[l, g]) for g in range(groups)])

        @pl.loop(0, half_t - 2)
        def _(k):
            l = half_t - 1 - k
            raws = [dot(mats[0, l], back_u[l, g]) for g in range(groups)]
            counts(l)
            put_u(l - 1, (l - 1).astype(F32), lambda m, g, c0, cc, r: piece(raws, g, c0, r))

        counts(1)

    @pl.when(x == 1)
    def _late():
        top = half_t - 1
        fill_emission(top)
        for m, g, cc, c0, r in chunks():
            rr = pl.ds(r, chunk)
            back_u[top, g, rr, cc] = emem[top, rr, lane(m)].astype(BF)

        def back_step(l, put):
            raws = [dot(mats[0, l], back_u[l, g]) for g in range(groups)]
            t = jnp.asarray(l + half_t).astype(F32)
            sums = per_tile(raws, 0)
            store_rows(svrow, l, sums)
            store_rows(yrow, l, per_tile(raws, 1))
            inv = [1.0 / v for v in sums]
            on = [(t > start_of(m)) & (t < stop_of(m)) for m in range(tiles)]
            for m, g, cc, c0, r in chunks():
                put(m, g, cc, r, jnp.where(on[m], piece(raws, g, c0, r) * inv[m], 1.0))

        @pl.loop(0, top)
        def _(k):
            l = top - k
            fill_emission(l - 1)

            def put(m, g, cc, r, v):
                rr = pl.ds(r, chunk)
                back_u[l - 1, g, rr, cc] = (v * emem[l - 1, rr, lane(m)]).astype(BF)

            back_step(l, put)

        def put(m, g, cc, r, v):
            alph[half_t, g, pl.ds(r, chunk), cc] = v.astype(BF)

        back_step(0, put)
        for g in range(groups):
            cross(g).start()
        for g in range(groups):
            cross(g).wait()
        q = junction()
        for m in range(tiles):
            span[2, m:m + 1, :] = q[m]
            span[3, m:m + 1, :] = q[m]

        @pl.loop(0, half_t)
        def _(l):
            raws = [dot(mats[1, l], alph[l, g]) for g in range(groups)]
            t = (l + half_t).astype(F32)
            sums, inv = forward_step(l, t, raws, l + 1)

            @pl.when(l > 0)
            def _():
                store_rows(srow, l - 1, sums)

            parts = []
            scaled = []
            for m in range(tiles):
                g, cc = m // per_group, pl.ds((m % per_group) * 128, 128)
                moving = (t > start_of(m)) & (t < stop_of(m))
                d = jnp.where(start_of(m) == t - 1.0, span[3, m:m + 1, :], span[2, m:m + 1, :])
                d = d * inv[m] * row(svrow, l, m)
                span[2, m:m + 1, :] = d
                span[3, m:m + 1, :] = row(yrow, l, m)
                w = jnp.where(moving, 1.0 / d, 0.0)
                scaled.append((alph[l, g, zrow, cc].astype(F32) * inv[m] * w).astype(BF))
            for g in range(groups):
                a = jnp.concatenate(scaled[g * per_group:(g + 1) * per_group], axis=1)
                parts.append(dot_nt(a, back_u[l, g]))
            own_counts(l, parts)

        last = [dot(ext, alph[half_t, g]) for g in range(groups)]
        store_rows(srow, half_t - 1, per_tile(last, 0))
        put_ll()

    mine = x * 2 + s
    ll_copies = []
    for j, dev in enumerate([partner, across, corner]):
        c = rcopy(llbox.at[mine], llbox.at[mine], lls_sem.at[j], llr_sem.at[j], dev)
        c.start()
        ll_copies.append(c)
    lane_out = lax.broadcasted_iota(jnp.int32, (zr, 128), 1)
    sums = jnp.zeros((zr, 128), F32)
    for k in range(half_t):
        part = jnp.sum(prb[k, :, :half] * cacc[k, 0] + prb[k, :, half:] * cacc[k, 1], axis=1, keepdims=True)
        sums = sums + jnp.where(lane_out == k, part, 0.0)
    rts[...] = sums
    rc = rcopy(rts, rtr, r_sem.at[0], r_sem.at[1], partner)
    rc.start()
    yc.wait()
    years = ybox[0, 0:1, 0:1] + ybox[1, 0:1, 0:1]
    factor = float(num_states * num_states * nt) / years
    rc.wait_recv()
    rtot = rts[...] + rtr[...]
    for k in range(half_t):
        rcopy(cacc.at[k, 1 - s], crecv.at[k], cs_sem.at[k], cr_sem.at[k], partner).wait()
        pr = jnp.where(first_core, prb[k, :, :half], prb[k, :, half:])
        out[k] = factor * (pr * ((cacc[k, s] + crecv[k]) - rtot[:, k:k + 1]))
    for c in ll_copies:
        c.wait_recv()
    ll = (llbox[0, 0:1, :] + llbox[1, 0:1, :]) + (llbox[2, 0:1, :] + llbox[3, 0:1, :])
    llout[...] = ll / years

    for c in hist + near + ll_copies + [rc]:
        c.wait_send()


def fused_device(
    earnings, starts, lengths, block_count, trans_logits, init_logits, state_mean, log_sd
):
    num_states = init_logits.shape[0]
    nt = earnings.shape[1]
    slot_rows = earnings.shape[0]
    cap = slot_rows // HB
    nz = lax.axis_size("hh")
    nsrc = nz * 2
    own_t = trans_logits.shape[0]
    half_t = nt // 2
    half = num_states // 2
    zr = num_states // nz
    lanes = 256
    groups = nsrc * HB // 2 // lanes
    wide = groups * lanes
    cfg = (nz, nt, half_t, own_t, num_states, groups, lanes)
    V = pltpu.VMEM
    D = pltpu.SemaphoreType.DMA
    vm = pl.BlockSpec(memory_space=pltpu.VMEM)
    hbm = pl.BlockSpec(memory_space=pltpu.HBM)
    pinned = lambda v: pltpu.with_memory_space_constraint(v, pltpu.HBM)
    grad, ll = pl.pallas_call(
        functools.partial(fused_kernel, cfg),
        out_shape=(jax.ShapeDtypeStruct((half_t, zr, half), F32),
                   jax.ShapeDtypeStruct((1, 128), F32)),
        in_specs=[hbm, hbm, hbm, pl.BlockSpec(memory_space=pltpu.SMEM), hbm, hbm, hbm, hbm],
        out_specs=(vm, vm),
        scratch_shapes=[
            V((nt, slot_rows), F32), V((cap, HB), jnp.int32), V((cap, HB), jnp.int32), V((3, 1, num_states), F32),
            V((2, 8, 256), F32),
            V((nsrc, 8, 256), F32),
            V((half_t, wide // 128, 128), F32),
            V((4, wide // 128, 128), F32),
            V((half_t, num_states, num_states), BF),
            V((2, half_t, EXT + num_states, num_states), BF),
            V((4, num_states, 128), F32),
            V((half_t + 1, groups, num_states, lanes), BF),
            V((half_t, groups, num_states, lanes), BF),
            V((half_t, num_states, wide), F32),
            V((half_t, wide // 128, 128), F32),
            V((half_t, wide // 128, 128), F32),
            V((half_t, wide // 128, 128), F32),
            V((half_t, 2, zr, half), F32),
            V((half_t, zr, half), F32),
            V((half_t, zr, num_states), F32),
            V((4, 8, 128), F32),
            V((2, 8, 128), F32),
            V((zr, 128), F32),
            V((zr, 128), F32),
            D((nsrc - 1,)), D((nsrc - 1,)), D((2 * own_t,)), D((own_t,)),
            D((groups,)), D((groups,)), D((half_t,)), D((half_t,)), D((2,)), D((3,)), D((3,)), D((2,)), D((6,)),
        ],
        compiler_params=pltpu.CompilerParams(
            collective_id=0, has_side_effects=True, vmem_limit_bytes=40 * 1024 * 1024),
        name="chain",
    )(pinned(earnings.T), pinned(starts.reshape(cap, HB)), pinned(lengths.reshape(cap, HB)), block_count,
      pinned(trans_logits), pinned(init_logits[None]), pinned(state_mean[None]), pinned(log_sd[None]))
    return grad, ll[0, 0:1]


def solution(mesh):
    fits = mesh.shape["per"] == 2 and mesh.shape["st"] == 2 and mesh.shape["hh"] == 4
    body = fused_device if fits else per_device
    placed = (
        P(("hh", "per"), None),
        P(("hh", "per")),
        P(("hh", "per")),
        P(("hh", "per")),
        P(("grp", "per", "st"), None, None),
        P("grp"),
        P("grp"),
        P("grp"),
    )
    return jax.shard_map(
        body,
        mesh=mesh,
        in_specs=placed,
        out_specs=(P(("grp", "per"), "hh", "st"), P("grp")),
        check_vma=False,
    )
```

```python
import functools

import jax
import jax.numpy as jnp
from jax import lax
from jax.sharding import PartitionSpec as P
from jax.experimental import pallas as pl
from jax.experimental.pallas import tpu as pltpu

HB = 128


top_precision = lax.Precision.HIGHEST


def emission(column, state_mean, log_sd):
    z_score = (column[:, None] - state_mean[None, :]) / jnp.exp(log_sd)[None, :]
    return jnp.exp(-0.5 * z_score * z_score - log_sd[None, :])


def per_device(
    earnings, starts, lengths, block_count, trans_logits, init_logits, state_mean, log_sd
):
    num_states = init_logits.shape[0]
    num_periods = earnings.shape[1]
    slot_rows = earnings.shape[0]
    group_size = lax.axis_size(("hh", "per"))
    core_count = lax.axis_size("st")
    half_states = num_states // core_count
    lead_state = lax.axis_index("st") * half_states
    whole_logits = lax.all_gather(trans_logits, ("per", "st"), axis=0, tiled=True)
    raised = jnp.exp(whole_logits.astype(jnp.float32))
    trans_probs = raised / jnp.sum(raised, axis=2, keepdims=True)
    raised_first = jnp.exp(init_logits)
    first_probs = raised_first / jnp.sum(raised_first)
    source_rows = slot_rows // group_size
    count_out = jnp.broadcast_to(block_count.reshape(1, 1), (1, group_size))
    got_earn, got_start, got_len, got_count = (
        lax.all_to_all(
            earnings.reshape(source_rows, group_size, num_periods),
            ("hh", "per"),
            split_axis=1,
            concat_axis=1,
            tiled=True,
        ),
        lax.all_to_all(
            starts.reshape(source_rows, group_size),
            ("hh", "per"),
            split_axis=1,
            concat_axis=1,
            tiled=True,
        ),
        lax.all_to_all(
            lengths.reshape(source_rows, group_size),
            ("hh", "per"),
            split_axis=1,
            concat_axis=1,
            tiled=True,
        ),
        lax.all_to_all(count_out, ("hh", "per"), split_axis=1, concat_axis=1, tiled=True),
    )
    per_source = got_count[0] * (HB // group_size)
    source_order = jnp.arange(group_size, dtype=jnp.int32)
    up_to = source_order[None, :] <= source_order[:, None]
    ends_at = jnp.sum(jnp.where(up_to, per_source[None, :], 0), axis=1)
    target_ids = jnp.arange(HB, dtype=jnp.int32)
    before_mask = ends_at[None, :] <= target_ids[:, None]
    source_ids = jnp.sum(before_mask.astype(jnp.int32), axis=1)
    begins_at = jnp.sum(jnp.where(before_mask, per_source[None, :], 0), axis=1)
    pick_ids = (target_ids - begins_at) * group_size + source_ids
    rows_earn = jnp.take(got_earn.reshape(source_rows * group_size, num_periods), pick_ids, axis=0)
    rows_start = jnp.take(got_start.reshape(source_rows * group_size), pick_ids)
    rows_len = jnp.take(got_len.reshape(source_rows * group_size), pick_ids)
    row_live = jnp.ones((HB,), dtype=bool)
    years_local = jnp.sum(jnp.where(row_live, rows_len, 0)).astype(jnp.float32)
    row_total_count = rows_earn.shape[0]
    columns = rows_earn.T
    period_ids = jnp.arange(num_periods, dtype=jnp.int32)

    def observed(step_now):
        return row_live & (step_now >= rows_start) & (step_now < rows_start + rows_len)

    def forward(prev_alpha, inputs):
        matrix, column, step_now = inputs
        fresh_start = (step_now <= rows_start)[:, None]
        moved_mass = jnp.dot(
            prev_alpha, matrix, precision=top_precision, preferred_element_type=jnp.float32
        )
        joint_mass = jnp.where(fresh_start, first_probs[None, :], moved_mass) * emission(
            column, state_mean, log_sd
        )
        seen_now = observed(step_now)
        scale_now = jnp.where(seen_now, jnp.sum(joint_mass, axis=1), 1.0)
        new_alpha = jnp.where(seen_now[:, None], joint_mass / scale_now[:, None], prev_alpha)
        return (new_alpha, (new_alpha, scale_now))

    start_alpha = jnp.broadcast_to(first_probs[None, :], (row_total_count, num_states))
    _, (alphas, scales) = lax.scan(forward, start_alpha, (trans_probs, columns, period_ids))

    def carry_of(back_now, column, scale_now, step_now):
        seen_now = observed(step_now)
        return jnp.where(
            seen_now[:, None],
            emission(column, state_mean, log_sd) * back_now / scale_now[:, None],
            0.0,
        )

    def backward(carry_now, inputs):
        matrix, alpha_prev, column_prev, scale_prev, step_now = inputs
        moving = row_live & (step_now > rows_start) & (step_now < rows_start + rows_len)
        weights = jnp.where(moving[:, None], alpha_prev, 0.0)
        own_carry = lax.dynamic_slice_in_dim(carry_now, lead_state, half_states, 1)
        grad_term = lax.dot_general(
            weights,
            own_carry,
            (((0,), (0,)), ((), ())),
            precision=top_precision,
            preferred_element_type=jnp.float32,
        )
        pulled = lax.dot_general(
            carry_now,
            matrix,
            (((1,), (1,)), ((), ())),
            precision=top_precision,
            preferred_element_type=jnp.float32,
        )
        back_now = jnp.where(moving[:, None], pulled, 1.0)
        return (carry_of(back_now, column_prev, scale_prev, step_now - 1), grad_term)

    ones_back = jnp.ones((row_total_count, num_states), jnp.float32)
    last_carry = carry_of(
        ones_back, columns[num_periods - 1], scales[num_periods - 1], num_periods - 1
    )
    _, grad_terms = lax.scan(
        backward,
        last_carry,
        (trans_probs[1:], alphas[:-1], columns[:-1], scales[:-1], period_ids[1:]),
        reverse=True,
    )
    zero_first = jnp.zeros((1,) + grad_terms.shape[1:], jnp.float32)
    partial_counts = jnp.concatenate([zero_first, grad_terms], axis=0)
    loglik_local = jnp.sum(jnp.log(scales))
    summed = lax.psum_scatter(partial_counts, "hh", scatter_dimension=1, tiled=True)
    summed = lax.psum_scatter(summed, "per", scatter_dimension=0, tiled=True)
    loglik_share = loglik_local / core_count
    years_share = years_local / core_count
    period_block = summed.shape[0]
    row_block_size = summed.shape[1]
    local_probs = lax.dynamic_slice(
        trans_probs,
        (lax.axis_index("per") * period_block, lax.axis_index("hh") * row_block_size, lead_state),
        (period_block, row_block_size, half_states),
    )
    weighted = local_probs * summed
    row_total, loglik_core, years_core = lax.psum(
        (jnp.sum(weighted, axis=2), loglik_share, years_share), "st"
    )
    loglik_all, years_all = lax.psum((loglik_core, years_core), ("hh", "per"))
    factor = float(num_states * num_states * num_periods) / years_all
    trans_grad = factor * (weighted - local_probs * row_total[:, :, None])
    mean_loglik = jnp.reshape(loglik_all / years_all, (1,))
    return (trans_grad, mean_loglik)


F32 = jnp.float32
BF = jnp.bfloat16
MESH = pl.DeviceIdType.MESH
EXT = 16
LOG2E = 1.4426950408889634
NT_DIMS = (((1,), (1,)), ((), ()))


def dot(p, q):
    return jnp.dot(p, q, preferred_element_type=F32)


def dot_nt(p, q):
    return lax.dot_general(p, q, NT_DIMS, preferred_element_type=F32)


def fused_kernel(cfg, earn_h, begin_h, length_h, count, logits, init_h, mean_h, sd_h, out, llout,
                 earn, begin, length, params, pack, got, people, span, lg, mats, cols, exts, alph, back_u, emem,
                 srow, irow, yrow, cacc, crecv, prb, llbox, ybox,
                 in_sem, hs_sem, hr_sem, lr_sem, ls_sem, xs_sem, xr_sem, fs_sem, fr_sem, cs_sem, cr_sem,
                 lls_sem, llr_sem, y_sem):
    nz, nt, half_t, own_t, num_states, groups, lanes, parts = cfg
    x = lax.axis_index("per")
    z = lax.axis_index("hh")
    s = lax.axis_index("st")
    half = num_states // 2
    nsrc = nz * 2
    zr = num_states // nz
    per_group = lanes // 128
    chunk = 64
    first_core = s == 0

    def rcopy(src, dst, ss, rs, dev):
        return pltpu.make_async_remote_copy(
            src_ref=src, dst_ref=dst, send_sem=ss, recv_sem=rs,
            device_id=dev, device_id_type=MESH)

    partner = {"hh": z, "per": x, "st": 1 - s}
    across = {"hh": z, "per": 1 - x, "st": s}
    corner = {"hh": z, "per": 1 - x, "st": 1 - s}
    mine = lax.rem(z, 2)
    other = 1 - mine
    pair = {"hh": z + 1 - 2 * mine, "per": x, "st": s}
    peers = []
    for dz in range(nz):
        for dx in range(2):
            if dz or dx:
                px = x if dx == 0 else 1 - x
                peers.append((px, {"hh": lax.rem(z + dz, nz), "per": px, "st": s}))

    loads = [pltpu.make_async_copy(src, dst, in_sem.at[i]) for i, (src, dst) in enumerate([
        (earn_h, earn), (begin_h, begin), (length_h, length),
        (init_h, params.at[0]), (mean_h, params.at[1]), (sd_h, params.at[2])])]
    for c in loads:
        c.start()
    barrier = pltpu.get_barrier_semaphore()
    for dev in [d for _, d in peers] + [partner, corner]:
        pl.semaphore_signal(barrier, inc=1, device_id=dev, device_id_type=MESH)
    local = []
    for i in range(own_t):
        c = pltpu.make_async_copy(logits.at[i], lg.at[own_t * s + i], lr_sem.at[i])
        c.start()
        local.append(c)

    low = lax.broadcasted_iota(jnp.int32, (8, 128), 1) < 64

    def to_low(v):
        return jnp.where(first_core, v, pltpu.roll(v, 64, 1))

    def to_high(v):
        return jnp.where(first_core, pltpu.roll(v, 64, 1), v)

    for c in loads[:3]:
        c.wait()
    cnt = count[0].astype(F32)
    about = jnp.concatenate(
        [begin[...].astype(F32), length[...].astype(F32), jnp.full((2, 128), 1.0, F32) * cnt], axis=0)
    about = to_high(about)
    for h in range(2):
        e = [earn[h * half_t:(h + 1) * half_t, b * 128:(b + 1) * 128] for b in range(3)]
        pack[h, :, 0:128] = jnp.where(low, to_low(e[0]), to_high(e[1]))
        pack[h, :, 128:256] = jnp.where(low, to_low(e[2]), about)

    zrow = pl.ds(pl.multiple_of(z * zr, zr), zr)

    def make_probs(l):
        ext = exts[...]
        eye = jnp.where(lax.broadcasted_iota(jnp.int32, (num_states, num_states), 0)
                        == lax.broadcasted_iota(jnp.int32, (num_states, num_states), 1), 1.0, 0.0).astype(BF)
        r = jnp.exp(lg[l].astype(F32))
        p = (r * (1.0 / jnp.sum(r, axis=1, keepdims=True))).astype(BF)
        mats[0, l, 0:EXT] = ext
        mats[1, l, 0:EXT] = ext
        mats[0, l, EXT:] = p
        mats[1, l, EXT:] = dot_nt(eye, p).astype(BF)
        rz = jnp.exp(lg[l, zrow, :].astype(F32))
        prb[l] = rz / jnp.sum(rz, axis=1, keepdims=True)

    def own_work():
        for c in loads[3:]:
            c.wait()
        mean = params[1]
        log_sd = params[2]
        raised_first = jnp.exp(params[0])
        first = raised_first / jnp.sum(raised_first, axis=1, keepdims=True)
        slope = jnp.exp(-log_sd) * ((0.5 * LOG2E) ** 0.5)
        for i, v in enumerate([slope, slope * mean, log_sd * (-LOG2E), first]):
            cols[i] = jnp.broadcast_to(v, (128, num_states)).T
        ext_row = lax.broadcasted_iota(jnp.int32, (EXT, num_states), 0)
        exts[...] = jnp.where(ext_row == 0, 1.0, jnp.where(
            ext_row == 1, jnp.broadcast_to(first, (EXT, num_states)), 0.0)).astype(BF)
        for c in local:
            c.wait()

        @pl.loop(0, own_t)
        def _(i):
            make_probs(own_t * s + i)

    @pl.when(z < nz - 1)
    def _():
        own_work()

    pl.semaphore_wait(barrier, len(peers) + 2)
    me_src = z * 2 + x
    hist = []
    for n, (px, dev) in enumerate(peers):
        c = rcopy(pack.at[px], got.at[me_src], hs_sem.at[n], hr_sem.at[me_src], dev)
        c.start()
        hist.append(c)
    near = []
    for i in range(own_t):
        c = rcopy(logits.at[i], lg.at[own_t * s + i], ls_sem.at[i], lr_sem.at[own_t + i], partner)
        c.start()
        near.append(c)
    pltpu.make_async_copy(pack.at[x], got.at[me_src], hr_sem.at[me_src]).start()

    @pl.when(z == nz - 1)
    def _():
        own_work()

    for c in near:
        c.wait_recv()

    @pl.loop(0, own_t)
    def _(i):
        make_probs(own_t * (1 - s) + i)

    tiles = groups * per_group
    high_bit = jnp.where(lax.broadcasted_iota(jnp.int32, (1, 128), 1) < 64, 0.0, 1.0)
    base = jnp.zeros((1, 128), F32)
    xs = [jnp.zeros((8, 128), F32) for _ in range(tiles)]
    starts = [jnp.zeros((1, 128), F32) for _ in range(tiles)]
    spans = [jnp.zeros((1, 128), F32) for _ in range(tiles)]
    for d in range(nsrc):
        rcopy(pack.at[0], got.at[d], hs_sem.at[0], hr_sem.at[d], across).wait_recv()
        t0, t1 = got[d, :, 0:128], got[d, :, 128:256]
        r0, r1 = pltpu.roll(t0, 64, 1), pltpu.roll(t1, 64, 1)
        held = [jnp.where(low, t0, r0), jnp.where(low, r0, t0), jnp.where(low, t1, r1)]
        about = jnp.where(low, r1, t1)
        live = about[6:7]
        for b in range(3):
            spot = jnp.where(live > float(b), base + float(b), -2.0) - high_bit
            for m in range(tiles):
                hit = spot == float(2 * m)
                xs[m] = jnp.where(hit, held[b], xs[m])
                starts[m] = jnp.where(hit, about[b:b + 1], starts[m])
                spans[m] = jnp.where(hit, about[3 + b:4 + b], spans[m])
        base = base + live
    years_own = jnp.zeros((1, 1), F32)
    for m in range(tiles):
        g, c = m // per_group, m % per_group
        for t in range(half_t):
            people[t, g, c:c + 1, :] = xs[m][t:t + 1]
        span[0, g, c:c + 1, :] = starts[m]
        span[1, g, c:c + 1, :] = starts[m] + spans[m]
        years_own = years_own + jnp.sum(spans[m], axis=1, keepdims=True)
    ybox[0] = jnp.broadcast_to(years_own, (8, 128))
    yc = rcopy(ybox.at[0], ybox.at[1], y_sem.at[0], y_sem.at[1], partner)
    yc.start()

    cells = [(m, pl.ds(m * 128, 128), m * 128, r, pl.ds(r, chunk))
             for m in range(per_group) for r in range(0, num_states, chunk)]

    def row(ref, l, g):
        return [ref[l, g, m:m + 1, :] for m in range(per_group)]

    def put_row(ref, l, g, vals):
        for m in range(per_group):
            ref[l, g, m:m + 1, :] = vals[m]

    def ext_row_of(raw, i):
        return [raw[i:i + 1, m * 128:(m + 1) * 128] for m in range(per_group)]

    def piece(raw, c0, r):
        return raw[EXT + r:EXT + r + chunk, c0:c0 + 128]

    def moving(t, g):
        return [(t > a) & (t < b) for a, b in zip(row(span, 0, g), row(span, 1, g))]

    def fill_emission(l, g):
        xrow = row(people, l, g)
        for m, cc, c0, r, rr in cells:
            off = cols[0, rr, :] * xrow[m] - cols[1, rr, :]
            emem[l, g, rr, cc] = jnp.exp2(cols[2, rr, :] - off * off)

    def forward_step(l, t, g, raw, inv):
        fresh = [t <= a for a in row(span, 0, g)]
        for m, cc, c0, r, rr in cells:
            moved = jnp.where(fresh[m], cols[3, rr, :], piece(raw, c0, r) * inv[m])
            alph[l + 1, g, rr, cc] = (moved * emem[l, g, rr, cc]).astype(BF)

    def part_rows(k):
        return pl.ds(k * (num_states // parts), num_states // parts)

    def cross(k):
        return rcopy(alph.at[half_t, mine, part_rows(k)], alph.at[0, mine, part_rows(k)],
                     xs_sem.at[k], xr_sem.at[k], across)

    def onward(k, g):
        return rcopy(alph.at[0, g, part_rows(k)], alph.at[0, g, part_rows(k)], fs_sem.at[k], fr_sem.at[k], pair)

    def send_cross():
        for k in range(parts):
            cross(k).start()

    def pass_on():
        for k in range(parts):
            cross(k).wait_recv()
            onward(k, mine).start()

    def take_other():
        for k in range(parts):
            onward(k, other).wait_recv()

    def junction(g):
        q = []
        for m in range(per_group):
            acc = jnp.zeros((chunk, 128), F32)
            for r in range(0, num_states, chunk):
                rr, cc = pl.ds(r, chunk), pl.ds(m * 128, 128)
                acc = acc + alph[half_t, g, rr, cc].astype(F32) * alph[0, g, rr, cc].astype(F32)
            q.append(jnp.sum(acc, axis=0, keepdims=True))
        return q

    def counts_copy(l):
        return rcopy(cacc.at[l], crecv.at[l], cs_sem.at[l], cr_sem.at[l], partner)

    def add_counts(l, v, last):
        if last:
            cacc[l] = cacc[l] + v
            counts_copy(l).start()
        else:
            cacc[l] = v

    def send_ll(logs):
        llbox[x * 2 + s] = jnp.broadcast_to(
            jnp.sum(jnp.sum(logs, axis=0, keepdims=True), axis=1, keepdims=True), (8, 128))
        at = x * 2 + s
        for j, dev in enumerate([partner, across, corner]):
            rcopy(llbox.at[at], llbox.at[at], lls_sem.at[j], llr_sem.at[j], dev).start()

    def finish(order):
        yc.wait()
        years = ybox[0, 0:1, 0:1] + ybox[1, 0:1, 0:1]
        factor = float(num_states * num_states * nt) / years
        at = x * 2 + s
        for j, dev in enumerate([partner, across, corner]):
            rcopy(llbox.at[at], llbox.at[at], lls_sem.at[j], llr_sem.at[j], dev).wait()
        ll = (llbox[0, 0:1, :] + llbox[1, 0:1, :]) + (llbox[2, 0:1, :] + llbox[3, 0:1, :])
        llout[...] = ll / years
        for l in order:
            counts_copy(l).wait()
            w = prb[l] * (cacc[l] + crecv[l])
            total = jnp.sum(w, axis=1, keepdims=True)
            w_own = jnp.where(first_core, w[:, :half], w[:, half:])
            p_own = jnp.where(first_core, prb[l, :, :half], prb[l, :, half:])
            out[l] = factor * (w_own - p_own * total)

    @pl.when(x == 0)
    def _early():
        def first_pass(g):
            fill_emission(0, g)
            for m, cc, c0, r, rr in cells:
                alph[1, g, rr, cc] = (cols[3, rr, :] * emem[0, g, rr, cc]).astype(BF)

            @pl.loop(1, half_t)
            def _(l):
                raw = dot(mats[1, l], alph[l, g])
                fill_emission(l, g)
                sums = ext_row_of(raw, 0)
                put_row(srow, l - 1, g, sums)
                forward_step(l, l.astype(F32), g, raw, [1.0 / v for v in sums])

        first_pass(mine)
        send_cross()
        first_pass(other)
        logs = jnp.zeros((per_group, 128), F32)
        for g in range(groups):
            put_row(srow, half_t - 1, g, ext_row_of(dot(exts[...], alph[half_t, g]), 0))
            for l in range(half_t):
                seen = (float(l) >= span[0, g]) & (float(l) < span[1, g])
                if l == half_t - 1:
                    seen = seen & (span[1, g] == float(half_t))
                logs = logs + jnp.where(seen, jnp.log(srow[l, g]), 0.0)
        irow[...] = 1.0 / srow[...]
        send_ll(logs)

        def put_u(l, t, g, get):
            on = moving(t + 1.0, g)
            gain = [jnp.where(a, b, 0.0) for a, b in zip(moving(t, g), row(irow, l - 1, g))]
            inv_s = row(irow, l, g)
            for m, cc, c0, r, rr in cells:
                y = jnp.where(on[m], get(m, cc, c0, r, rr), inv_s[m])
                back_u[l, g, rr, cc] = (emem[l, g, rr, cc] * y * gain[m]).astype(BF)

        def second_pass(g, last):
            inv_q = [1.0 / v for v in junction(g)]
            put_u(half_t - 1, float(half_t - 1), g,
                  lambda m, cc, c0, r, rr: alph[0, g, rr, cc].astype(F32) * inv_q[m])

            @pl.loop(0, half_t - 2)
            def _(k):
                l = half_t - 1 - k
                raw = dot(mats[0, l], back_u[l, g])
                add_counts(l, dot_nt(alph[l, g, zrow, :], back_u[l, g]), last)
                put_u(l - 1, (l - 1).astype(F32), g, lambda m, cc, c0, r, rr: piece(raw, c0, r))

            add_counts(1, dot_nt(alph[1, g, zrow, :], back_u[1, g]), last)

        pass_on()
        second_pass(mine, False)
        take_other()
        second_pass(other, True)
        out[0] = jnp.zeros(out.shape[1:], F32)
        finish(range(half_t - 1, 0, -1))

    @pl.when(x == 1)
    def _late():
        top = half_t - 1

        def first_pass(g):
            fill_emission(top, g)
            for m, cc, c0, r, rr in cells:
                back_u[top, g, rr, cc] = emem[top, g, rr, cc].astype(BF)

            def back_step(l, t, put):
                raw = dot(mats[0, l], back_u[l, g])
                sums = ext_row_of(raw, 0)
                put_row(srow, l, g, sums)
                put_row(yrow, l, g, ext_row_of(raw, 1))
                inv = [1.0 / v for v in sums]
                on = moving(t, g)
                for m, cc, c0, r, rr in cells:
                    put(rr, cc, jnp.where(on[m], piece(raw, c0, r) * inv[m], 1.0))

            @pl.loop(0, top)
            def _(k):
                l = top - k
                fill_emission(l - 1, g)

                def put(rr, cc, v):
                    back_u[l - 1, g, rr, cc] = (v * emem[l - 1, g, rr, cc]).astype(BF)

                back_step(l, (l + half_t).astype(F32), put)

            def put(rr, cc, v):
                alph[half_t, g, rr, cc] = v.astype(BF)

            back_step(0, float(half_t), put)

        first_pass(mine)
        send_cross()
        first_pass(other)
        logs = jnp.zeros((per_group, 128), F32)
        for g in range(groups):
            for l in range(half_t):
                t = float(l + half_t)
                on = (t > span[0, g]) & (t < span[1, g])
                logs = logs + jnp.where(on, jnp.log(srow[l, g]), 0.0)
                logs = logs + jnp.where(span[0, g] == t, jnp.log(yrow[l, g]), 0.0)

        def join(g):
            q = junction(g)
            put_row(span, 2, g, q)
            put_row(span, 3, g, q)
            t = float(half_t)
            return jnp.where((t > span[0, g]) & (t < span[1, g]), jnp.log(span[2, g]), 0.0)

        def second_pass(g, last):
            def one(l, t, sums):
                inv = [1.0 / v for v in sums]
                on = moving(t, g)
                scaled = []
                for m in range(per_group):
                    cc = pl.ds(m * 128, 128)
                    d = jnp.where(span[0, g, m:m + 1, :] == t - 1.0, span[3, g, m:m + 1, :], span[2, g, m:m + 1, :])
                    d = d * inv[m] * srow[l, g, m:m + 1, :]
                    span[2, g, m:m + 1, :] = d
                    span[3, g, m:m + 1, :] = yrow[l, g, m:m + 1, :]
                    w = jnp.where(on[m], 1.0 / d, 0.0)
                    scaled.append((alph[l, g, zrow, cc].astype(F32) * inv[m] * w).astype(BF))
                add_counts(l, dot_nt(jnp.concatenate(scaled, axis=1), back_u[l, g]), last)
                return inv

            @pl.loop(0, top)
            def _(l):
                raw = dot(mats[1, l], alph[l, g])
                t = (l + half_t).astype(F32)
                inv = one(l, t, ext_row_of(raw, 0))
                forward_step(l, t, g, raw, inv)

            one(top, float(top + half_t), ext_row_of(dot(exts[...], alph[top, g]), 0))

        pass_on()
        logs = logs + join(mine)
        second_pass(mine, False)
        take_other()
        send_ll(logs + join(other))
        second_pass(other, True)
        finish(range(half_t))

    for c in hist + near:
        c.wait_send()
    for k in range(parts):
        cross(k).wait_send()
        onward(k, mine).wait_send()


def write_out(grad, ll, out, llout, sem):
    c = pltpu.make_async_copy(grad, out, sem)
    c.start()
    llout[0] = ll[0, 0]
    c.wait()


def fused_device(
    earnings, starts, lengths, block_count, trans_logits, init_logits, state_mean, log_sd
):
    num_states = init_logits.shape[0]
    nt = earnings.shape[1]
    slot_rows = earnings.shape[0]
    cap = slot_rows // HB
    nz = lax.axis_size("hh")
    nsrc = nz * 2
    own_t = trans_logits.shape[0]
    half_t = nt // 2
    half = num_states // 2
    zr = num_states // nz
    lanes = 256
    groups = nsrc * HB // 2 // lanes
    wide = groups * lanes
    parts = 4
    cfg = (nz, nt, half_t, own_t, num_states, groups, lanes, parts)
    V = pltpu.VMEM
    D = pltpu.SemaphoreType.DMA
    vm = pl.BlockSpec(memory_space=pltpu.VMEM)
    sm = pl.BlockSpec(memory_space=pltpu.SMEM)
    hbm = pl.BlockSpec(memory_space=pltpu.HBM)
    pinned = lambda v: pltpu.with_memory_space_constraint(v, pltpu.HBM)
    held = lambda v: pltpu.with_memory_space_constraint(v, pltpu.VMEM)
    rows_of = V((half_t, groups, lanes // 128, 128), F32)
    grad, ll = pl.pallas_call(
        functools.partial(fused_kernel, cfg),
        out_shape=(pltpu.VMEM((half_t, zr, half), F32), pltpu.VMEM((1, 128), F32)),
        in_specs=[hbm, hbm, hbm, sm, hbm, hbm, hbm, hbm],
        out_specs=(vm, vm),
        scratch_shapes=[
            V((nt, slot_rows), F32), V((cap, HB), jnp.int32), V((cap, HB), jnp.int32), V((3, 1, num_states), F32),
            V((2, 8, 256), F32),
            V((nsrc, 8, 256), F32),
            rows_of,
            V((4, groups, lanes // 128, 128), F32),
            V((half_t, num_states, num_states), BF),
            V((2, half_t, EXT + num_states, num_states), BF),
            V((4, num_states, 128), F32),
            V((EXT, num_states), BF),
            V((half_t + 1, groups, num_states, lanes), BF),
            V((half_t, groups, num_states, lanes), BF),
            V((half_t, groups, num_states, lanes), F32),
            rows_of, rows_of, rows_of,
            V((half_t, zr, num_states), F32),
            V((half_t, zr, num_states), F32),
            V((half_t, zr, num_states), F32),
            V((4, 8, 128), F32),
            V((2, 8, 128), F32),
            D((6,)), D((nsrc - 1,)), D((nsrc,)), D((2 * own_t,)), D((own_t,)),
            D((parts,)), D((parts,)), D((parts,)), D((parts,)), D((half_t,)), D((half_t,)),
            D((3,)), D((3,)), D((2,)),
        ],
        compiler_params=pltpu.CompilerParams(
            collective_id=0, has_side_effects=True, vmem_limit_bytes=40 * 1024 * 1024),
        name="chain",
    )(pinned(earnings.T), pinned(starts.reshape(cap, HB)), pinned(lengths.reshape(cap, HB)), block_count,
      pinned(trans_logits), pinned(init_logits[None]), pinned(state_mean[None]), pinned(log_sd[None]))
    return pl.pallas_call(
        write_out,
        out_shape=(jax.ShapeDtypeStruct(grad.shape, F32), jax.ShapeDtypeStruct((1,), F32)),
        in_specs=[vm, vm],
        out_specs=(hbm, sm),
        scratch_shapes=[pltpu.SemaphoreType.DMA],
        name="write_out",
    )(held(grad), held(ll))


def solution(mesh):
    fits = mesh.shape["per"] == 2 and mesh.shape["st"] == 2 and mesh.shape["hh"] == 4
    body = fused_device if fits else per_device
    placed = (
        P(("hh", "per"), None),
        P(("hh", "per")),
        P(("hh", "per")),
        P(("hh", "per")),
        P(("grp", "per", "st"), None, None),
        P("grp"),
        P("grp"),
        P("grp"),
    )
    return jax.shard_map(
        body,
        mesh=mesh,
        in_specs=placed,
        out_specs=(P(("grp", "per"), "hh", "st"), P("grp")),
        check_vma=False,
    )
```

```python
import functools

import jax
import jax.numpy as jnp
from jax import lax
from jax.sharding import PartitionSpec as P
from jax.experimental import pallas as pl
from jax.experimental.pallas import tpu as pltpu

HB = 128


top_precision = lax.Precision.HIGHEST


def emission(column, state_mean, log_sd):
    z_score = (column[:, None] - state_mean[None, :]) / jnp.exp(log_sd)[None, :]
    return jnp.exp(-0.5 * z_score * z_score - log_sd[None, :])


def per_device(
    earnings, starts, lengths, block_count, trans_logits, init_logits, state_mean, log_sd
):
    num_states = init_logits.shape[0]
    num_periods = earnings.shape[1]
    slot_rows = earnings.shape[0]
    group_size = lax.axis_size(("hh", "per"))
    core_count = lax.axis_size("st")
    half_states = num_states // core_count
    lead_state = lax.axis_index("st") * half_states
    whole_logits = lax.all_gather(trans_logits, ("per", "st"), axis=0, tiled=True)
    raised = jnp.exp(whole_logits.astype(jnp.float32))
    trans_probs = raised / jnp.sum(raised, axis=2, keepdims=True)
    raised_first = jnp.exp(init_logits)
    first_probs = raised_first / jnp.sum(raised_first)
    source_rows = slot_rows // group_size
    count_out = jnp.broadcast_to(block_count.reshape(1, 1), (1, group_size))
    got_earn, got_start, got_len, got_count = (
        lax.all_to_all(
            earnings.reshape(source_rows, group_size, num_periods),
            ("hh", "per"),
            split_axis=1,
            concat_axis=1,
            tiled=True,
        ),
        lax.all_to_all(
            starts.reshape(source_rows, group_size),
            ("hh", "per"),
            split_axis=1,
            concat_axis=1,
            tiled=True,
        ),
        lax.all_to_all(
            lengths.reshape(source_rows, group_size),
            ("hh", "per"),
            split_axis=1,
            concat_axis=1,
            tiled=True,
        ),
        lax.all_to_all(count_out, ("hh", "per"), split_axis=1, concat_axis=1, tiled=True),
    )
    per_source = got_count[0] * (HB // group_size)
    source_order = jnp.arange(group_size, dtype=jnp.int32)
    up_to = source_order[None, :] <= source_order[:, None]
    ends_at = jnp.sum(jnp.where(up_to, per_source[None, :], 0), axis=1)
    target_ids = jnp.arange(HB, dtype=jnp.int32)
    before_mask = ends_at[None, :] <= target_ids[:, None]
    source_ids = jnp.sum(before_mask.astype(jnp.int32), axis=1)
    begins_at = jnp.sum(jnp.where(before_mask, per_source[None, :], 0), axis=1)
    pick_ids = (target_ids - begins_at) * group_size + source_ids
    rows_earn = jnp.take(got_earn.reshape(source_rows * group_size, num_periods), pick_ids, axis=0)
    rows_start = jnp.take(got_start.reshape(source_rows * group_size), pick_ids)
    rows_len = jnp.take(got_len.reshape(source_rows * group_size), pick_ids)
    row_live = jnp.ones((HB,), dtype=bool)
    years_local = jnp.sum(jnp.where(row_live, rows_len, 0)).astype(jnp.float32)
    row_total_count = rows_earn.shape[0]
    columns = rows_earn.T
    period_ids = jnp.arange(num_periods, dtype=jnp.int32)

    def observed(step_now):
        return row_live & (step_now >= rows_start) & (step_now < rows_start + rows_len)

    def forward(prev_alpha, inputs):
        matrix, column, step_now = inputs
        fresh_start = (step_now <= rows_start)[:, None]
        moved_mass = jnp.dot(
            prev_alpha, matrix, precision=top_precision, preferred_element_type=jnp.float32
        )
        joint_mass = jnp.where(fresh_start, first_probs[None, :], moved_mass) * emission(
            column, state_mean, log_sd
        )
        seen_now = observed(step_now)
        scale_now = jnp.where(seen_now, jnp.sum(joint_mass, axis=1), 1.0)
        new_alpha = jnp.where(seen_now[:, None], joint_mass / scale_now[:, None], prev_alpha)
        return (new_alpha, (new_alpha, scale_now))

    start_alpha = jnp.broadcast_to(first_probs[None, :], (row_total_count, num_states))
    _, (alphas, scales) = lax.scan(forward, start_alpha, (trans_probs, columns, period_ids))

    def carry_of(back_now, column, scale_now, step_now):
        seen_now = observed(step_now)
        return jnp.where(
            seen_now[:, None],
            emission(column, state_mean, log_sd) * back_now / scale_now[:, None],
            0.0,
        )

    def backward(carry_now, inputs):
        matrix, alpha_prev, column_prev, scale_prev, step_now = inputs
        moving = row_live & (step_now > rows_start) & (step_now < rows_start + rows_len)
        weights = jnp.where(moving[:, None], alpha_prev, 0.0)
        own_carry = lax.dynamic_slice_in_dim(carry_now, lead_state, half_states, 1)
        grad_term = lax.dot_general(
            weights,
            own_carry,
            (((0,), (0,)), ((), ())),
            precision=top_precision,
            preferred_element_type=jnp.float32,
        )
        pulled = lax.dot_general(
            carry_now,
            matrix,
            (((1,), (1,)), ((), ())),
            precision=top_precision,
            preferred_element_type=jnp.float32,
        )
        back_now = jnp.where(moving[:, None], pulled, 1.0)
        return (carry_of(back_now, column_prev, scale_prev, step_now - 1), grad_term)

    ones_back = jnp.ones((row_total_count, num_states), jnp.float32)
    last_carry = carry_of(
        ones_back, columns[num_periods - 1], scales[num_periods - 1], num_periods - 1
    )
    _, grad_terms = lax.scan(
        backward,
        last_carry,
        (trans_probs[1:], alphas[:-1], columns[:-1], scales[:-1], period_ids[1:]),
        reverse=True,
    )
    zero_first = jnp.zeros((1,) + grad_terms.shape[1:], jnp.float32)
    partial_counts = jnp.concatenate([zero_first, grad_terms], axis=0)
    loglik_local = jnp.sum(jnp.log(scales))
    summed = lax.psum_scatter(partial_counts, "hh", scatter_dimension=1, tiled=True)
    summed = lax.psum_scatter(summed, "per", scatter_dimension=0, tiled=True)
    loglik_share = loglik_local / core_count
    years_share = years_local / core_count
    period_block = summed.shape[0]
    row_block_size = summed.shape[1]
    local_probs = lax.dynamic_slice(
        trans_probs,
        (lax.axis_index("per") * period_block, lax.axis_index("hh") * row_block_size, lead_state),
        (period_block, row_block_size, half_states),
    )
    weighted = local_probs * summed
    row_total, loglik_core, years_core = lax.psum(
        (jnp.sum(weighted, axis=2), loglik_share, years_share), "st"
    )
    loglik_all, years_all = lax.psum((loglik_core, years_core), ("hh", "per"))
    factor = float(num_states * num_states * num_periods) / years_all
    trans_grad = factor * (weighted - local_probs * row_total[:, :, None])
    mean_loglik = jnp.reshape(loglik_all / years_all, (1,))
    return (trans_grad, mean_loglik)


F32 = jnp.float32
BF = jnp.bfloat16
MESH = pl.DeviceIdType.MESH
EXT = 16
LOG2E = 1.4426950408889634
NT_DIMS = (((1,), (1,)), ((), ()))


def dot(p, q):
    return jnp.dot(p, q, preferred_element_type=F32)


def dot_nt(p, q):
    return lax.dot_general(p, q, NT_DIMS, preferred_element_type=F32)


def fused_kernel(cfg, earn_h, begin_h, length_h, count, logits, init_h, mean_h, sd_h, out, llout,
                 earn, begin, length, params, pack, got, people, span, lg, mats, cols, exts, alph, back_u, emem,
                 srow, irow, yrow, weighed, cacc, crecv, prb, llbox, ybox,
                 in_sem, hs_sem, hr_sem, lr_sem, ls_sem, xs_sem, xr_sem, fs_sem, fr_sem, cs_sem, cr_sem,
                 lls_sem, llr_sem, y_sem):
    nz, nt, half_t, own_t, num_states, groups, lanes, parts = cfg
    x = lax.axis_index("per")
    z = lax.axis_index("hh")
    s = lax.axis_index("st")
    half = num_states // 2
    nsrc = nz * 2
    zr = num_states // nz
    per_group = lanes // 128
    chunk = 64
    first_core = s == 0

    def rcopy(src, dst, ss, rs, dev):
        return pltpu.make_async_remote_copy(
            src_ref=src, dst_ref=dst, send_sem=ss, recv_sem=rs,
            device_id=dev, device_id_type=MESH)

    partner = {"hh": z, "per": x, "st": 1 - s}
    across = {"hh": z, "per": 1 - x, "st": s}
    corner = {"hh": z, "per": 1 - x, "st": 1 - s}
    mine = lax.rem(z, 2)
    other = 1 - mine
    pair = {"hh": z + 1 - 2 * mine, "per": x, "st": s}
    peers = []
    for dz in range(nz):
        for dx in range(2):
            if dz or dx:
                px = x if dx == 0 else 1 - x
                peers.append((px, {"hh": lax.rem(z + dz, nz), "per": px, "st": s}))

    loads = [pltpu.make_async_copy(src, dst, in_sem.at[i]) for i, (src, dst) in enumerate([
        (earn_h, earn), (begin_h, begin), (length_h, length),
        (init_h, params.at[0]), (mean_h, params.at[1]), (sd_h, params.at[2])])]
    for c in loads:
        c.start()
    barrier = pltpu.get_barrier_semaphore()
    for dev in [d for _, d in peers] + [partner, corner]:
        pl.semaphore_signal(barrier, inc=1, device_id=dev, device_id_type=MESH)
    local = []
    for i in range(own_t):
        c = pltpu.make_async_copy(logits.at[i], lg.at[i], lr_sem.at[i])
        c.start()
        local.append(c)

    low = lax.broadcasted_iota(jnp.int32, (8, 128), 1) < 64

    def to_low(v):
        return jnp.where(first_core, v, pltpu.roll(v, 64, 1))

    def to_high(v):
        return jnp.where(first_core, pltpu.roll(v, 64, 1), v)

    for c in loads[:3]:
        c.wait()
    cnt = count[0].astype(F32)
    about = jnp.concatenate(
        [begin[...].astype(F32), length[...].astype(F32), jnp.full((2, 128), 1.0, F32) * cnt], axis=0)
    about = to_high(about)
    for h in range(2):
        e = [earn[h * half_t:(h + 1) * half_t, b * 128:(b + 1) * 128] for b in range(3)]
        pack[h, :, 0:128] = jnp.where(low, to_low(e[0]), to_high(e[1]))
        pack[h, :, 128:256] = jnp.where(low, to_low(e[2]), about)

    zrow = pl.ds(pl.multiple_of(z * zr, zr), zr)

    def make_probs(i):
        l = own_t * s + i
        ext = exts[...]
        eye = jnp.where(lax.broadcasted_iota(jnp.int32, (num_states, num_states), 0)
                        == lax.broadcasted_iota(jnp.int32, (num_states, num_states), 1), 1.0, 0.0).astype(BF)
        r = jnp.exp(lg[i].astype(F32))
        p = (r * (1.0 / jnp.sum(r, axis=1, keepdims=True))).astype(BF)
        mats[0, l, 0:EXT] = ext
        mats[1, l, 0:EXT] = ext
        mats[0, l, EXT:] = p
        mats[1, l, EXT:] = dot_nt(eye, p).astype(BF)
        rz = jnp.exp(lg[i, zrow, :].astype(F32))
        prb[l] = rz / jnp.sum(rz, axis=1, keepdims=True)

    def own_work():
        for c in loads[3:]:
            c.wait()
        mean = params[1]
        log_sd = params[2]
        raised_first = jnp.exp(params[0])
        first = raised_first / jnp.sum(raised_first, axis=1, keepdims=True)
        slope = jnp.exp(-log_sd) * ((0.5 * LOG2E) ** 0.5)
        for i, v in enumerate([slope, slope * mean, log_sd * (-LOG2E), first]):
            cols[i] = jnp.broadcast_to(v, (128, num_states)).T
        ext_row = lax.broadcasted_iota(jnp.int32, (EXT, num_states), 0)
        exts[...] = jnp.where(ext_row == 0, 1.0, jnp.where(
            ext_row == 1, jnp.broadcast_to(first, (EXT, num_states)), 0.0)).astype(BF)
        for c in local:
            c.wait()

        @pl.loop(0, own_t)
        def _(i):
            make_probs(i)

    own_span = pl.ds(own_t * s, own_t)
    near = []
    for i in range(own_t):
        at = (1 - x, own_t * s + i)
        near.append(rcopy(mats.at[at], mats.at[at], ls_sem.at[i], lr_sem.at[own_t + i], partner))
    rest = [rcopy(mats.at[x, own_span], mats.at[x, own_span], ls_sem.at[own_t], lr_sem.at[2 * own_t], partner),
            rcopy(prb.at[own_span], prb.at[own_span], ls_sem.at[own_t + 1], lr_sem.at[2 * own_t + 1], partner)]

    @pl.when(z < nz - 1)
    def _():
        own_work()

    pl.semaphore_wait(barrier, len(peers) + 2)

    @pl.when(z < nz - 1)
    def _():
        for c in near:
            c.start()

    me_src = z * 2 + x
    hist = []
    for n, (px, dev) in enumerate(peers):
        c = rcopy(pack.at[px], got.at[me_src], hs_sem.at[n], hr_sem.at[me_src], dev)
        c.start()
        hist.append(c)
    pltpu.make_async_copy(pack.at[x], got.at[me_src], hr_sem.at[me_src]).start()

    @pl.when(z == nz - 1)
    def _():
        own_work()
        for c in near:
            c.start()

    for c in rest:
        c.start()

    tiles = groups * per_group
    high_bit = jnp.where(lax.broadcasted_iota(jnp.int32, (1, 128), 1) < 64, 0.0, 1.0)
    base = jnp.zeros((1, 128), F32)
    xs = [jnp.zeros((8, 128), F32) for _ in range(tiles)]
    starts = [jnp.zeros((1, 128), F32) for _ in range(tiles)]
    spans = [jnp.zeros((1, 128), F32) for _ in range(tiles)]
    for d in range(nsrc):
        rcopy(pack.at[0], got.at[d], hs_sem.at[0], hr_sem.at[d], across).wait_recv()
        t0, t1 = got[d, :, 0:128], got[d, :, 128:256]
        r0, r1 = pltpu.roll(t0, 64, 1), pltpu.roll(t1, 64, 1)
        held = [jnp.where(low, t0, r0), jnp.where(low, r0, t0), jnp.where(low, t1, r1)]
        about = jnp.where(low, r1, t1)
        live = about[6:7]
        for b in range(3):
            spot = jnp.where(live > float(b), base + float(b), -2.0) - high_bit
            for m in range(tiles):
                hit = spot == float(2 * m)
                xs[m] = jnp.where(hit, held[b], xs[m])
                starts[m] = jnp.where(hit, about[b:b + 1], starts[m])
                spans[m] = jnp.where(hit, about[3 + b:4 + b], spans[m])
        base = base + live
    years_own = jnp.zeros((1, 1), F32)
    for m in range(tiles):
        g, c = m // per_group, m % per_group
        for t in range(half_t):
            people[t, g, c:c + 1, :] = xs[m][t:t + 1]
        span[0, g, c:c + 1, :] = starts[m]
        span[1, g, c:c + 1, :] = starts[m] + spans[m]
        years_own = years_own + jnp.sum(spans[m], axis=1, keepdims=True)
    ybox[0] = jnp.broadcast_to(years_own, (8, 128))
    yc = rcopy(ybox.at[0], ybox.at[1], y_sem.at[0], y_sem.at[1], partner)
    yc.start()

    for c in near:
        c.wait_recv()

    cells = [(m, pl.ds(m * 128, 128), m * 128, r, pl.ds(r, chunk))
             for m in range(per_group) for r in range(0, num_states, chunk)]

    def row(ref, l, g):
        return [ref[l, g, m:m + 1, :] for m in range(per_group)]

    def put_row(ref, l, g, vals):
        for m in range(per_group):
            ref[l, g, m:m + 1, :] = vals[m]

    def ext_row_of(raw, i):
        return [raw[i:i + 1, m * 128:(m + 1) * 128] for m in range(per_group)]

    def piece(raw, c0, r):
        return raw[EXT + r:EXT + r + chunk, c0:c0 + 128]

    def moving(t, g):
        return [(t > a) & (t < b) for a, b in zip(row(span, 0, g), row(span, 1, g))]

    def fill_emission(l, g):
        xrow = row(people, l, g)
        for m, cc, c0, r, rr in cells:
            off = cols[0, rr, :] * xrow[m] - cols[1, rr, :]
            emem[l, g, rr, cc] = jnp.exp2(cols[2, rr, :] - off * off)

    def forward_step(l, t, g, raw, inv):
        fresh = [t <= a for a in row(span, 0, g)]
        for m, cc, c0, r, rr in cells:
            moved = jnp.where(fresh[m], cols[3, rr, :], piece(raw, c0, r) * inv[m])
            alph[l + 1, g, rr, cc] = (moved * emem[l, g, rr, cc]).astype(BF)

    def part_rows(k):
        return pl.ds(k * (num_states // parts), num_states // parts)

    def cross(k):
        return rcopy(alph.at[half_t, mine, part_rows(k)], alph.at[0, mine, part_rows(k)],
                     xs_sem.at[k], xr_sem.at[k], across)

    def onward(k, g):
        return rcopy(alph.at[0, g, part_rows(k)], alph.at[0, g, part_rows(k)], fs_sem.at[k], fr_sem.at[k], pair)

    def send_cross():
        for k in range(parts):
            cross(k).start()

    def pass_on():
        for c in rest:
            c.wait_recv()
        for k in range(parts):
            cross(k).wait_recv()
            onward(k, mine).start()

    def take_other():
        for k in range(parts):
            onward(k, other).wait_recv()

    def junction(g):
        q = []
        for m in range(per_group):
            acc = jnp.zeros((chunk, 128), F32)
            for r in range(0, num_states, chunk):
                rr, cc = pl.ds(r, chunk), pl.ds(m * 128, 128)
                acc = acc + alph[half_t, g, rr, cc].astype(F32) * alph[0, g, rr, cc].astype(F32)
            q.append(jnp.sum(acc, axis=0, keepdims=True))
        return q

    def counts_copy(l):
        return rcopy(cacc.at[l], crecv.at[l], cs_sem.at[l], cr_sem.at[l], partner)

    def add_counts(l, v, last):
        if last:
            cacc[l] = cacc[l] + v
            counts_copy(l).start()
        else:
            cacc[l] = v

    def send_ll(logs):
        llbox[x * 2 + s] = jnp.broadcast_to(
            jnp.sum(jnp.sum(logs, axis=0, keepdims=True), axis=1, keepdims=True), (8, 128))
        at = x * 2 + s
        for j, dev in enumerate([partner, across, corner]):
            rcopy(llbox.at[at], llbox.at[at], lls_sem.at[j], llr_sem.at[j], dev).start()

    def finish(order):
        yc.wait()
        years = ybox[0, 0:1, 0:1] + ybox[1, 0:1, 0:1]
        factor = float(num_states * num_states * nt) / years
        at = x * 2 + s
        for j, dev in enumerate([partner, across, corner]):
            rcopy(llbox.at[at], llbox.at[at], lls_sem.at[j], llr_sem.at[j], dev).wait()
        ll = (llbox[0, 0:1, :] + llbox[1, 0:1, :]) + (llbox[2, 0:1, :] + llbox[3, 0:1, :])
        llout[...] = ll / years
        order = list(order)
        for n, l in enumerate(order):
            if n == 0:
                for k in order[:-2]:
                    counts_copy(k).wait()
            if n >= len(order) - 2:
                counts_copy(l).wait()
            w = prb[l] * (cacc[l] + crecv[l])
            total = jnp.sum(w, axis=1, keepdims=True)
            w_own = jnp.where(first_core, w[:, :half], w[:, half:])
            p_own = jnp.where(first_core, prb[l, :, :half], prb[l, :, half:])
            out[l] = factor * (w_own - p_own * total)

    @pl.when(x == 0)
    def _early():
        def first_pass(g):
            fill_emission(0, g)
            for m, cc, c0, r, rr in cells:
                alph[1, g, rr, cc] = (cols[3, rr, :] * emem[0, g, rr, cc]).astype(BF)

            @pl.loop(1, half_t)
            def _(l):
                raw = dot(mats[1, l], alph[l, g])
                fill_emission(l, g)
                sums = ext_row_of(raw, 0)
                put_row(srow, l - 1, g, sums)
                forward_step(l, l.astype(F32), g, raw, [1.0 / v for v in sums])

        first_pass(mine)
        send_cross()
        first_pass(other)
        logs = jnp.zeros((per_group, 128), F32)
        for g in range(groups):
            put_row(srow, half_t - 1, g, ext_row_of(dot(exts[...], alph[half_t, g]), 0))
            for l in range(half_t):
                seen = (float(l) >= span[0, g]) & (float(l) < span[1, g])
                if l == half_t - 1:
                    seen = seen & (span[1, g] == float(half_t))
                logs = logs + jnp.where(seen, jnp.log(srow[l, g]), 0.0)
        irow[...] = 1.0 / srow[...]
        send_ll(logs)

        def put_u(l, t, g, get):
            on = moving(t + 1.0, g)
            gain = [jnp.where(a, b, 0.0) for a, b in zip(moving(t, g), row(irow, l - 1, g))]
            inv_s = row(irow, l, g)
            for m, cc, c0, r, rr in cells:
                y = jnp.where(on[m], get(m, cc, c0, r, rr), inv_s[m])
                back_u[l, g, rr, cc] = (emem[l, g, rr, cc] * y * gain[m]).astype(BF)

        def second_pass(g, last):
            inv_q = [1.0 / v for v in junction(g)]
            put_u(half_t - 1, float(half_t - 1), g,
                  lambda m, cc, c0, r, rr: alph[0, g, rr, cc].astype(F32) * inv_q[m])

            def counts(l):
                add_counts(l, dot_nt(alph[l, g, zrow, :], back_u[l, g]), last)

            def step(l, t, ready):
                raw = dot(mats[0, l], back_u[l, g])
                if ready:
                    counts(l + 1)
                put_u(l - 1, t - 1.0, g, lambda m, cc, c0, r, rr: piece(raw, c0, r))

            step(half_t - 1, half_t - 1.0, False)

            @pl.loop(0, half_t - 3)
            def _(k):
                l = half_t - 2 - k
                step(l, l.astype(F32), True)

            counts(2)
            counts(1)

        pass_on()
        second_pass(mine, False)
        take_other()
        second_pass(other, True)
        out[0] = jnp.zeros(out.shape[1:], F32)
        finish(range(half_t - 1, 0, -1))

    @pl.when(x == 1)
    def _late():
        top = half_t - 1

        def first_pass(g):
            fill_emission(top, g)
            for m, cc, c0, r, rr in cells:
                back_u[top, g, rr, cc] = emem[top, g, rr, cc].astype(BF)

            def back_step(l, t, put):
                raw = dot(mats[0, l], back_u[l, g])
                sums = ext_row_of(raw, 0)
                put_row(srow, l, g, sums)
                put_row(yrow, l, g, ext_row_of(raw, 1))
                inv = [1.0 / v for v in sums]
                on = moving(t, g)
                for m, cc, c0, r, rr in cells:
                    put(rr, cc, jnp.where(on[m], piece(raw, c0, r) * inv[m], 1.0))

            @pl.loop(0, top)
            def _(k):
                l = top - k
                fill_emission(l - 1, g)

                def put(rr, cc, v):
                    back_u[l - 1, g, rr, cc] = (v * emem[l - 1, g, rr, cc]).astype(BF)

                back_step(l, (l + half_t).astype(F32), put)

            def put(rr, cc, v):
                alph[half_t, g, rr, cc] = v.astype(BF)

            back_step(0, float(half_t), put)

        first_pass(mine)
        send_cross()
        first_pass(other)
        logs = jnp.zeros((per_group, 128), F32)
        for g in range(groups):
            for l in range(half_t):
                t = float(l + half_t)
                on = (t > span[0, g]) & (t < span[1, g])
                logs = logs + jnp.where(on, jnp.log(srow[l, g]), 0.0)
                logs = logs + jnp.where(span[0, g] == t, jnp.log(yrow[l, g]), 0.0)

        def join(g):
            q = junction(g)
            put_row(span, 2, g, q)
            put_row(span, 3, g, q)
            t = float(half_t)
            return jnp.where((t > span[0, g]) & (t < span[1, g]), jnp.log(span[2, g]), 0.0)

        def second_pass(g, last):
            def weigh(l, t, sums):
                inv = [1.0 / v for v in sums]
                on = moving(t, g)
                for m in range(per_group):
                    cc = pl.ds(m * 128, 128)
                    d = jnp.where(span[0, g, m:m + 1, :] == t - 1.0, span[3, g, m:m + 1, :], span[2, g, m:m + 1, :])
                    d = d * inv[m] * srow[l, g, m:m + 1, :]
                    span[2, g, m:m + 1, :] = d
                    span[3, g, m:m + 1, :] = yrow[l, g, m:m + 1, :]
                    w = jnp.where(on[m], 1.0 / d, 0.0)
                    weighed[l, :, cc] = (alph[l, g, zrow, cc].astype(F32) * inv[m] * w).astype(BF)
                return inv

            def counts(l):
                add_counts(l, dot_nt(weighed[l], back_u[l, g]), last)

            def step(l, t, ready):
                raw = dot(mats[1, l], alph[l, g])
                if ready:
                    counts(l - 1)
                inv = weigh(l, t, ext_row_of(raw, 0))
                forward_step(l, t, g, raw, inv)

            step(0, float(half_t), False)

            @pl.loop(1, top)
            def _(l):
                step(l, (l + half_t).astype(F32), True)

            sums = ext_row_of(dot(exts[...], alph[top, g]), 0)
            counts(top - 1)
            weigh(top, float(top + half_t), sums)
            counts(top)

        pass_on()
        logs = logs + join(mine)
        second_pass(mine, False)
        take_other()
        send_ll(logs + join(other))
        second_pass(other, True)
        finish(range(half_t))

    for c in hist + near + rest:
        c.wait_send()
    for k in range(parts):
        cross(k).wait_send()
        onward(k, mine).wait_send()


def write_out(grad, ll, out, llout, sem):
    c = pltpu.make_async_copy(grad, out, sem)
    c.start()
    llout[0] = ll[0, 0]
    c.wait()


def fused_device(
    earnings, starts, lengths, block_count, trans_logits, init_logits, state_mean, log_sd
):
    num_states = init_logits.shape[0]
    nt = earnings.shape[1]
    slot_rows = earnings.shape[0]
    cap = slot_rows // HB
    nz = lax.axis_size("hh")
    nsrc = nz * 2
    own_t = trans_logits.shape[0]
    half_t = nt // 2
    half = num_states // 2
    zr = num_states // nz
    lanes = 256
    groups = nsrc * HB // 2 // lanes
    wide = groups * lanes
    parts = 4
    cfg = (nz, nt, half_t, own_t, num_states, groups, lanes, parts)
    V = pltpu.VMEM
    D = pltpu.SemaphoreType.DMA
    vm = pl.BlockSpec(memory_space=pltpu.VMEM)
    sm = pl.BlockSpec(memory_space=pltpu.SMEM)
    hbm = pl.BlockSpec(memory_space=pltpu.HBM)
    pinned = lambda v: pltpu.with_memory_space_constraint(v, pltpu.HBM)
    held = lambda v: pltpu.with_memory_space_constraint(v, pltpu.VMEM)
    rows_of = V((half_t, groups, lanes // 128, 128), F32)
    grad, ll = pl.pallas_call(
        functools.partial(fused_kernel, cfg),
        out_shape=(pltpu.VMEM((half_t, zr, half), F32), pltpu.VMEM((1, 128), F32)),
        in_specs=[hbm, hbm, hbm, sm, hbm, hbm, hbm, hbm],
        out_specs=(vm, vm),
        scratch_shapes=[
            V((nt, slot_rows), F32), V((cap, HB), jnp.int32), V((cap, HB), jnp.int32), V((3, 1, num_states), F32),
            V((2, 8, 256), F32),
            V((nsrc, 8, 256), F32),
            rows_of,
            V((4, groups, lanes // 128, 128), F32),
            V((own_t, num_states, num_states), BF),
            V((2, half_t, EXT + num_states, num_states), BF),
            V((4, num_states, 128), F32),
            V((EXT, num_states), BF),
            V((half_t + 1, groups, num_states, lanes), BF),
            V((half_t, groups, num_states, lanes), BF),
            V((half_t, groups, num_states, lanes), F32),
            rows_of, rows_of, rows_of,
            V((half_t, zr, lanes), BF),
            V((half_t, zr, num_states), F32),
            V((half_t, zr, num_states), F32),
            V((half_t, zr, num_states), F32),
            V((4, 8, 128), F32),
            V((2, 8, 128), F32),
            D((6,)), D((nsrc - 1,)), D((nsrc,)), D((2 * own_t + 2,)), D((own_t + 2,)),
            D((parts,)), D((parts,)), D((parts,)), D((parts,)), D((half_t,)), D((half_t,)),
            D((3,)), D((3,)), D((2,)),
        ],
        compiler_params=pltpu.CompilerParams(
            collective_id=0, has_side_effects=True, vmem_limit_bytes=40 * 1024 * 1024),
        name="chain",
    )(pinned(earnings.T), pinned(starts.reshape(cap, HB)), pinned(lengths.reshape(cap, HB)), block_count,
      pinned(trans_logits), pinned(init_logits[None]), pinned(state_mean[None]), pinned(log_sd[None]))
    return pl.pallas_call(
        write_out,
        out_shape=(jax.ShapeDtypeStruct(grad.shape, F32), jax.ShapeDtypeStruct((1,), F32)),
        in_specs=[vm, vm],
        out_specs=(hbm, sm),
        scratch_shapes=[pltpu.SemaphoreType.DMA],
        name="write_out",
    )(held(grad), held(ll))


def solution(mesh):
    fits = mesh.shape["per"] == 2 and mesh.shape["st"] == 2 and mesh.shape["hh"] == 4
    body = fused_device if fits else per_device
    placed = (
        P(("hh", "per"), None),
        P(("hh", "per")),
        P(("hh", "per")),
        P(("hh", "per")),
        P(("grp", "per", "st"), None, None),
        P("grp"),
        P("grp"),
        P("grp"),
    )
    return jax.shard_map(
        body,
        mesh=mesh,
        in_specs=placed,
        out_specs=(P(("grp", "per"), "hh", "st"), P("grp")),
        check_vma=False,
    )
```

```python
import functools

import jax
import jax.numpy as jnp
from jax import lax
from jax.sharding import PartitionSpec as P
from jax.experimental import pallas as pl
from jax.experimental.pallas import tpu as pltpu

HB = 128


top_precision = lax.Precision.HIGHEST


def emission(column, state_mean, log_sd):
    z_score = (column[:, None] - state_mean[None, :]) / jnp.exp(log_sd)[None, :]
    return jnp.exp(-0.5 * z_score * z_score - log_sd[None, :])


def per_device(
    earnings, starts, lengths, block_count, trans_logits, init_logits, state_mean, log_sd
):
    num_states = init_logits.shape[0]
    num_periods = earnings.shape[1]
    slot_rows = earnings.shape[0]
    group_size = lax.axis_size(("hh", "per"))
    core_count = lax.axis_size("st")
    half_states = num_states // core_count
    lead_state = lax.axis_index("st") * half_states
    whole_logits = lax.all_gather(trans_logits, ("per", "st"), axis=0, tiled=True)
    raised = jnp.exp(whole_logits.astype(jnp.float32))
    trans_probs = raised / jnp.sum(raised, axis=2, keepdims=True)
    raised_first = jnp.exp(init_logits)
    first_probs = raised_first / jnp.sum(raised_first)
    source_rows = slot_rows // group_size
    count_out = jnp.broadcast_to(block_count.reshape(1, 1), (1, group_size))
    got_earn, got_start, got_len, got_count = (
        lax.all_to_all(
            earnings.reshape(source_rows, group_size, num_periods),
            ("hh", "per"),
            split_axis=1,
            concat_axis=1,
            tiled=True,
        ),
        lax.all_to_all(
            starts.reshape(source_rows, group_size),
            ("hh", "per"),
            split_axis=1,
            concat_axis=1,
            tiled=True,
        ),
        lax.all_to_all(
            lengths.reshape(source_rows, group_size),
            ("hh", "per"),
            split_axis=1,
            concat_axis=1,
            tiled=True,
        ),
        lax.all_to_all(count_out, ("hh", "per"), split_axis=1, concat_axis=1, tiled=True),
    )
    per_source = got_count[0] * (HB // group_size)
    source_order = jnp.arange(group_size, dtype=jnp.int32)
    up_to = source_order[None, :] <= source_order[:, None]
    ends_at = jnp.sum(jnp.where(up_to, per_source[None, :], 0), axis=1)
    target_ids = jnp.arange(HB, dtype=jnp.int32)
    before_mask = ends_at[None, :] <= target_ids[:, None]
    source_ids = jnp.sum(before_mask.astype(jnp.int32), axis=1)
    begins_at = jnp.sum(jnp.where(before_mask, per_source[None, :], 0), axis=1)
    pick_ids = (target_ids - begins_at) * group_size + source_ids
    rows_earn = jnp.take(got_earn.reshape(source_rows * group_size, num_periods), pick_ids, axis=0)
    rows_start = jnp.take(got_start.reshape(source_rows * group_size), pick_ids)
    rows_len = jnp.take(got_len.reshape(source_rows * group_size), pick_ids)
    row_live = jnp.ones((HB,), dtype=bool)
    years_local = jnp.sum(jnp.where(row_live, rows_len, 0)).astype(jnp.float32)
    row_total_count = rows_earn.shape[0]
    columns = rows_earn.T
    period_ids = jnp.arange(num_periods, dtype=jnp.int32)

    def observed(step_now):
        return row_live & (step_now >= rows_start) & (step_now < rows_start + rows_len)

    def forward(prev_alpha, inputs):
        matrix, column, step_now = inputs
        fresh_start = (step_now <= rows_start)[:, None]
        moved_mass = jnp.dot(
            prev_alpha, matrix, precision=top_precision, preferred_element_type=jnp.float32
        )
        joint_mass = jnp.where(fresh_start, first_probs[None, :], moved_mass) * emission(
            column, state_mean, log_sd
        )
        seen_now = observed(step_now)
        scale_now = jnp.where(seen_now, jnp.sum(joint_mass, axis=1), 1.0)
        new_alpha = jnp.where(seen_now[:, None], joint_mass / scale_now[:, None], prev_alpha)
        return (new_alpha, (new_alpha, scale_now))

    start_alpha = jnp.broadcast_to(first_probs[None, :], (row_total_count, num_states))
    _, (alphas, scales) = lax.scan(forward, start_alpha, (trans_probs, columns, period_ids))

    def carry_of(back_now, column, scale_now, step_now):
        seen_now = observed(step_now)
        return jnp.where(
            seen_now[:, None],
            emission(column, state_mean, log_sd) * back_now / scale_now[:, None],
            0.0,
        )

    def backward(carry_now, inputs):
        matrix, alpha_prev, column_prev, scale_prev, step_now = inputs
        moving = row_live & (step_now > rows_start) & (step_now < rows_start + rows_len)
        weights = jnp.where(moving[:, None], alpha_prev, 0.0)
        own_carry = lax.dynamic_slice_in_dim(carry_now, lead_state, half_states, 1)
        grad_term = lax.dot_general(
            weights,
            own_carry,
            (((0,), (0,)), ((), ())),
            precision=top_precision,
            preferred_element_type=jnp.float32,
        )
        pulled = lax.dot_general(
            carry_now,
            matrix,
            (((1,), (1,)), ((), ())),
            precision=top_precision,
            preferred_element_type=jnp.float32,
        )
        back_now = jnp.where(moving[:, None], pulled, 1.0)
        return (carry_of(back_now, column_prev, scale_prev, step_now - 1), grad_term)

    ones_back = jnp.ones((row_total_count, num_states), jnp.float32)
    last_carry = carry_of(
        ones_back, columns[num_periods - 1], scales[num_periods - 1], num_periods - 1
    )
    _, grad_terms = lax.scan(
        backward,
        last_carry,
        (trans_probs[1:], alphas[:-1], columns[:-1], scales[:-1], period_ids[1:]),
        reverse=True,
    )
    zero_first = jnp.zeros((1,) + grad_terms.shape[1:], jnp.float32)
    partial_counts = jnp.concatenate([zero_first, grad_terms], axis=0)
    loglik_local = jnp.sum(jnp.log(scales))
    summed = lax.psum_scatter(partial_counts, "hh", scatter_dimension=1, tiled=True)
    summed = lax.psum_scatter(summed, "per", scatter_dimension=0, tiled=True)
    loglik_share = loglik_local / core_count
    years_share = years_local / core_count
    period_block = summed.shape[0]
    row_block_size = summed.shape[1]
    local_probs = lax.dynamic_slice(
        trans_probs,
        (lax.axis_index("per") * period_block, lax.axis_index("hh") * row_block_size, lead_state),
        (period_block, row_block_size, half_states),
    )
    weighted = local_probs * summed
    row_total, loglik_core, years_core = lax.psum(
        (jnp.sum(weighted, axis=2), loglik_share, years_share), "st"
    )
    loglik_all, years_all = lax.psum((loglik_core, years_core), ("hh", "per"))
    factor = float(num_states * num_states * num_periods) / years_all
    trans_grad = factor * (weighted - local_probs * row_total[:, :, None])
    mean_loglik = jnp.reshape(loglik_all / years_all, (1,))
    return (trans_grad, mean_loglik)


F32 = jnp.float32
BF = jnp.bfloat16
MESH = pl.DeviceIdType.MESH
EXT = 16
LOG2E = 1.4426950408889634
NT_DIMS = (((1,), (1,)), ((), ()))


def dot(p, q):
    return jnp.dot(p, q, preferred_element_type=F32)


def dot_nt(p, q):
    return lax.dot_general(p, q, NT_DIMS, preferred_element_type=F32)


def fused_kernel(cfg, earn_h, begin_h, length_h, count, logits, init_h, mean_h, sd_h, out, llout,
                 earn, begin, length, params, pack, got, people, span, lg, mats, cols, exts, alph, back_u, emem,
                 srow, irow, yrow, weighed, cacc, crecv, prb, llbox, ybox,
                 in_sem, hs_sem, hr_sem, lr_sem, ls_sem, xs_sem, xr_sem, fs_sem, fr_sem, cs_sem, cr_sem,
                 lls_sem, llr_sem, y_sem, up_sem):
    nz, nt, half_t, own_t, num_states, groups, lanes, parts = cfg
    x = lax.axis_index("per")
    z = lax.axis_index("hh")
    s = lax.axis_index("st")
    half = num_states // 2
    nsrc = nz * 2
    zr = num_states // nz
    per_group = lanes // 128
    chunk = 64
    first_core = s == 0

    def rcopy(src, dst, ss, rs, dev):
        return pltpu.make_async_remote_copy(
            src_ref=src, dst_ref=dst, send_sem=ss, recv_sem=rs,
            device_id=dev, device_id_type=MESH)

    partner = {"hh": z, "per": x, "st": 1 - s}
    across = {"hh": z, "per": 1 - x, "st": s}
    corner = {"hh": z, "per": 1 - x, "st": 1 - s}
    mine = lax.rem(z, 2)
    other = 1 - mine
    pair = {"hh": z + 1 - 2 * mine, "per": x, "st": s}
    peers = []
    for zt in range(nz):
        for dx in range(2):
            px = x if dx == 0 else 1 - x
            dev = {"hh": zt, "per": px, "st": s}
            beside = (z == zt) & (dx == 1)
            aside = beside | (zt != z)
            sends = aside & ((z > 0) | (zt < 2))
            hears = aside & ((zt > 0) | (z < 2))
            peers.append((px, dev, sends, hears))
    out_degree = jnp.where(z == 0, 5, nsrc + 1)

    loads = [pltpu.make_async_copy(src, dst, in_sem.at[i]) for i, (src, dst) in enumerate([
        (earn_h, earn), (begin_h, begin), (length_h, length),
        (init_h, params.at[0]), (mean_h, params.at[1]), (sd_h, params.at[2])])]
    for c in loads:
        c.start()
    barrier = pltpu.get_barrier_semaphore()
    for _, dev, _, hears in peers:
        @pl.when(hears)
        def _():
            pl.semaphore_signal(barrier, inc=1, device_id=dev, device_id_type=MESH)
    for dev in [partner, corner]:
        pl.semaphore_signal(barrier, inc=1, device_id=dev, device_id_type=MESH)
    local = []
    for i in range(own_t):
        c = pltpu.make_async_copy(logits.at[i], lg.at[i], lr_sem.at[i])
        c.start()
        local.append(c)

    low = lax.broadcasted_iota(jnp.int32, (8, 128), 1) < 64

    def to_low(v):
        return jnp.where(first_core, v, pltpu.roll(v, 64, 1))

    def to_high(v):
        return jnp.where(first_core, pltpu.roll(v, 64, 1), v)

    for c in loads[:3]:
        c.wait()
    cnt = count[0].astype(F32)
    about = jnp.concatenate(
        [begin[...].astype(F32), length[...].astype(F32), jnp.full((2, 128), 1.0, F32) * cnt], axis=0)
    about = to_high(about)
    for h in range(2):
        e = [earn[h * half_t:(h + 1) * half_t, b * 128:(b + 1) * 128] for b in range(3)]
        pack[h, :, 0:128] = jnp.where(low, to_low(e[0]), to_high(e[1]))
        pack[h, :, 128:256] = jnp.where(low, to_low(e[2]), about)

    zrow = pl.ds(pl.multiple_of(z * zr, zr), zr)

    def make_probs(i):
        l = own_t * s + i
        ext = exts[...]
        eye = jnp.where(lax.broadcasted_iota(jnp.int32, (num_states, num_states), 0)
                        == lax.broadcasted_iota(jnp.int32, (num_states, num_states), 1), 1.0, 0.0).astype(BF)
        r = jnp.exp(lg[i].astype(F32))
        p = (r * (1.0 / jnp.sum(r, axis=1, keepdims=True))).astype(BF)
        mats[0, l, 0:EXT] = ext
        mats[1, l, 0:EXT] = ext
        mats[0, l, EXT:] = p
        mats[1, l, EXT:] = dot_nt(eye, p).astype(BF)
        rz = jnp.exp(lg[i, zrow, :].astype(F32))
        prb[l] = rz / jnp.sum(rz, axis=1, keepdims=True)

    def own_work():
        for c in loads[3:]:
            c.wait()
        mean = params[1]
        log_sd = params[2]
        raised_first = jnp.exp(params[0])
        first = raised_first / jnp.sum(raised_first, axis=1, keepdims=True)
        slope = jnp.exp(-log_sd) * ((0.5 * LOG2E) ** 0.5)
        for i, v in enumerate([slope, slope * mean, log_sd * (-LOG2E), first]):
            cols[i] = jnp.broadcast_to(v, (128, num_states)).T
        ext_row = lax.broadcasted_iota(jnp.int32, (EXT, num_states), 0)
        exts[...] = jnp.where(ext_row == 0, 1.0, jnp.where(
            ext_row == 1, jnp.broadcast_to(first, (EXT, num_states)), 0.0)).astype(BF)
        for c in local:
            c.wait()

        @pl.loop(0, own_t)
        def _(i):
            make_probs(i)

    own_span = pl.ds(own_t * s, own_t)
    near = []
    for i in range(own_t):
        at = (1 - x, own_t * s + i)
        near.append(rcopy(mats.at[at], mats.at[at], ls_sem.at[i], lr_sem.at[own_t + i], partner))
    rest = [rcopy(mats.at[x, own_span], mats.at[x, own_span], ls_sem.at[own_t], lr_sem.at[2 * own_t], partner),
            rcopy(prb.at[own_span], prb.at[own_span], ls_sem.at[own_t + 1], lr_sem.at[2 * own_t + 1], partner)]

    @pl.when(z < nz - 2)
    def _():
        own_work()

    pl.semaphore_wait(barrier, out_degree)

    @pl.when(z < nz - 2)
    def _():
        for c in near:
            c.start()

    me_src = z * 2 + x
    for n, (px, dev, sends, _) in enumerate(peers):
        @pl.when(sends)
        def _():
            rcopy(pack.at[px], got.at[me_src], hs_sem.at[n], hr_sem.at[me_src], dev).start()
    pltpu.make_async_copy(pack.at[x], got.at[me_src], hr_sem.at[me_src]).start()

    @pl.when(z >= nz - 2)
    def _():
        own_work()
        for c in near:
            c.start()

    for c in rest:
        c.start()

    climbs = z == 1

    def climb(d, zt):
        return rcopy(got.at[d], got.at[d], up_sem.at[d * nz + zt], hr_sem.at[d], {"hh": zt, "per": x, "st": s})

    tiles = groups * per_group
    high_bit = jnp.where(lax.broadcasted_iota(jnp.int32, (1, 128), 1) < 64, 0.0, 1.0)
    base = jnp.zeros((1, 128), F32)
    xs = [jnp.zeros((8, 128), F32) for _ in range(tiles)]
    starts = [jnp.zeros((1, 128), F32) for _ in range(tiles)]
    spans = [jnp.zeros((1, 128), F32) for _ in range(tiles)]
    for d in range(nsrc):
        rcopy(pack.at[0], got.at[d], hs_sem.at[0], hr_sem.at[d], across).wait_recv()
        if d < 2:
            @pl.when(climbs)
            def _():
                for zt in range(nz - 1, 1, -1):
                    climb(d, zt).start()
        t0, t1 = got[d, :, 0:128], got[d, :, 128:256]
        r0, r1 = pltpu.roll(t0, 64, 1), pltpu.roll(t1, 64, 1)
        held = [jnp.where(low, t0, r0), jnp.where(low, r0, t0), jnp.where(low, t1, r1)]
        about = jnp.where(low, r1, t1)
        live = about[6:7]
        for b in range(3):
            spot = jnp.where(live > float(b), base + float(b), -2.0) - high_bit
            for m in range(tiles):
                hit = spot == float(2 * m)
                xs[m] = jnp.where(hit, held[b], xs[m])
                starts[m] = jnp.where(hit, about[b:b + 1], starts[m])
                spans[m] = jnp.where(hit, about[3 + b:4 + b], spans[m])
        base = base + live
    years_own = jnp.zeros((1, 1), F32)
    for m in range(tiles):
        g, c = m // per_group, m % per_group
        for t in range(half_t):
            people[t, g, c:c + 1, :] = xs[m][t:t + 1]
        span[0, g, c:c + 1, :] = starts[m]
        span[1, g, c:c + 1, :] = starts[m] + spans[m]
        years_own = years_own + jnp.sum(spans[m], axis=1, keepdims=True)
    ybox[0] = jnp.broadcast_to(years_own, (8, 128))
    yc = rcopy(ybox.at[0], ybox.at[1], y_sem.at[0], y_sem.at[1], partner)
    yc.start()

    for c in near:
        c.wait_recv()

    cells = [(m, pl.ds(m * 128, 128), m * 128, r, pl.ds(r, chunk))
             for m in range(per_group) for r in range(0, num_states, chunk)]

    def row(ref, l, g):
        return [ref[l, g, m:m + 1, :] for m in range(per_group)]

    def put_row(ref, l, g, vals):
        for m in range(per_group):
            ref[l, g, m:m + 1, :] = vals[m]

    def ext_row_of(raw, i):
        return [raw[i:i + 1, m * 128:(m + 1) * 128] for m in range(per_group)]

    def piece(raw, c0, r):
        return raw[EXT + r:EXT + r + chunk, c0:c0 + 128]

    def moving(t, g):
        return [(t > a) & (t < b) for a, b in zip(row(span, 0, g), row(span, 1, g))]

    def fill_emission(l, g):
        xrow = row(people, l, g)
        for m, cc, c0, r, rr in cells:
            off = cols[0, rr, :] * xrow[m] - cols[1, rr, :]
            emem[l, g, rr, cc] = jnp.exp2(cols[2, rr, :] - off * off)

    def forward_step(l, t, g, raw, inv):
        fresh = [t <= a for a in row(span, 0, g)]
        for m, cc, c0, r, rr in cells:
            moved = jnp.where(fresh[m], cols[3, rr, :], piece(raw, c0, r) * inv[m])
            alph[l + 1, g, rr, cc] = (moved * emem[l, g, rr, cc]).astype(BF)

    def part_rows(k):
        return pl.ds(k * (num_states // parts), num_states // parts)

    def cross(k):
        return rcopy(alph.at[half_t, mine, part_rows(k)], alph.at[0, mine, part_rows(k)],
                     xs_sem.at[k], xr_sem.at[k], across)

    def onward(k, g):
        return rcopy(alph.at[0, g, part_rows(k)], alph.at[0, g, part_rows(k)], fs_sem.at[k], fr_sem.at[k], pair)

    def send_cross():
        for k in range(parts):
            cross(k).start()

    def pass_on():
        for c in rest:
            c.wait_recv()
        for k in range(parts):
            cross(k).wait_recv()
            onward(k, mine).start()

    def take_other():
        for k in range(parts):
            onward(k, other).wait_recv()

    def junction(g):
        q = []
        for m in range(per_group):
            acc = jnp.zeros((chunk, 128), F32)
            for r in range(0, num_states, chunk):
                rr, cc = pl.ds(r, chunk), pl.ds(m * 128, 128)
                acc = acc + alph[half_t, g, rr, cc].astype(F32) * alph[0, g, rr, cc].astype(F32)
            q.append(jnp.sum(acc, axis=0, keepdims=True))
        return q

    def counts_copy(l):
        return rcopy(cacc.at[l], crecv.at[l], cs_sem.at[l], cr_sem.at[l], partner)

    def add_counts(l, v, last):
        if last:
            cacc[l] = cacc[l] + v
            counts_copy(l).start()
        else:
            cacc[l] = v

    def send_ll(logs):
        llbox[x * 2 + s] = jnp.broadcast_to(
            jnp.sum(jnp.sum(logs, axis=0, keepdims=True), axis=1, keepdims=True), (8, 128))
        at = x * 2 + s
        for j, dev in enumerate([partner, across, corner]):
            rcopy(llbox.at[at], llbox.at[at], lls_sem.at[j], llr_sem.at[j], dev).start()

    def finish(order):
        yc.wait()
        years = ybox[0, 0:1, 0:1] + ybox[1, 0:1, 0:1]
        factor = float(num_states * num_states * nt) / years
        at = x * 2 + s
        for j, dev in enumerate([partner, across, corner]):
            rcopy(llbox.at[at], llbox.at[at], lls_sem.at[j], llr_sem.at[j], dev).wait()
        ll = (llbox[0, 0:1, :] + llbox[1, 0:1, :]) + (llbox[2, 0:1, :] + llbox[3, 0:1, :])
        llout[...] = ll / years
        order = list(order)
        for n, l in enumerate(order):
            if n == 0:
                for k in order[:-2]:
                    counts_copy(k).wait()
            if n >= len(order) - 2:
                counts_copy(l).wait()
            w = prb[l] * (cacc[l] + crecv[l])
            total = jnp.sum(w, axis=1, keepdims=True)
            w_own = jnp.where(first_core, w[:, :half], w[:, half:])
            p_own = jnp.where(first_core, prb[l, :, :half], prb[l, :, half:])
            out[l] = factor * (w_own - p_own * total)

    @pl.when(x == 0)
    def _early():
        def first_pass(g):
            fill_emission(0, g)
            for m, cc, c0, r, rr in cells:
                alph[1, g, rr, cc] = (cols[3, rr, :] * emem[0, g, rr, cc]).astype(BF)

            @pl.loop(1, half_t)
            def _(l):
                raw = dot(mats[1, l], alph[l, g])
                fill_emission(l, g)
                sums = ext_row_of(raw, 0)
                put_row(srow, l - 1, g, sums)
                forward_step(l, l.astype(F32), g, raw, [1.0 / v for v in sums])

        first_pass(mine)
        send_cross()
        first_pass(other)
        logs = jnp.zeros((per_group, 128), F32)
        for g in range(groups):
            put_row(srow, half_t - 1, g, ext_row_of(dot(exts[...], alph[half_t, g]), 0))
            for l in range(half_t):
                seen = (float(l) >= span[0, g]) & (float(l) < span[1, g])
                if l == half_t - 1:
                    seen = seen & (span[1, g] == float(half_t))
                logs = logs + jnp.where(seen, jnp.log(srow[l, g]), 0.0)
        irow[...] = 1.0 / srow[...]
        send_ll(logs)

        def put_u(l, t, g, get):
            on = moving(t + 1.0, g)
            gain = [jnp.where(a, b, 0.0) for a, b in zip(moving(t, g), row(irow, l - 1, g))]
            inv_s = row(irow, l, g)
            for m, cc, c0, r, rr in cells:
                y = jnp.where(on[m], get(m, cc, c0, r, rr), inv_s[m])
                back_u[l, g, rr, cc] = (emem[l, g, rr, cc] * y * gain[m]).astype(BF)

        def second_pass(g, last):
            inv_q = [1.0 / v for v in junction(g)]
            put_u(half_t - 1, float(half_t - 1), g,
                  lambda m, cc, c0, r, rr: alph[0, g, rr, cc].astype(F32) * inv_q[m])

            def counts(l):
                add_counts(l, dot_nt(alph[l, g, zrow, :], back_u[l, g]), last)

            def step(l, t, ready):
                raw = dot(mats[0, l], back_u[l, g])
                if ready:
                    counts(l + 1)
                put_u(l - 1, t - 1.0, g, lambda m, cc, c0, r, rr: piece(raw, c0, r))

            step(half_t - 1, half_t - 1.0, False)

            @pl.loop(0, half_t - 3)
            def _(k):
                l = half_t - 2 - k
                step(l, l.astype(F32), True)

            counts(2)
            counts(1)

        pass_on()
        second_pass(mine, False)
        take_other()
        second_pass(other, True)
        out[0] = jnp.zeros(out.shape[1:], F32)
        finish(range(half_t - 1, 0, -1))

    @pl.when(x == 1)
    def _late():
        top = half_t - 1

        def first_pass(g):
            fill_emission(top, g)
            for m, cc, c0, r, rr in cells:
                back_u[top, g, rr, cc] = emem[top, g, rr, cc].astype(BF)

            def back_step(l, t, put):
                raw = dot(mats[0, l], back_u[l, g])
                sums = ext_row_of(raw, 0)
                put_row(srow, l, g, sums)
                put_row(yrow, l, g, ext_row_of(raw, 1))
                inv = [1.0 / v for v in sums]
                on = moving(t, g)
                for m, cc, c0, r, rr in cells:
                    put(rr, cc, jnp.where(on[m], piece(raw, c0, r) * inv[m], 1.0))

            @pl.loop(0, top)
            def _(k):
                l = top - k
                fill_emission(l - 1, g)

                def put(rr, cc, v):
                    back_u[l - 1, g, rr, cc] = (v * emem[l - 1, g, rr, cc]).astype(BF)

                back_step(l, (l + half_t).astype(F32), put)

            def put(rr, cc, v):
                alph[half_t, g, rr, cc] = v.astype(BF)

            back_step(0, float(half_t), put)

        first_pass(mine)
        send_cross()
        first_pass(other)
        logs = jnp.zeros((per_group, 128), F32)
        for g in range(groups):
            for l in range(half_t):
                t = float(l + half_t)
                on = (t > span[0, g]) & (t < span[1, g])
                logs = logs + jnp.where(on, jnp.log(srow[l, g]), 0.0)
                logs = logs + jnp.where(span[0, g] == t, jnp.log(yrow[l, g]), 0.0)

        def join(g):
            q = junction(g)
            put_row(span, 2, g, q)
            put_row(span, 3, g, q)
            t = float(half_t)
            return jnp.where((t > span[0, g]) & (t < span[1, g]), jnp.log(span[2, g]), 0.0)

        def second_pass(g, last):
            def weigh(l, t, sums):
                inv = [1.0 / v for v in sums]
                on = moving(t, g)
                for m in range(per_group):
                    cc = pl.ds(m * 128, 128)
                    d = jnp.where(span[0, g, m:m + 1, :] == t - 1.0, span[3, g, m:m + 1, :], span[2, g, m:m + 1, :])
                    d = d * inv[m] * srow[l, g, m:m + 1, :]
                    span[2, g, m:m + 1, :] = d
                    span[3, g, m:m + 1, :] = yrow[l, g, m:m + 1, :]
                    w = jnp.where(on[m], 1.0 / d, 0.0)
                    weighed[l, :, cc] = (alph[l, g, zrow, cc].astype(F32) * inv[m] * w).astype(BF)
                return inv

            def counts(l):
                add_counts(l, dot_nt(weighed[l], back_u[l, g]), last)

            def step(l, t, ready):
                raw = dot(mats[1, l], alph[l, g])
                if ready:
                    counts(l - 1)
                inv = weigh(l, t, ext_row_of(raw, 0))
                forward_step(l, t, g, raw, inv)

            step(0, float(half_t), False)

            @pl.loop(1, top)
            def _(l):
                step(l, (l + half_t).astype(F32), True)

            sums = ext_row_of(dot(exts[...], alph[top, g]), 0)
            counts(top - 1)
            weigh(top, float(top + half_t), sums)
            counts(top)

        pass_on()
        logs = logs + join(mine)
        second_pass(mine, False)
        take_other()
        send_ll(logs + join(other))
        second_pass(other, True)
        finish(range(half_t))

    for n, (px, dev, sends, _) in enumerate(peers):
        @pl.when(sends)
        def _():
            rcopy(pack.at[px], got.at[me_src], hs_sem.at[n], hr_sem.at[me_src], dev).wait_send()
    for d in range(2):
        @pl.when(climbs)
        def _():
            for zt in range(2, nz):
                climb(d, zt).wait_send()
    for c in near + rest:
        c.wait_send()
    for k in range(parts):
        cross(k).wait_send()
        onward(k, mine).wait_send()


def write_out(grad, ll, out, llout, sem):
    c = pltpu.make_async_copy(grad, out, sem)
    c.start()
    llout[0] = ll[0, 0]
    c.wait()


def fused_device(
    earnings, starts, lengths, block_count, trans_logits, init_logits, state_mean, log_sd
):
    num_states = init_logits.shape[0]
    nt = earnings.shape[1]
    slot_rows = earnings.shape[0]
    cap = slot_rows // HB
    nz = lax.axis_size("hh")
    nsrc = nz * 2
    own_t = trans_logits.shape[0]
    half_t = nt // 2
    half = num_states // 2
    zr = num_states // nz
    lanes = 256
    groups = nsrc * HB // 2 // lanes
    wide = groups * lanes
    parts = 4
    cfg = (nz, nt, half_t, own_t, num_states, groups, lanes, parts)
    V = pltpu.VMEM
    D = pltpu.SemaphoreType.DMA
    vm = pl.BlockSpec(memory_space=pltpu.VMEM)
    sm = pl.BlockSpec(memory_space=pltpu.SMEM)
    hbm = pl.BlockSpec(memory_space=pltpu.HBM)
    pinned = lambda v: pltpu.with_memory_space_constraint(v, pltpu.HBM)
    held = lambda v: pltpu.with_memory_space_constraint(v, pltpu.VMEM)
    rows_of = V((half_t, groups, lanes // 128, 128), F32)
    grad, ll = pl.pallas_call(
        functools.partial(fused_kernel, cfg),
        out_shape=(pltpu.VMEM((half_t, zr, half), F32), pltpu.VMEM((1, 128), F32)),
        in_specs=[hbm, hbm, hbm, sm, hbm, hbm, hbm, hbm],
        out_specs=(vm, vm),
        scratch_shapes=[
            V((nt, slot_rows), F32), V((cap, HB), jnp.int32), V((cap, HB), jnp.int32), V((3, 1, num_states), F32),
            V((2, 8, 256), F32),
            V((nsrc, 8, 256), F32),
            rows_of,
            V((4, groups, lanes // 128, 128), F32),
            V((own_t, num_states, num_states), BF),
            V((2, half_t, EXT + num_states, num_states), BF),
            V((4, num_states, 128), F32),
            V((EXT, num_states), BF),
            V((half_t + 1, groups, num_states, lanes), BF),
            V((half_t, groups, num_states, lanes), BF),
            V((half_t, groups, num_states, lanes), F32),
            rows_of, rows_of, rows_of,
            V((half_t, zr, lanes), BF),
            V((half_t, zr, num_states), F32),
            V((half_t, zr, num_states), F32),
            V((half_t, zr, num_states), F32),
            V((4, 8, 128), F32),
            V((2, 8, 128), F32),
            D((6,)), D((nsrc,)), D((nsrc,)), D((2 * own_t + 2,)), D((own_t + 2,)),
            D((parts,)), D((parts,)), D((parts,)), D((parts,)), D((half_t,)), D((half_t,)),
            D((3,)), D((3,)), D((2,)), D((2 * nz,)),
        ],
        compiler_params=pltpu.CompilerParams(
            collective_id=0, has_side_effects=True, vmem_limit_bytes=40 * 1024 * 1024),
        name="chain",
    )(pinned(earnings.T), pinned(starts.reshape(cap, HB)), pinned(lengths.reshape(cap, HB)), block_count,
      pinned(trans_logits), pinned(init_logits[None]), pinned(state_mean[None]), pinned(log_sd[None]))
    return pl.pallas_call(
        write_out,
        out_shape=(jax.ShapeDtypeStruct(grad.shape, F32), jax.ShapeDtypeStruct((1,), F32)),
        in_specs=[vm, vm],
        out_specs=(hbm, sm),
        scratch_shapes=[pltpu.SemaphoreType.DMA],
        name="write_out",
    )(held(grad), held(ll))


def solution(mesh):
    fits = mesh.shape["per"] == 2 and mesh.shape["st"] == 2 and mesh.shape["hh"] == 4
    body = fused_device if fits else per_device
    placed = (
        P(("hh", "per"), None),
        P(("hh", "per")),
        P(("hh", "per")),
        P(("hh", "per")),
        P(("grp", "per", "st"), None, None),
        P("grp"),
        P("grp"),
        P("grp"),
    )
    return jax.shard_map(
        body,
        mesh=mesh,
        in_specs=placed,
        out_specs=(P(("grp", "per"), "hh", "st"), P("grp")),
        check_vma=False,
    )
```

```python
import functools

import jax
import jax.numpy as jnp
from jax import lax
from jax.sharding import PartitionSpec as P
from jax.experimental import pallas as pl
from jax.experimental.pallas import tpu as pltpu

HB = 128


top_precision = lax.Precision.HIGHEST


def emission(column, state_mean, log_sd):
    z_score = (column[:, None] - state_mean[None, :]) / jnp.exp(log_sd)[None, :]
    return jnp.exp(-0.5 * z_score * z_score - log_sd[None, :])


def per_device(
    earnings, starts, lengths, block_count, trans_logits, init_logits, state_mean, log_sd
):
    num_states = init_logits.shape[0]
    num_periods = earnings.shape[1]
    slot_rows = earnings.shape[0]
    group_size = lax.axis_size(("hh", "per"))
    core_count = lax.axis_size("st")
    half_states = num_states // core_count
    lead_state = lax.axis_index("st") * half_states
    whole_logits = lax.all_gather(trans_logits, ("per", "st"), axis=0, tiled=True)
    raised = jnp.exp(whole_logits.astype(jnp.float32))
    trans_probs = raised / jnp.sum(raised, axis=2, keepdims=True)
    raised_first = jnp.exp(init_logits)
    first_probs = raised_first / jnp.sum(raised_first)
    source_rows = slot_rows // group_size
    count_out = jnp.broadcast_to(block_count.reshape(1, 1), (1, group_size))
    got_earn, got_start, got_len, got_count = (
        lax.all_to_all(
            earnings.reshape(source_rows, group_size, num_periods),
            ("hh", "per"),
            split_axis=1,
            concat_axis=1,
            tiled=True,
        ),
        lax.all_to_all(
            starts.reshape(source_rows, group_size),
            ("hh", "per"),
            split_axis=1,
            concat_axis=1,
            tiled=True,
        ),
        lax.all_to_all(
            lengths.reshape(source_rows, group_size),
            ("hh", "per"),
            split_axis=1,
            concat_axis=1,
            tiled=True,
        ),
        lax.all_to_all(count_out, ("hh", "per"), split_axis=1, concat_axis=1, tiled=True),
    )
    per_source = got_count[0] * (HB // group_size)
    source_order = jnp.arange(group_size, dtype=jnp.int32)
    up_to = source_order[None, :] <= source_order[:, None]
    ends_at = jnp.sum(jnp.where(up_to, per_source[None, :], 0), axis=1)
    target_ids = jnp.arange(HB, dtype=jnp.int32)
    before_mask = ends_at[None, :] <= target_ids[:, None]
    source_ids = jnp.sum(before_mask.astype(jnp.int32), axis=1)
    begins_at = jnp.sum(jnp.where(before_mask, per_source[None, :], 0), axis=1)
    pick_ids = (target_ids - begins_at) * group_size + source_ids
    rows_earn = jnp.take(got_earn.reshape(source_rows * group_size, num_periods), pick_ids, axis=0)
    rows_start = jnp.take(got_start.reshape(source_rows * group_size), pick_ids)
    rows_len = jnp.take(got_len.reshape(source_rows * group_size), pick_ids)
    row_live = jnp.ones((HB,), dtype=bool)
    years_local = jnp.sum(jnp.where(row_live, rows_len, 0)).astype(jnp.float32)
    row_total_count = rows_earn.shape[0]
    columns = rows_earn.T
    period_ids = jnp.arange(num_periods, dtype=jnp.int32)

    def observed(step_now):
        return row_live & (step_now >= rows_start) & (step_now < rows_start + rows_len)

    def forward(prev_alpha, inputs):
        matrix, column, step_now = inputs
        fresh_start = (step_now <= rows_start)[:, None]
        moved_mass = jnp.dot(
            prev_alpha, matrix, precision=top_precision, preferred_element_type=jnp.float32
        )
        joint_mass = jnp.where(fresh_start, first_probs[None, :], moved_mass) * emission(
            column, state_mean, log_sd
        )
        seen_now = observed(step_now)
        scale_now = jnp.where(seen_now, jnp.sum(joint_mass, axis=1), 1.0)
        new_alpha = jnp.where(seen_now[:, None], joint_mass / scale_now[:, None], prev_alpha)
        return (new_alpha, (new_alpha, scale_now))

    start_alpha = jnp.broadcast_to(first_probs[None, :], (row_total_count, num_states))
    _, (alphas, scales) = lax.scan(forward, start_alpha, (trans_probs, columns, period_ids))

    def carry_of(back_now, column, scale_now, step_now):
        seen_now = observed(step_now)
        return jnp.where(
            seen_now[:, None],
            emission(column, state_mean, log_sd) * back_now / scale_now[:, None],
            0.0,
        )

    def backward(carry_now, inputs):
        matrix, alpha_prev, column_prev, scale_prev, step_now = inputs
        moving = row_live & (step_now > rows_start) & (step_now < rows_start + rows_len)
        weights = jnp.where(moving[:, None], alpha_prev, 0.0)
        own_carry = lax.dynamic_slice_in_dim(carry_now, lead_state, half_states, 1)
        grad_term = lax.dot_general(
            weights,
            own_carry,
            (((0,), (0,)), ((), ())),
            precision=top_precision,
            preferred_element_type=jnp.float32,
        )
        pulled = lax.dot_general(
            carry_now,
            matrix,
            (((1,), (1,)), ((), ())),
            precision=top_precision,
            preferred_element_type=jnp.float32,
        )
        back_now = jnp.where(moving[:, None], pulled, 1.0)
        return (carry_of(back_now, column_prev, scale_prev, step_now - 1), grad_term)

    ones_back = jnp.ones((row_total_count, num_states), jnp.float32)
    last_carry = carry_of(
        ones_back, columns[num_periods - 1], scales[num_periods - 1], num_periods - 1
    )
    _, grad_terms = lax.scan(
        backward,
        last_carry,
        (trans_probs[1:], alphas[:-1], columns[:-1], scales[:-1], period_ids[1:]),
        reverse=True,
    )
    zero_first = jnp.zeros((1,) + grad_terms.shape[1:], jnp.float32)
    partial_counts = jnp.concatenate([zero_first, grad_terms], axis=0)
    loglik_local = jnp.sum(jnp.log(scales))
    summed = lax.psum_scatter(partial_counts, "hh", scatter_dimension=1, tiled=True)
    summed = lax.psum_scatter(summed, "per", scatter_dimension=0, tiled=True)
    loglik_share = loglik_local / core_count
    years_share = years_local / core_count
    period_block = summed.shape[0]
    row_block_size = summed.shape[1]
    local_probs = lax.dynamic_slice(
        trans_probs,
        (lax.axis_index("per") * period_block, lax.axis_index("hh") * row_block_size, lead_state),
        (period_block, row_block_size, half_states),
    )
    weighted = local_probs * summed
    row_total, loglik_core, years_core = lax.psum(
        (jnp.sum(weighted, axis=2), loglik_share, years_share), "st"
    )
    loglik_all, years_all = lax.psum((loglik_core, years_core), ("hh", "per"))
    factor = float(num_states * num_states * num_periods) / years_all
    trans_grad = factor * (weighted - local_probs * row_total[:, :, None])
    mean_loglik = jnp.reshape(loglik_all / years_all, (1,))
    return (trans_grad, mean_loglik)


F32 = jnp.float32
BF = jnp.bfloat16
MESH = pl.DeviceIdType.MESH
EXT = 16
LOG2E = 1.4426950408889634
NT_DIMS = (((1,), (1,)), ((), ()))


def dot(p, q):
    return jnp.dot(p, q, preferred_element_type=F32)


def dot_nt(p, q):
    return lax.dot_general(p, q, NT_DIMS, preferred_element_type=F32)


def fused_kernel(cfg, earn_h, begin_h, length_h, count, logits, init_h, mean_h, sd_h, out, llout,
                 earn, begin, length, params, pack, got, people, span, lg, mats, cols, exts, alph, back_u, emem,
                 srow, irow, yrow, weighed, cacc, crecv, prb, llbox, ybox,
                 in_sem, hs_sem, hr_sem, lr_sem, ls_sem, xs_sem, xr_sem, fs_sem, fr_sem, cs_sem, cr_sem,
                 lls_sem, llr_sem, y_sem, up_sem):
    nz, nt, half_t, own_t, num_states, groups, lanes, parts = cfg
    x = lax.axis_index("per")
    z = lax.axis_index("hh")
    s = lax.axis_index("st")
    half = num_states // 2
    nsrc = nz * 2
    zr = num_states // nz
    per_group = lanes // 128
    chunk = 64
    first_core = s == 0

    def rcopy(src, dst, ss, rs, dev):
        return pltpu.make_async_remote_copy(
            src_ref=src, dst_ref=dst, send_sem=ss, recv_sem=rs,
            device_id=dev, device_id_type=MESH)

    partner = {"hh": z, "per": x, "st": 1 - s}
    across = {"hh": z, "per": 1 - x, "st": s}
    corner = {"hh": z, "per": 1 - x, "st": 1 - s}
    mine = lax.rem(z, 2)
    other = 1 - mine
    pair = {"hh": z + 1 - 2 * mine, "per": x, "st": s}
    peers = []
    for zt in range(nz):
        for dx in range(2):
            px = x if dx == 0 else 1 - x
            dev = {"hh": zt, "per": px, "st": s}
            beside = (z == zt) & (dx == 1)
            aside = beside | (zt != z)
            sends = aside & ((z > 0) | (zt < 2))
            hears = aside & ((zt > 0) | (z < 2))
            peers.append((px, dev, sends, hears))
    out_degree = jnp.where(z == 0, 5, nsrc + 1)

    loads = [pltpu.make_async_copy(src, dst, in_sem.at[i]) for i, (src, dst) in enumerate([
        (earn_h, earn), (begin_h, begin), (length_h, length),
        (init_h, params.at[0]), (mean_h, params.at[1]), (sd_h, params.at[2])])]
    for c in loads:
        c.start()
    barrier = pltpu.get_barrier_semaphore()
    for _, dev, _, hears in peers:
        @pl.when(hears)
        def _():
            pl.semaphore_signal(barrier, inc=1, device_id=dev, device_id_type=MESH)
    for dev in [partner, corner]:
        pl.semaphore_signal(barrier, inc=1, device_id=dev, device_id_type=MESH)
    local = []
    for i in range(own_t):
        c = pltpu.make_async_copy(logits.at[i], lg.at[i], lr_sem.at[i])
        c.start()
        local.append(c)

    low = lax.broadcasted_iota(jnp.int32, (8, 128), 1) < 64

    def to_low(v):
        return jnp.where(first_core, v, pltpu.roll(v, 64, 1))

    def to_high(v):
        return jnp.where(first_core, pltpu.roll(v, 64, 1), v)

    for c in loads[:3]:
        c.wait()
    cnt = count[0].astype(F32)
    about = jnp.concatenate(
        [begin[...].astype(F32), length[...].astype(F32), jnp.full((2, 128), 1.0, F32) * cnt], axis=0)
    about = to_high(about)
    for h in range(2):
        e = [earn[h * half_t:(h + 1) * half_t, b * 128:(b + 1) * 128] for b in range(3)]
        pack[h, :, 0:128] = jnp.where(low, to_low(e[0]), to_high(e[1]))
        pack[h, :, 128:256] = jnp.where(low, to_low(e[2]), about)

    zrow = pl.ds(pl.multiple_of(z * zr, zr), zr)

    def make_probs(i):
        l = own_t * s + i
        ext = exts[...]
        eye = jnp.where(lax.broadcasted_iota(jnp.int32, (num_states, num_states), 0)
                        == lax.broadcasted_iota(jnp.int32, (num_states, num_states), 1), 1.0, 0.0).astype(BF)
        r = jnp.exp(lg[i].astype(F32))
        p = (r * (1.0 / jnp.sum(r, axis=1, keepdims=True))).astype(BF)
        mats[0, l, 0:EXT] = ext
        mats[1, l, 0:EXT] = ext
        mats[0, l, EXT:] = p
        mats[1, l, EXT:] = dot_nt(eye, p).astype(BF)
        rz = jnp.exp(lg[i, zrow, :].astype(F32))
        prb[l] = rz / jnp.sum(rz, axis=1, keepdims=True)

    def own_work():
        for c in loads[3:]:
            c.wait()
        mean = params[1]
        log_sd = params[2]
        raised_first = jnp.exp(params[0])
        first = raised_first / jnp.sum(raised_first, axis=1, keepdims=True)
        slope = jnp.exp(-log_sd) * ((0.5 * LOG2E) ** 0.5)
        for i, v in enumerate([slope, slope * mean, log_sd * (-LOG2E), first]):
            cols[i] = jnp.broadcast_to(v, (128, num_states)).T
        ext_row = lax.broadcasted_iota(jnp.int32, (EXT, num_states), 0)
        exts[...] = jnp.where(ext_row == 0, 1.0, jnp.where(
            ext_row == 1, jnp.broadcast_to(first, (EXT, num_states)), 0.0)).astype(BF)
        for c in local:
            c.wait()

        @pl.loop(0, own_t)
        def _(i):
            make_probs(i)

    own_span = pl.ds(own_t * s, own_t)
    near = []
    for i in range(own_t):
        at = (1 - x, own_t * s + i)
        near.append(rcopy(mats.at[at], mats.at[at], ls_sem.at[i], lr_sem.at[own_t + i], partner))
    rest = [rcopy(mats.at[x, own_span], mats.at[x, own_span], ls_sem.at[own_t], lr_sem.at[2 * own_t], partner),
            rcopy(prb.at[own_span], prb.at[own_span], ls_sem.at[own_t + 1], lr_sem.at[2 * own_t + 1], partner)]

    @pl.when(z < nz - 2)
    def _():
        own_work()

    pl.semaphore_wait(barrier, out_degree)

    @pl.when(z < nz - 2)
    def _():
        for c in near:
            c.start()

    me_src = z * 2 + x
    for n, (px, dev, sends, _) in enumerate(peers):
        @pl.when(sends)
        def _():
            rcopy(pack.at[px], got.at[me_src], hs_sem.at[n], hr_sem.at[me_src], dev).start()
    pltpu.make_async_copy(pack.at[x], got.at[me_src], hr_sem.at[me_src]).start()

    @pl.when(z >= nz - 2)
    def _():
        own_work()
        for c in near:
            c.start()

    for c in rest:
        c.start()

    climbs = z == 1

    def climb(d, zt):
        return rcopy(got.at[d], got.at[d], up_sem.at[d * nz + zt], hr_sem.at[d], {"hh": zt, "per": x, "st": s})

    tiles = groups * per_group
    high_bit = jnp.where(lax.broadcasted_iota(jnp.int32, (1, 128), 1) < 64, 0.0, 1.0)
    base = jnp.zeros((1, 128), F32)
    xs = [jnp.zeros((8, 128), F32) for _ in range(tiles)]
    starts = [jnp.zeros((1, 128), F32) for _ in range(tiles)]
    spans = [jnp.zeros((1, 128), F32) for _ in range(tiles)]
    for d in range(nsrc):
        rcopy(pack.at[0], got.at[d], hs_sem.at[0], hr_sem.at[d], across).wait_recv()
        if d < 2:
            @pl.when(climbs)
            def _():
                for zt in range(nz - 1, 1, -1):
                    climb(d, zt).start()
        t0, t1 = got[d, :, 0:128], got[d, :, 128:256]
        r0, r1 = pltpu.roll(t0, 64, 1), pltpu.roll(t1, 64, 1)
        held = [jnp.where(low, t0, r0), jnp.where(low, r0, t0), jnp.where(low, t1, r1)]
        about = jnp.where(low, r1, t1)
        live = about[6:7]
        for b in range(3):
            spot = jnp.where(live > float(b), base + float(b), -2.0) - high_bit
            for m in range(tiles):
                hit = spot == float(2 * m)
                xs[m] = jnp.where(hit, held[b], xs[m])
                starts[m] = jnp.where(hit, about[b:b + 1], starts[m])
                spans[m] = jnp.where(hit, about[3 + b:4 + b], spans[m])
        base = base + live
    years_own = jnp.zeros((1, 1), F32)
    for m in range(tiles):
        g, c = m // per_group, m % per_group
        for t in range(half_t):
            people[t, g, c:c + 1, :] = xs[m][t:t + 1]
        span[0, g, c:c + 1, :] = starts[m]
        span[1, g, c:c + 1, :] = starts[m] + spans[m]
        years_own = years_own + jnp.sum(spans[m], axis=1, keepdims=True)
    ybox[0] = jnp.broadcast_to(years_own, (8, 128))
    yc = rcopy(ybox.at[0], ybox.at[1], y_sem.at[0], y_sem.at[1], partner)
    yc.start()

    for c in near:
        c.wait_recv()

    cells = [(m, pl.ds(m * 128, 128), m * 128, r, pl.ds(r, chunk))
             for m in range(per_group) for r in range(0, num_states, chunk)]

    def row(ref, l, g):
        return [ref[l, g, m:m + 1, :] for m in range(per_group)]

    def put_row(ref, l, g, vals):
        for m in range(per_group):
            ref[l, g, m:m + 1, :] = vals[m]

    def ext_row_of(raw, i):
        return [raw[i:i + 1, m * 128:(m + 1) * 128] for m in range(per_group)]

    def piece(raw, c0, r):
        return raw[EXT + r:EXT + r + chunk, c0:c0 + 128]

    def moving(t, g):
        return [(t > a) & (t < b) for a, b in zip(row(span, 0, g), row(span, 1, g))]

    def fill_emission(l, g):
        xrow = row(people, l, g)
        for m, cc, c0, r, rr in cells:
            off = cols[0, rr, :] * xrow[m] - cols[1, rr, :]
            emem[l, g, rr, cc] = jnp.exp2(cols[2, rr, :] - off * off)

    def forward_step(l, t, g, raw, inv):
        fresh = [t <= a for a in row(span, 0, g)]
        for m, cc, c0, r, rr in cells:
            moved = jnp.where(fresh[m], cols[3, rr, :], piece(raw, c0, r) * inv[m])
            alph[l + 1, g, rr, cc] = (moved * emem[l, g, rr, cc]).astype(BF)

    def part_rows(k):
        return pl.ds(k * (num_states // parts), num_states // parts)

    def cross(k):
        return rcopy(alph.at[half_t, mine, part_rows(k)], alph.at[0, mine, part_rows(k)],
                     xs_sem.at[k], xr_sem.at[k], across)

    def onward(k, g):
        return rcopy(alph.at[0, g, part_rows(k)], alph.at[0, g, part_rows(k)], fs_sem.at[k], fr_sem.at[k], pair)

    def beside(k):
        return rcopy(alph.at[half_t, other, part_rows(k)], alph.at[0, other, part_rows(k)], fs_sem.at[k], fr_sem.at[k], across)

    def send_cross():
        for k in range(parts):
            cross(k).start()

    def pass_on():
        for c in rest:
            c.wait_recv()
        for k in range(parts):
            cross(k).wait_recv()
            if k < parts // 2:
                onward(k, mine).start()

    def take_other():
        for k in range(parts):
            onward(k, other).wait_recv()

    def junction(g):
        q = []
        for m in range(per_group):
            acc = jnp.zeros((chunk, 128), F32)
            for r in range(0, num_states, chunk):
                rr, cc = pl.ds(r, chunk), pl.ds(m * 128, 128)
                acc = acc + alph[half_t, g, rr, cc].astype(F32) * alph[0, g, rr, cc].astype(F32)
            q.append(jnp.sum(acc, axis=0, keepdims=True))
        return q

    def counts_copy(l):
        return rcopy(cacc.at[l], crecv.at[l], cs_sem.at[l], cr_sem.at[l], partner)

    def add_counts(l, v, last):
        if last:
            cacc[l] = cacc[l] + v
            counts_copy(l).start()
        else:
            cacc[l] = v

    def send_ll(logs):
        llbox[x * 2 + s] = jnp.broadcast_to(
            jnp.sum(jnp.sum(logs, axis=0, keepdims=True), axis=1, keepdims=True), (8, 128))
        at = x * 2 + s
        for j, dev in enumerate([partner, across, corner]):
            rcopy(llbox.at[at], llbox.at[at], lls_sem.at[j], llr_sem.at[j], dev).start()

    def finish(order):
        yc.wait()
        years = ybox[0, 0:1, 0:1] + ybox[1, 0:1, 0:1]
        factor = float(num_states * num_states * nt) / years
        at = x * 2 + s
        for j, dev in enumerate([partner, across, corner]):
            rcopy(llbox.at[at], llbox.at[at], lls_sem.at[j], llr_sem.at[j], dev).wait()
        ll = (llbox[0, 0:1, :] + llbox[1, 0:1, :]) + (llbox[2, 0:1, :] + llbox[3, 0:1, :])
        llout[...] = ll / years
        order = list(order)
        for n, l in enumerate(order):
            if n == 0:
                for k in order[:-2]:
                    counts_copy(k).wait()
            if n >= len(order) - 2:
                counts_copy(l).wait()
            w = prb[l] * (cacc[l] + crecv[l])
            total = jnp.sum(w, axis=1, keepdims=True)
            w_own = jnp.where(first_core, w[:, :half], w[:, half:])
            p_own = jnp.where(first_core, prb[l, :, :half], prb[l, :, half:])
            out[l] = factor * (w_own - p_own * total)

    @pl.when(x == 0)
    def _early():
        def first_pass(g):
            fill_emission(0, g)
            for m, cc, c0, r, rr in cells:
                alph[1, g, rr, cc] = (cols[3, rr, :] * emem[0, g, rr, cc]).astype(BF)

            @pl.loop(1, half_t)
            def _(l):
                raw = dot(mats[1, l], alph[l, g])
                fill_emission(l, g)
                sums = ext_row_of(raw, 0)
                put_row(srow, l - 1, g, sums)
                forward_step(l, l.astype(F32), g, raw, [1.0 / v for v in sums])

        first_pass(mine)
        send_cross()
        first_pass(other)
        for k in range(parts // 2, parts):
            beside(k).start()
        logs = jnp.zeros((per_group, 128), F32)
        for g in range(groups):
            put_row(srow, half_t - 1, g, ext_row_of(dot(exts[...], alph[half_t, g]), 0))
            for l in range(half_t):
                seen = (float(l) >= span[0, g]) & (float(l) < span[1, g])
                if l == half_t - 1:
                    seen = seen & (span[1, g] == float(half_t))
                logs = logs + jnp.where(seen, jnp.log(srow[l, g]), 0.0)
        irow[...] = 1.0 / srow[...]
        send_ll(logs)

        def put_u(l, t, g, get):
            on = moving(t + 1.0, g)
            gain = [jnp.where(a, b, 0.0) for a, b in zip(moving(t, g), row(irow, l - 1, g))]
            inv_s = row(irow, l, g)
            for m, cc, c0, r, rr in cells:
                y = jnp.where(on[m], get(m, cc, c0, r, rr), inv_s[m])
                back_u[l, g, rr, cc] = (emem[l, g, rr, cc] * y * gain[m]).astype(BF)

        def second_pass(g, last):
            inv_q = [1.0 / v for v in junction(g)]
            put_u(half_t - 1, float(half_t - 1), g,
                  lambda m, cc, c0, r, rr: alph[0, g, rr, cc].astype(F32) * inv_q[m])

            def counts(l):
                add_counts(l, dot_nt(alph[l, g, zrow, :], back_u[l, g]), last)

            def step(l, t, ready):
                raw = dot(mats[0, l], back_u[l, g])
                if ready:
                    counts(l + 1)
                put_u(l - 1, t - 1.0, g, lambda m, cc, c0, r, rr: piece(raw, c0, r))

            step(half_t - 1, half_t - 1.0, False)

            @pl.loop(0, half_t - 3)
            def _(k):
                l = half_t - 2 - k
                step(l, l.astype(F32), True)

            counts(2)
            counts(1)

        pass_on()
        second_pass(mine, False)
        take_other()
        second_pass(other, True)
        out[0] = jnp.zeros(out.shape[1:], F32)
        finish(range(half_t - 1, 0, -1))

    @pl.when(x == 1)
    def _late():
        top = half_t - 1

        def first_pass(g):
            fill_emission(top, g)
            for m, cc, c0, r, rr in cells:
                back_u[top, g, rr, cc] = emem[top, g, rr, cc].astype(BF)

            def back_step(l, t, put):
                raw = dot(mats[0, l], back_u[l, g])
                sums = ext_row_of(raw, 0)
                put_row(srow, l, g, sums)
                put_row(yrow, l, g, ext_row_of(raw, 1))
                inv = [1.0 / v for v in sums]
                on = moving(t, g)
                for m, cc, c0, r, rr in cells:
                    put(rr, cc, jnp.where(on[m], piece(raw, c0, r) * inv[m], 1.0))

            @pl.loop(0, top)
            def _(k):
                l = top - k
                fill_emission(l - 1, g)

                def put(rr, cc, v):
                    back_u[l - 1, g, rr, cc] = (v * emem[l - 1, g, rr, cc]).astype(BF)

                back_step(l, (l + half_t).astype(F32), put)

            def put(rr, cc, v):
                alph[half_t, g, rr, cc] = v.astype(BF)

            back_step(0, float(half_t), put)

        first_pass(mine)
        send_cross()
        first_pass(other)
        for k in range(parts // 2, parts):
            beside(k).start()
        logs = jnp.zeros((per_group, 128), F32)
        for g in range(groups):
            for l in range(half_t):
                t = float(l + half_t)
                on = (t > span[0, g]) & (t < span[1, g])
                logs = logs + jnp.where(on, jnp.log(srow[l, g]), 0.0)
                logs = logs + jnp.where(span[0, g] == t, jnp.log(yrow[l, g]), 0.0)

        def join(g):
            q = junction(g)
            put_row(span, 2, g, q)
            put_row(span, 3, g, q)
            t = float(half_t)
            return jnp.where((t > span[0, g]) & (t < span[1, g]), jnp.log(span[2, g]), 0.0)

        def second_pass(g, last):
            def weigh(l, t, sums):
                inv = [1.0 / v for v in sums]
                on = moving(t, g)
                for m in range(per_group):
                    cc = pl.ds(m * 128, 128)
                    d = jnp.where(span[0, g, m:m + 1, :] == t - 1.0, span[3, g, m:m + 1, :], span[2, g, m:m + 1, :])
                    d = d * inv[m] * srow[l, g, m:m + 1, :]
                    span[2, g, m:m + 1, :] = d
                    span[3, g, m:m + 1, :] = yrow[l, g, m:m + 1, :]
                    w = jnp.where(on[m], 1.0 / d, 0.0)
                    weighed[l, :, cc] = (alph[l, g, zrow, cc].astype(F32) * inv[m] * w).astype(BF)
                return inv

            def counts(l):
                add_counts(l, dot_nt(weighed[l], back_u[l, g]), last)

            def step(l, t, ready):
                raw = dot(mats[1, l], alph[l, g])
                if ready:
                    counts(l - 1)
                inv = weigh(l, t, ext_row_of(raw, 0))
                forward_step(l, t, g, raw, inv)

            step(0, float(half_t), False)

            @pl.loop(1, top)
            def _(l):
                step(l, (l + half_t).astype(F32), True)

            sums = ext_row_of(dot(exts[...], alph[top, g]), 0)
            counts(top - 1)
            weigh(top, float(top + half_t), sums)
            counts(top)

        pass_on()
        logs = logs + join(mine)
        second_pass(mine, False)
        take_other()
        send_ll(logs + join(other))
        second_pass(other, True)
        finish(range(half_t))

    for n, (px, dev, sends, _) in enumerate(peers):
        @pl.when(sends)
        def _():
            rcopy(pack.at[px], got.at[me_src], hs_sem.at[n], hr_sem.at[me_src], dev).wait_send()
    for d in range(2):
        @pl.when(climbs)
        def _():
            for zt in range(2, nz):
                climb(d, zt).wait_send()
    for c in near + rest:
        c.wait_send()
    for k in range(parts):
        cross(k).wait_send()
        (onward(k, mine) if k < parts // 2 else beside(k)).wait_send()


def write_out(grad, ll, out, llout):
    out[...] = grad[...]
    llout[...] = ll[0, 0:1]


def fused_device(
    earnings, starts, lengths, block_count, trans_logits, init_logits, state_mean, log_sd
):
    num_states = init_logits.shape[0]
    nt = earnings.shape[1]
    slot_rows = earnings.shape[0]
    cap = slot_rows // HB
    nz = lax.axis_size("hh")
    nsrc = nz * 2
    own_t = trans_logits.shape[0]
    half_t = nt // 2
    half = num_states // 2
    zr = num_states // nz
    lanes = 256
    groups = nsrc * HB // 2 // lanes
    wide = groups * lanes
    parts = 4
    cfg = (nz, nt, half_t, own_t, num_states, groups, lanes, parts)
    V = pltpu.VMEM
    D = pltpu.SemaphoreType.DMA
    vm = pl.BlockSpec(memory_space=pltpu.VMEM)
    sm = pl.BlockSpec(memory_space=pltpu.SMEM)
    hbm = pl.BlockSpec(memory_space=pltpu.HBM)
    pinned = lambda v: pltpu.with_memory_space_constraint(v, pltpu.HBM)
    held = lambda v: pltpu.with_memory_space_constraint(v, pltpu.VMEM)
    rows_of = V((half_t, groups, lanes // 128, 128), F32)
    grad, ll = pl.pallas_call(
        functools.partial(fused_kernel, cfg),
        out_shape=(pltpu.VMEM((half_t, zr, half), F32), pltpu.VMEM((1, 128), F32)),
        in_specs=[hbm, hbm, hbm, sm, hbm, hbm, hbm, hbm],
        out_specs=(vm, vm),
        scratch_shapes=[
            V((nt, slot_rows), F32), V((cap, HB), jnp.int32), V((cap, HB), jnp.int32), V((3, 1, num_states), F32),
            V((2, 8, 256), F32),
            V((nsrc, 8, 256), F32),
            rows_of,
            V((4, groups, lanes // 128, 128), F32),
            V((own_t, num_states, num_states), BF),
            V((2, half_t, EXT + num_states, num_states), BF),
            V((4, num_states, 128), F32),
            V((EXT, num_states), BF),
            V((half_t + 1, groups, num_states, lanes), BF),
            V((half_t, groups, num_states, lanes), BF),
            V((half_t, groups, num_states, lanes), F32),
            rows_of, rows_of, rows_of,
            V((half_t, zr, lanes), BF),
            V((half_t, zr, num_states), F32),
            V((half_t, zr, num_states), F32),
            V((half_t, zr, num_states), F32),
            V((4, 8, 128), F32),
            V((2, 8, 128), F32),
            D((6,)), D((nsrc,)), D((nsrc,)), D((2 * own_t + 2,)), D((own_t + 2,)),
            D((parts,)), D((parts,)), D((parts,)), D((parts,)), D((half_t,)), D((half_t,)),
            D((3,)), D((3,)), D((2,)), D((2 * nz,)),
        ],
        compiler_params=pltpu.CompilerParams(
            collective_id=0, has_side_effects=True, vmem_limit_bytes=40 * 1024 * 1024),
        name="chain",
    )(pinned(earnings.T), pinned(starts.reshape(cap, HB)), pinned(lengths.reshape(cap, HB)), block_count,
      pinned(trans_logits), pinned(init_logits[None]), pinned(state_mean[None]), pinned(log_sd[None]))
    return pl.pallas_call(
        write_out,
        out_shape=(jax.ShapeDtypeStruct(grad.shape, F32), jax.ShapeDtypeStruct((1,), F32)),
        in_specs=[vm, vm],
        out_specs=(vm, vm),
        name="write_out",
    )(held(grad), held(ll))


def solution(mesh):
    fits = mesh.shape["per"] == 2 and mesh.shape["st"] == 2 and mesh.shape["hh"] == 4
    body = fused_device if fits else per_device
    placed = (
        P(("hh", "per"), None),
        P(("hh", "per")),
        P(("hh", "per")),
        P(("hh", "per")),
        P(("grp", "per", "st"), None, None),
        P("grp"),
        P("grp"),
        P("grp"),
    )
    return jax.shard_map(
        body,
        mesh=mesh,
        in_specs=placed,
        out_specs=(P(("grp", "per"), "hh", "st"), P("grp")),
        check_vma=False,
    )
```

```python
import functools

import jax
import jax.numpy as jnp
from jax import lax
from jax.sharding import PartitionSpec as P
from jax.experimental import pallas as pl
from jax.experimental.pallas import tpu as pltpu

HB = 128


top_precision = lax.Precision.HIGHEST


def emission(column, state_mean, log_sd):
    z_score = (column[:, None] - state_mean[None, :]) / jnp.exp(log_sd)[None, :]
    return jnp.exp(-0.5 * z_score * z_score - log_sd[None, :])


def per_device(
    earnings, starts, lengths, block_count, trans_logits, init_logits, state_mean, log_sd
):
    num_states = init_logits.shape[0]
    num_periods = earnings.shape[1]
    slot_rows = earnings.shape[0]
    group_size = lax.axis_size(("hh", "per"))
    core_count = lax.axis_size("st")
    half_states = num_states // core_count
    lead_state = lax.axis_index("st") * half_states
    whole_logits = lax.all_gather(trans_logits, ("per", "st"), axis=0, tiled=True)
    raised = jnp.exp(whole_logits.astype(jnp.float32))
    trans_probs = raised / jnp.sum(raised, axis=2, keepdims=True)
    raised_first = jnp.exp(init_logits)
    first_probs = raised_first / jnp.sum(raised_first)
    source_rows = slot_rows // group_size
    count_out = jnp.broadcast_to(block_count.reshape(1, 1), (1, group_size))
    got_earn, got_start, got_len, got_count = (
        lax.all_to_all(
            earnings.reshape(source_rows, group_size, num_periods),
            ("hh", "per"),
            split_axis=1,
            concat_axis=1,
            tiled=True,
        ),
        lax.all_to_all(
            starts.reshape(source_rows, group_size),
            ("hh", "per"),
            split_axis=1,
            concat_axis=1,
            tiled=True,
        ),
        lax.all_to_all(
            lengths.reshape(source_rows, group_size),
            ("hh", "per"),
            split_axis=1,
            concat_axis=1,
            tiled=True,
        ),
        lax.all_to_all(count_out, ("hh", "per"), split_axis=1, concat_axis=1, tiled=True),
    )
    per_source = got_count[0] * (HB // group_size)
    source_order = jnp.arange(group_size, dtype=jnp.int32)
    up_to = source_order[None, :] <= source_order[:, None]
    ends_at = jnp.sum(jnp.where(up_to, per_source[None, :], 0), axis=1)
    target_ids = jnp.arange(HB, dtype=jnp.int32)
    before_mask = ends_at[None, :] <= target_ids[:, None]
    source_ids = jnp.sum(before_mask.astype(jnp.int32), axis=1)
    begins_at = jnp.sum(jnp.where(before_mask, per_source[None, :], 0), axis=1)
    pick_ids = (target_ids - begins_at) * group_size + source_ids
    rows_earn = jnp.take(got_earn.reshape(source_rows * group_size, num_periods), pick_ids, axis=0)
    rows_start = jnp.take(got_start.reshape(source_rows * group_size), pick_ids)
    rows_len = jnp.take(got_len.reshape(source_rows * group_size), pick_ids)
    row_live = jnp.ones((HB,), dtype=bool)
    years_local = jnp.sum(jnp.where(row_live, rows_len, 0)).astype(jnp.float32)
    row_total_count = rows_earn.shape[0]
    columns = rows_earn.T
    period_ids = jnp.arange(num_periods, dtype=jnp.int32)

    def observed(step_now):
        return row_live & (step_now >= rows_start) & (step_now < rows_start + rows_len)

    def forward(prev_alpha, inputs):
        matrix, column, step_now = inputs
        fresh_start = (step_now <= rows_start)[:, None]
        moved_mass = jnp.dot(
            prev_alpha, matrix, precision=top_precision, preferred_element_type=jnp.float32
        )
        joint_mass = jnp.where(fresh_start, first_probs[None, :], moved_mass) * emission(
            column, state_mean, log_sd
        )
        seen_now = observed(step_now)
        scale_now = jnp.where(seen_now, jnp.sum(joint_mass, axis=1), 1.0)
        new_alpha = jnp.where(seen_now[:, None], joint_mass / scale_now[:, None], prev_alpha)
        return (new_alpha, (new_alpha, scale_now))

    start_alpha = jnp.broadcast_to(first_probs[None, :], (row_total_count, num_states))
    _, (alphas, scales) = lax.scan(forward, start_alpha, (trans_probs, columns, period_ids))

    def carry_of(back_now, column, scale_now, step_now):
        seen_now = observed(step_now)
        return jnp.where(
            seen_now[:, None],
            emission(column, state_mean, log_sd) * back_now / scale_now[:, None],
            0.0,
        )

    def backward(carry_now, inputs):
        matrix, alpha_prev, column_prev, scale_prev, step_now = inputs
        moving = row_live & (step_now > rows_start) & (step_now < rows_start + rows_len)
        weights = jnp.where(moving[:, None], alpha_prev, 0.0)
        own_carry = lax.dynamic_slice_in_dim(carry_now, lead_state, half_states, 1)
        grad_term = lax.dot_general(
            weights,
            own_carry,
            (((0,), (0,)), ((), ())),
            precision=top_precision,
            preferred_element_type=jnp.float32,
        )
        pulled = lax.dot_general(
            carry_now,
            matrix,
            (((1,), (1,)), ((), ())),
            precision=top_precision,
            preferred_element_type=jnp.float32,
        )
        back_now = jnp.where(moving[:, None], pulled, 1.0)
        return (carry_of(back_now, column_prev, scale_prev, step_now - 1), grad_term)

    ones_back = jnp.ones((row_total_count, num_states), jnp.float32)
    last_carry = carry_of(
        ones_back, columns[num_periods - 1], scales[num_periods - 1], num_periods - 1
    )
    _, grad_terms = lax.scan(
        backward,
        last_carry,
        (trans_probs[1:], alphas[:-1], columns[:-1], scales[:-1], period_ids[1:]),
        reverse=True,
    )
    zero_first = jnp.zeros((1,) + grad_terms.shape[1:], jnp.float32)
    partial_counts = jnp.concatenate([zero_first, grad_terms], axis=0)
    loglik_local = jnp.sum(jnp.log(scales))
    summed = lax.psum_scatter(partial_counts, "hh", scatter_dimension=1, tiled=True)
    summed = lax.psum_scatter(summed, "per", scatter_dimension=0, tiled=True)
    loglik_share = loglik_local / core_count
    years_share = years_local / core_count
    period_block = summed.shape[0]
    row_block_size = summed.shape[1]
    local_probs = lax.dynamic_slice(
        trans_probs,
        (lax.axis_index("per") * period_block, lax.axis_index("hh") * row_block_size, lead_state),
        (period_block, row_block_size, half_states),
    )
    weighted = local_probs * summed
    row_total, loglik_core, years_core = lax.psum(
        (jnp.sum(weighted, axis=2), loglik_share, years_share), "st"
    )
    loglik_all, years_all = lax.psum((loglik_core, years_core), ("hh", "per"))
    factor = float(num_states * num_states * num_periods) / years_all
    trans_grad = factor * (weighted - local_probs * row_total[:, :, None])
    mean_loglik = jnp.reshape(loglik_all / years_all, (1,))
    return (trans_grad, mean_loglik)


F32 = jnp.float32
BF = jnp.bfloat16
MESH = pl.DeviceIdType.MESH
EXT = 16
LOG2E = 1.4426950408889634
NT_DIMS = (((1,), (1,)), ((), ()))


def dot(p, q):
    return jnp.dot(p, q, preferred_element_type=F32)


def dot_nt(p, q):
    return lax.dot_general(p, q, NT_DIMS, preferred_element_type=F32)


def fused_kernel(cfg, earn_h, begin_h, length_h, count, logits, init_h, mean_h, sd_h, out, llout,
                 earn, begin, length, params, pack, got, people, span, lg, mats, cols, exts, alph, back_u, emem,
                 srow, irow, yrow, weighed, cacc, crecv, prb, llbox, ybox,
                 in_sem, hs_sem, hr_sem, lr_sem, ls_sem, xs_sem, xr_sem, fs_sem, fr_sem, cs_sem, cr_sem,
                 lls_sem, llr_sem, y_sem, up_sem):
    nz, nt, half_t, own_t, num_states, groups, lanes, parts = cfg
    x = lax.axis_index("per")
    z = lax.axis_index("hh")
    s = lax.axis_index("st")
    half = num_states // 2
    nsrc = nz * 2
    zr = num_states // nz
    per_group = lanes // 128
    chunk = 64
    first_core = s == 0

    def rcopy(src, dst, ss, rs, dev):
        return pltpu.make_async_remote_copy(
            src_ref=src, dst_ref=dst, send_sem=ss, recv_sem=rs,
            device_id=dev, device_id_type=MESH)

    partner = {"hh": z, "per": x, "st": 1 - s}
    across = {"hh": z, "per": 1 - x, "st": s}
    corner = {"hh": z, "per": 1 - x, "st": 1 - s}
    mine = lax.rem(z, 2)
    other = 1 - mine
    pair = {"hh": z + 1 - 2 * mine, "per": x, "st": s}
    peers = []
    for zt in range(nz):
        for dx in range(2):
            px = x if dx == 0 else 1 - x
            dev = {"hh": zt, "per": px, "st": s}
            beside = (z == zt) & (dx == 1)
            aside = beside | (zt != z)
            sends = aside & ((z > 0) | (zt < 2))
            hears = aside & ((zt > 0) | (z < 2))
            peers.append((px, dev, sends, hears))
    out_degree = jnp.where(z == 0, 5, nsrc + 1)

    loads = [pltpu.make_async_copy(src, dst, in_sem.at[i]) for i, (src, dst) in enumerate([
        (earn_h, earn), (begin_h, begin), (length_h, length),
        (init_h, params.at[0]), (mean_h, params.at[1]), (sd_h, params.at[2])])]
    for c in loads:
        c.start()
    barrier = pltpu.get_barrier_semaphore()
    for _, dev, _, hears in peers:
        @pl.when(hears)
        def _():
            pl.semaphore_signal(barrier, inc=1, device_id=dev, device_id_type=MESH)
    for dev in [partner, corner]:
        pl.semaphore_signal(barrier, inc=1, device_id=dev, device_id_type=MESH)
    local = []
    for i in range(own_t):
        c = pltpu.make_async_copy(logits.at[i], lg.at[i], lr_sem.at[i])
        c.start()
        local.append(c)

    low = lax.broadcasted_iota(jnp.int32, (8, 128), 1) < 64

    def to_low(v):
        return jnp.where(first_core, v, pltpu.roll(v, 64, 1))

    def to_high(v):
        return jnp.where(first_core, pltpu.roll(v, 64, 1), v)

    for c in loads[:3]:
        c.wait()
    cnt = count[0].astype(F32)
    about = jnp.concatenate(
        [begin[...].astype(F32), length[...].astype(F32), jnp.full((2, 128), 1.0, F32) * cnt], axis=0)
    about = to_high(about)
    for h in range(2):
        e = [earn[h * half_t:(h + 1) * half_t, b * 128:(b + 1) * 128] for b in range(3)]
        pack[h, :, 0:128] = jnp.where(low, to_low(e[0]), to_high(e[1]))
        pack[h, :, 128:256] = jnp.where(low, to_low(e[2]), about)

    zrow = pl.ds(pl.multiple_of(z * zr, zr), zr)

    def make_probs(i):
        l = own_t * s + i
        ext = exts[...]
        eye = jnp.where(lax.broadcasted_iota(jnp.int32, (num_states, num_states), 0)
                        == lax.broadcasted_iota(jnp.int32, (num_states, num_states), 1), 1.0, 0.0).astype(BF)
        r = jnp.exp(lg[i].astype(F32))
        p = (r * (1.0 / jnp.sum(r, axis=1, keepdims=True))).astype(BF)
        mats[0, l, 0:EXT] = ext
        mats[1, l, 0:EXT] = ext
        mats[0, l, EXT:] = p
        mats[1, l, EXT:] = dot_nt(eye, p).astype(BF)
        rz = jnp.exp(lg[i, zrow, :].astype(F32))
        prb[l] = rz / jnp.sum(rz, axis=1, keepdims=True)

    def own_work():
        for c in loads[3:]:
            c.wait()
        mean = params[1]
        log_sd = params[2]
        raised_first = jnp.exp(params[0])
        first = raised_first / jnp.sum(raised_first, axis=1, keepdims=True)
        slope = jnp.exp(-log_sd) * ((0.5 * LOG2E) ** 0.5)
        for i, v in enumerate([slope, slope * mean, log_sd * (-LOG2E), first]):
            cols[i] = jnp.broadcast_to(v, (128, num_states)).T
        ext_row = lax.broadcasted_iota(jnp.int32, (EXT, num_states), 0)
        exts[...] = jnp.where(ext_row == 0, 1.0, jnp.where(
            ext_row == 1, jnp.broadcast_to(first, (EXT, num_states)), 0.0)).astype(BF)
        for c in local:
            c.wait()

        @pl.loop(0, own_t)
        def _(i):
            make_probs(i)

    own_span = pl.ds(own_t * s, own_t)
    near = []
    for i in range(own_t):
        at = (1 - x, own_t * s + i)
        near.append(rcopy(mats.at[at], mats.at[at], ls_sem.at[i], lr_sem.at[own_t + i], partner))
    rest = [rcopy(mats.at[x, own_span], mats.at[x, own_span], ls_sem.at[own_t], lr_sem.at[2 * own_t], partner),
            rcopy(prb.at[own_span], prb.at[own_span], ls_sem.at[own_t + 1], lr_sem.at[2 * own_t + 1], partner)]

    @pl.when(z < nz - 2)
    def _():
        own_work()

    pl.semaphore_wait(barrier, out_degree)

    @pl.when(z < nz - 2)
    def _():
        for c in near:
            c.start()

    me_src = z * 2 + x
    for n, (px, dev, sends, _) in enumerate(peers):
        @pl.when(sends)
        def _():
            rcopy(pack.at[px], got.at[me_src], hs_sem.at[n], hr_sem.at[me_src], dev).start()
    pltpu.make_async_copy(pack.at[x], got.at[me_src], hr_sem.at[me_src]).start()

    @pl.when(z >= nz - 2)
    def _():
        own_work()
        for c in near:
            c.start()

    for c in rest:
        c.start()

    climbs = z == 1

    def climb(d, zt):
        return rcopy(got.at[d], got.at[d], up_sem.at[d * nz + zt], hr_sem.at[d], {"hh": zt, "per": x, "st": s})

    tiles = groups * per_group
    high_bit = jnp.where(low, 0.0, 1.0)
    base = jnp.zeros((8, 128), F32)
    xs = [jnp.zeros((8, 128), F32) for _ in range(tiles)]
    whens = [jnp.zeros((8, 128), F32) for _ in range(tiles)]
    for d in range(nsrc):
        rcopy(pack.at[0], got.at[d], hs_sem.at[0], hr_sem.at[d], across).wait_recv()
        if d < 2:
            @pl.when(climbs)
            def _():
                for zt in range(nz - 1, 1, -1):
                    climb(d, zt).start()
        t0, t1 = got[d, :, 0:128], got[d, :, 128:256]
        r0, r1 = pltpu.roll(t0, 64, 1), pltpu.roll(t1, 64, 1)
        held = [jnp.where(low, t0, r0), jnp.where(low, r0, t0), jnp.where(low, t1, r1)]
        about = jnp.where(low, r1, t1)
        live = jnp.broadcast_to(about[6:7], (8, 128))
        for b in range(3):
            spot = jnp.where(live > float(b), base + float(b), -2.0) - high_bit
            when = about if b == 0 else pltpu.roll(about, 8 - b, 0)
            for m in range(tiles):
                hit = spot == float(2 * m)
                xs[m] = jnp.where(hit, held[b], xs[m])
                whens[m] = jnp.where(hit, when, whens[m])
        base = base + live
    years_own = jnp.zeros((1, 1), F32)
    for m in range(tiles):
        g, c = m // per_group, m % per_group
        people[g, c] = xs[m]
        begins, lasts = whens[m][0:1], whens[m][3:4]
        span[0, g, c:c + 1, :] = begins
        span[1, g, c:c + 1, :] = begins + lasts
        years_own = years_own + jnp.sum(lasts, axis=1, keepdims=True)
    ybox[0] = jnp.broadcast_to(years_own, (8, 128))
    yc = rcopy(ybox.at[0], ybox.at[1], y_sem.at[0], y_sem.at[1], partner)
    yc.start()

    for c in near:
        c.wait_recv()

    cells = [(m, pl.ds(m * 128, 128), m * 128, r, pl.ds(r, chunk))
             for m in range(per_group) for r in range(0, num_states, chunk)]

    def row(ref, l, g):
        return [ref[l, g, m:m + 1, :] for m in range(per_group)]

    def put_row(ref, l, g, vals):
        for m in range(per_group):
            ref[l, g, m:m + 1, :] = vals[m]

    def ext_row_of(raw, i):
        return [raw[i:i + 1, m * 128:(m + 1) * 128] for m in range(per_group)]

    def piece(raw, c0, r):
        return raw[EXT + r:EXT + r + chunk, c0:c0 + 128]

    def moving(t, g):
        return [(t > a) & (t < b) for a, b in zip(row(span, 0, g), row(span, 1, g))]

    def fill_emission(l, g):
        xrow = [people[g, m, pl.ds(l, 1), :] for m in range(per_group)]
        for m, cc, c0, r, rr in cells:
            off = cols[0, rr, :] * xrow[m] - cols[1, rr, :]
            emem[l, g, rr, cc] = jnp.exp2(cols[2, rr, :] - off * off)

    def forward_step(l, t, g, raw, inv):
        fresh = [t <= a for a in row(span, 0, g)]
        for m, cc, c0, r, rr in cells:
            moved = jnp.where(fresh[m], cols[3, rr, :], piece(raw, c0, r) * inv[m])
            alph[l + 1, g, rr, cc] = (moved * emem[l, g, rr, cc]).astype(BF)

    def part_rows(k):
        return pl.ds(k * (num_states // parts), num_states // parts)

    def cross(k):
        return rcopy(alph.at[half_t, mine, part_rows(k)], alph.at[0, mine, part_rows(k)],
                     xs_sem.at[k], xr_sem.at[k], across)

    def onward(k, g):
        return rcopy(alph.at[0, g, part_rows(k)], alph.at[0, g, part_rows(k)], fs_sem.at[k], fr_sem.at[k], pair)

    def beside(k):
        return rcopy(alph.at[half_t, other, part_rows(k)], alph.at[0, other, part_rows(k)], fs_sem.at[k], fr_sem.at[k], across)

    def send_cross():
        for k in range(parts):
            cross(k).start()

    def pass_on():
        for c in rest:
            c.wait_recv()
        for k in range(parts):
            cross(k).wait_recv()
            if k < parts // 2:
                onward(k, mine).start()

    def take_other():
        for k in range(parts):
            onward(k, other).wait_recv()

    def junction(g):
        q = []
        for m in range(per_group):
            acc = jnp.zeros((chunk, 128), F32)
            for r in range(0, num_states, chunk):
                rr, cc = pl.ds(r, chunk), pl.ds(m * 128, 128)
                acc = acc + alph[half_t, g, rr, cc].astype(F32) * alph[0, g, rr, cc].astype(F32)
            q.append(jnp.sum(acc, axis=0, keepdims=True))
        return q

    def counts_copy(l):
        return rcopy(cacc.at[l], crecv.at[l], cs_sem.at[l], cr_sem.at[l], partner)

    def add_counts(l, v, last):
        if last:
            cacc[l] = cacc[l] + v
            counts_copy(l).start()
        else:
            cacc[l] = v

    def send_ll(logs):
        llbox[x * 2 + s] = jnp.broadcast_to(
            jnp.sum(jnp.sum(logs, axis=0, keepdims=True), axis=1, keepdims=True), (8, 128))
        at = x * 2 + s
        for j, dev in enumerate([partner, across, corner]):
            rcopy(llbox.at[at], llbox.at[at], lls_sem.at[j], llr_sem.at[j], dev).start()

    def finish(order):
        yc.wait()
        years = ybox[0, 0:1, 0:1] + ybox[1, 0:1, 0:1]
        factor = float(num_states * num_states * nt) / years
        at = x * 2 + s
        for j, dev in enumerate([partner, across, corner]):
            rcopy(llbox.at[at], llbox.at[at], lls_sem.at[j], llr_sem.at[j], dev).wait()
        ll = (llbox[0, 0:1, :] + llbox[1, 0:1, :]) + (llbox[2, 0:1, :] + llbox[3, 0:1, :])
        llout[...] = ll / years
        order = list(order)
        for n, l in enumerate(order):
            if n == 0:
                for k in order[:-2]:
                    counts_copy(k).wait()
            if n >= len(order) - 2:
                counts_copy(l).wait()
            w = prb[l] * (cacc[l] + crecv[l])
            total = jnp.sum(w, axis=1, keepdims=True)
            w_own = jnp.where(first_core, w[:, :half], w[:, half:])
            p_own = jnp.where(first_core, prb[l, :, :half], prb[l, :, half:])
            out[l] = factor * (w_own - p_own * total)

    @pl.when(x == 0)
    def _early():
        def first_pass(g):
            fill_emission(0, g)
            for m, cc, c0, r, rr in cells:
                alph[1, g, rr, cc] = (cols[3, rr, :] * emem[0, g, rr, cc]).astype(BF)

            @pl.loop(1, half_t)
            def _(l):
                raw = dot(mats[1, l], alph[l, g])
                fill_emission(l, g)
                sums = ext_row_of(raw, 0)
                put_row(srow, l - 1, g, sums)
                forward_step(l, l.astype(F32), g, raw, [1.0 / v for v in sums])

        first_pass(mine)
        send_cross()
        first_pass(other)
        for k in range(parts // 2, parts):
            beside(k).start()
        logs = jnp.zeros((per_group, 128), F32)
        for g in range(groups):
            put_row(srow, half_t - 1, g, ext_row_of(dot(exts[...], alph[half_t, g]), 0))
            for l in range(half_t):
                seen = (float(l) >= span[0, g]) & (float(l) < span[1, g])
                if l == half_t - 1:
                    seen = seen & (span[1, g] == float(half_t))
                logs = logs + jnp.where(seen, jnp.log(srow[l, g]), 0.0)
        irow[...] = 1.0 / srow[...]
        send_ll(logs)

        def put_u(l, t, g, get):
            on = moving(t + 1.0, g)
            gain = [jnp.where(a, b, 0.0) for a, b in zip(moving(t, g), row(irow, l - 1, g))]
            inv_s = row(irow, l, g)
            for m, cc, c0, r, rr in cells:
                y = jnp.where(on[m], get(m, cc, c0, r, rr), inv_s[m])
                back_u[l, g, rr, cc] = (emem[l, g, rr, cc] * y * gain[m]).astype(BF)

        def second_pass(g, last):
            inv_q = [1.0 / v for v in junction(g)]
            put_u(half_t - 1, float(half_t - 1), g,
                  lambda m, cc, c0, r, rr: alph[0, g, rr, cc].astype(F32) * inv_q[m])

            def counts(l):
                add_counts(l, dot_nt(alph[l, g, zrow, :], back_u[l, g]), last)

            def step(l, t, ready):
                raw = dot(mats[0, l], back_u[l, g])
                if ready:
                    counts(l + 1)
                put_u(l - 1, t - 1.0, g, lambda m, cc, c0, r, rr: piece(raw, c0, r))

            step(half_t - 1, half_t - 1.0, False)

            @pl.loop(0, half_t - 3)
            def _(k):
                l = half_t - 2 - k
                step(l, l.astype(F32), True)

            counts(2)
            counts(1)

        pass_on()
        second_pass(mine, False)
        take_other()
        second_pass(other, True)
        out[0] = jnp.zeros(out.shape[1:], F32)
        finish(range(half_t - 1, 0, -1))

    @pl.when(x == 1)
    def _late():
        top = half_t - 1

        def first_pass(g):
            fill_emission(top, g)
            for m, cc, c0, r, rr in cells:
                back_u[top, g, rr, cc] = emem[top, g, rr, cc].astype(BF)

            def back_step(l, t, put):
                raw = dot(mats[0, l], back_u[l, g])
                sums = ext_row_of(raw, 0)
                put_row(srow, l, g, sums)
                put_row(yrow, l, g, ext_row_of(raw, 1))
                inv = [1.0 / v for v in sums]
                on = moving(t, g)
                for m, cc, c0, r, rr in cells:
                    put(rr, cc, jnp.where(on[m], piece(raw, c0, r) * inv[m], 1.0))

            @pl.loop(0, top)
            def _(k):
                l = top - k
                fill_emission(l - 1, g)

                def put(rr, cc, v):
                    back_u[l - 1, g, rr, cc] = (v * emem[l - 1, g, rr, cc]).astype(BF)

                back_step(l, (l + half_t).astype(F32), put)

            def put(rr, cc, v):
                alph[half_t, g, rr, cc] = v.astype(BF)

            back_step(0, float(half_t), put)

        first_pass(mine)
        send_cross()
        first_pass(other)
        for k in range(parts // 2, parts):
            beside(k).start()
        logs = jnp.zeros((per_group, 128), F32)
        for g in range(groups):
            for l in range(half_t):
                t = float(l + half_t)
                on = (t > span[0, g]) & (t < span[1, g])
                logs = logs + jnp.where(on, jnp.log(srow[l, g]), 0.0)
                logs = logs + jnp.where(span[0, g] == t, jnp.log(yrow[l, g]), 0.0)

        def join(g):
            q = junction(g)
            put_row(span, 2, g, q)
            put_row(span, 3, g, q)
            t = float(half_t)
            return jnp.where((t > span[0, g]) & (t < span[1, g]), jnp.log(span[2, g]), 0.0)

        def second_pass(g, last):
            def weigh(l, t, sums):
                inv = [1.0 / v for v in sums]
                on = moving(t, g)
                for m in range(per_group):
                    cc = pl.ds(m * 128, 128)
                    d = jnp.where(span[0, g, m:m + 1, :] == t - 1.0, span[3, g, m:m + 1, :], span[2, g, m:m + 1, :])
                    d = d * inv[m] * srow[l, g, m:m + 1, :]
                    span[2, g, m:m + 1, :] = d
                    span[3, g, m:m + 1, :] = yrow[l, g, m:m + 1, :]
                    w = jnp.where(on[m], 1.0 / d, 0.0)
                    weighed[l, :, cc] = (alph[l, g, zrow, cc].astype(F32) * inv[m] * w).astype(BF)
                return inv

            def counts(l):
                add_counts(l, dot_nt(weighed[l], back_u[l, g]), last)

            def step(l, t, ready):
                raw = dot(mats[1, l], alph[l, g])
                if ready:
                    counts(l - 1)
                inv = weigh(l, t, ext_row_of(raw, 0))
                forward_step(l, t, g, raw, inv)

            step(0, float(half_t), False)

            @pl.loop(1, top)
            def _(l):
                step(l, (l + half_t).astype(F32), True)

            sums = ext_row_of(dot(exts[...], alph[top, g]), 0)
            counts(top - 1)
            weigh(top, float(top + half_t), sums)
            counts(top)

        pass_on()
        logs = logs + join(mine)
        second_pass(mine, False)
        take_other()
        send_ll(logs + join(other))
        second_pass(other, True)
        finish(range(half_t))

    for n, (px, dev, sends, _) in enumerate(peers):
        @pl.when(sends)
        def _():
            rcopy(pack.at[px], got.at[me_src], hs_sem.at[n], hr_sem.at[me_src], dev).wait_send()
    for d in range(2):
        @pl.when(climbs)
        def _():
            for zt in range(2, nz):
                climb(d, zt).wait_send()
    for c in near + rest:
        c.wait_send()
    for k in range(parts):
        cross(k).wait_send()
        (onward(k, mine) if k < parts // 2 else beside(k)).wait_send()


def write_out(grad, ll, out, llout):
    out[...] = grad[...]
    llout[...] = ll[0, 0:1]


def fused_device(
    earnings, starts, lengths, block_count, trans_logits, init_logits, state_mean, log_sd
):
    num_states = init_logits.shape[0]
    nt = earnings.shape[1]
    slot_rows = earnings.shape[0]
    cap = slot_rows // HB
    nz = lax.axis_size("hh")
    nsrc = nz * 2
    own_t = trans_logits.shape[0]
    half_t = nt // 2
    half = num_states // 2
    zr = num_states // nz
    lanes = 256
    groups = nsrc * HB // 2 // lanes
    wide = groups * lanes
    parts = 4
    cfg = (nz, nt, half_t, own_t, num_states, groups, lanes, parts)
    V = pltpu.VMEM
    D = pltpu.SemaphoreType.DMA
    vm = pl.BlockSpec(memory_space=pltpu.VMEM)
    sm = pl.BlockSpec(memory_space=pltpu.SMEM)
    hbm = pl.BlockSpec(memory_space=pltpu.HBM)
    pinned = lambda v: pltpu.with_memory_space_constraint(v, pltpu.HBM)
    held = lambda v: pltpu.with_memory_space_constraint(v, pltpu.VMEM)
    rows_of = V((half_t, groups, lanes // 128, 128), F32)
    grad, ll = pl.pallas_call(
        functools.partial(fused_kernel, cfg),
        out_shape=(pltpu.VMEM((half_t, zr, half), F32), pltpu.VMEM((1, 128), F32)),
        in_specs=[hbm, hbm, hbm, sm, hbm, hbm, hbm, hbm],
        out_specs=(vm, vm),
        scratch_shapes=[
            V((nt, slot_rows), F32), V((cap, HB), jnp.int32), V((cap, HB), jnp.int32), V((3, 1, num_states), F32),
            V((2, 8, 256), F32),
            V((nsrc, 8, 256), F32),
            V((groups, lanes // 128, half_t, 128), F32),
            V((4, groups, lanes // 128, 128), F32),
            V((own_t, num_states, num_states), BF),
            V((2, half_t, EXT + num_states, num_states), BF),
            V((4, num_states, 128), F32),
            V((EXT, num_states), BF),
            V((half_t + 1, groups, num_states, lanes), BF),
            V((half_t, groups, num_states, lanes), BF),
            V((half_t, groups, num_states, lanes), F32),
            rows_of, rows_of, rows_of,
            V((half_t, zr, lanes), BF),
            V((half_t, zr, num_states), F32),
            V((half_t, zr, num_states), F32),
            V((half_t, zr, num_states), F32),
            V((4, 8, 128), F32),
            V((2, 8, 128), F32),
            D((6,)), D((nsrc,)), D((nsrc,)), D((2 * own_t + 2,)), D((own_t + 2,)),
            D((parts,)), D((parts,)), D((parts,)), D((parts,)), D((half_t,)), D((half_t,)),
            D((3,)), D((3,)), D((2,)), D((2 * nz,)),
        ],
        compiler_params=pltpu.CompilerParams(
            collective_id=0, has_side_effects=True, vmem_limit_bytes=40 * 1024 * 1024),
        name="chain",
    )(pinned(earnings.T), pinned(starts.reshape(cap, HB)), pinned(lengths.reshape(cap, HB)), block_count,
      pinned(trans_logits), pinned(init_logits[None]), pinned(state_mean[None]), pinned(log_sd[None]))
    return pl.pallas_call(
        write_out,
        out_shape=(jax.ShapeDtypeStruct(grad.shape, F32), jax.ShapeDtypeStruct((1,), F32)),
        in_specs=[vm, vm],
        out_specs=(vm, vm),
        name="write_out",
    )(held(grad), held(ll))


def solution(mesh):
    fits = mesh.shape["per"] == 2 and mesh.shape["st"] == 2 and mesh.shape["hh"] == 4
    body = fused_device if fits else per_device
    placed = (
        P(("hh", "per"), None),
        P(("hh", "per")),
        P(("hh", "per")),
        P(("hh", "per")),
        P(("grp", "per", "st"), None, None),
        P("grp"),
        P("grp"),
        P("grp"),
    )
    return jax.shard_map(
        body,
        mesh=mesh,
        in_specs=placed,
        out_specs=(P(("grp", "per"), "hh", "st"), P("grp")),
        check_vma=False,
    )
```

```python
import functools

import jax
import jax.numpy as jnp
from jax import lax
from jax.sharding import PartitionSpec as P
from jax.experimental import pallas as pl
from jax.experimental.pallas import tpu as pltpu

HB = 128


top_precision = lax.Precision.HIGHEST


def emission(column, state_mean, log_sd):
    z_score = (column[:, None] - state_mean[None, :]) / jnp.exp(log_sd)[None, :]
    return jnp.exp(-0.5 * z_score * z_score - log_sd[None, :])


def per_device(
    earnings, starts, lengths, block_count, trans_logits, init_logits, state_mean, log_sd
):
    num_states = init_logits.shape[0]
    num_periods = earnings.shape[1]
    slot_rows = earnings.shape[0]
    group_size = lax.axis_size(("hh", "per"))
    core_count = lax.axis_size("st")
    half_states = num_states // core_count
    lead_state = lax.axis_index("st") * half_states
    whole_logits = lax.all_gather(trans_logits, ("per", "st"), axis=0, tiled=True)
    raised = jnp.exp(whole_logits.astype(jnp.float32))
    trans_probs = raised / jnp.sum(raised, axis=2, keepdims=True)
    raised_first = jnp.exp(init_logits)
    first_probs = raised_first / jnp.sum(raised_first)
    source_rows = slot_rows // group_size
    count_out = jnp.broadcast_to(block_count.reshape(1, 1), (1, group_size))
    got_earn, got_start, got_len, got_count = (
        lax.all_to_all(
            earnings.reshape(source_rows, group_size, num_periods),
            ("hh", "per"),
            split_axis=1,
            concat_axis=1,
            tiled=True,
        ),
        lax.all_to_all(
            starts.reshape(source_rows, group_size),
            ("hh", "per"),
            split_axis=1,
            concat_axis=1,
            tiled=True,
        ),
        lax.all_to_all(
            lengths.reshape(source_rows, group_size),
            ("hh", "per"),
            split_axis=1,
            concat_axis=1,
            tiled=True,
        ),
        lax.all_to_all(count_out, ("hh", "per"), split_axis=1, concat_axis=1, tiled=True),
    )
    per_source = got_count[0] * (HB // group_size)
    source_order = jnp.arange(group_size, dtype=jnp.int32)
    up_to = source_order[None, :] <= source_order[:, None]
    ends_at = jnp.sum(jnp.where(up_to, per_source[None, :], 0), axis=1)
    target_ids = jnp.arange(HB, dtype=jnp.int32)
    before_mask = ends_at[None, :] <= target_ids[:, None]
    source_ids = jnp.sum(before_mask.astype(jnp.int32), axis=1)
    begins_at = jnp.sum(jnp.where(before_mask, per_source[None, :], 0), axis=1)
    pick_ids = (target_ids - begins_at) * group_size + source_ids
    rows_earn = jnp.take(got_earn.reshape(source_rows * group_size, num_periods), pick_ids, axis=0)
    rows_start = jnp.take(got_start.reshape(source_rows * group_size), pick_ids)
    rows_len = jnp.take(got_len.reshape(source_rows * group_size), pick_ids)
    row_live = jnp.ones((HB,), dtype=bool)
    years_local = jnp.sum(jnp.where(row_live, rows_len, 0)).astype(jnp.float32)
    row_total_count = rows_earn.shape[0]
    columns = rows_earn.T
    period_ids = jnp.arange(num_periods, dtype=jnp.int32)

    def observed(step_now):
        return row_live & (step_now >= rows_start) & (step_now < rows_start + rows_len)

    def forward(prev_alpha, inputs):
        matrix, column, step_now = inputs
        fresh_start = (step_now <= rows_start)[:, None]
        moved_mass = jnp.dot(
            prev_alpha, matrix, precision=top_precision, preferred_element_type=jnp.float32
        )
        joint_mass = jnp.where(fresh_start, first_probs[None, :], moved_mass) * emission(
            column, state_mean, log_sd
        )
        seen_now = observed(step_now)
        scale_now = jnp.where(seen_now, jnp.sum(joint_mass, axis=1), 1.0)
        new_alpha = jnp.where(seen_now[:, None], joint_mass / scale_now[:, None], prev_alpha)
        return (new_alpha, (new_alpha, scale_now))

    start_alpha = jnp.broadcast_to(first_probs[None, :], (row_total_count, num_states))
    _, (alphas, scales) = lax.scan(forward, start_alpha, (trans_probs, columns, period_ids))

    def carry_of(back_now, column, scale_now, step_now):
        seen_now = observed(step_now)
        return jnp.where(
            seen_now[:, None],
            emission(column, state_mean, log_sd) * back_now / scale_now[:, None],
            0.0,
        )

    def backward(carry_now, inputs):
        matrix, alpha_prev, column_prev, scale_prev, step_now = inputs
        moving = row_live & (step_now > rows_start) & (step_now < rows_start + rows_len)
        weights = jnp.where(moving[:, None], alpha_prev, 0.0)
        own_carry = lax.dynamic_slice_in_dim(carry_now, lead_state, half_states, 1)
        grad_term = lax.dot_general(
            weights,
            own_carry,
            (((0,), (0,)), ((), ())),
            precision=top_precision,
            preferred_element_type=jnp.float32,
        )
        pulled = lax.dot_general(
            carry_now,
            matrix,
            (((1,), (1,)), ((), ())),
            precision=top_precision,
            preferred_element_type=jnp.float32,
        )
        back_now = jnp.where(moving[:, None], pulled, 1.0)
        return (carry_of(back_now, column_prev, scale_prev, step_now - 1), grad_term)

    ones_back = jnp.ones((row_total_count, num_states), jnp.float32)
    last_carry = carry_of(
        ones_back, columns[num_periods - 1], scales[num_periods - 1], num_periods - 1
    )
    _, grad_terms = lax.scan(
        backward,
        last_carry,
        (trans_probs[1:], alphas[:-1], columns[:-1], scales[:-1], period_ids[1:]),
        reverse=True,
    )
    zero_first = jnp.zeros((1,) + grad_terms.shape[1:], jnp.float32)
    partial_counts = jnp.concatenate([zero_first, grad_terms], axis=0)
    loglik_local = jnp.sum(jnp.log(scales))
    summed = lax.psum_scatter(partial_counts, "hh", scatter_dimension=1, tiled=True)
    summed = lax.psum_scatter(summed, "per", scatter_dimension=0, tiled=True)
    loglik_share = loglik_local / core_count
    years_share = years_local / core_count
    period_block = summed.shape[0]
    row_block_size = summed.shape[1]
    local_probs = lax.dynamic_slice(
        trans_probs,
        (lax.axis_index("per") * period_block, lax.axis_index("hh") * row_block_size, lead_state),
        (period_block, row_block_size, half_states),
    )
    weighted = local_probs * summed
    row_total, loglik_core, years_core = lax.psum(
        (jnp.sum(weighted, axis=2), loglik_share, years_share), "st"
    )
    loglik_all, years_all = lax.psum((loglik_core, years_core), ("hh", "per"))
    factor = float(num_states * num_states * num_periods) / years_all
    trans_grad = factor * (weighted - local_probs * row_total[:, :, None])
    mean_loglik = jnp.reshape(loglik_all / years_all, (1,))
    return (trans_grad, mean_loglik)


F32 = jnp.float32
BF = jnp.bfloat16
MESH = pl.DeviceIdType.MESH
EXT = 16
LOG2E = 1.4426950408889634
NT_DIMS = (((1,), (1,)), ((), ()))


def dot(p, q):
    return jnp.dot(p, q, preferred_element_type=F32)


def dot_nt(p, q):
    return lax.dot_general(p, q, NT_DIMS, preferred_element_type=F32)


def fused_kernel(cfg, earn_h, begin_h, length_h, count, logits, init_h, mean_h, sd_h, out, llout,
                 earn, begin, length, params, pack, got, people, span, lg, mats, cols, exts, alph, back_u, emem,
                 srow, irow, yrow, weighed, cacc, crecv, prb, llbox, ybox,
                 in_sem, hs_sem, hr_sem, lr_sem, ls_sem, xs_sem, xr_sem, fs_sem, fr_sem, cs_sem, cr_sem,
                 lls_sem, llr_sem, y_sem, up_sem):
    nz, nt, half_t, own_t, num_states, groups, lanes, parts = cfg
    x = lax.axis_index("per")
    z = lax.axis_index("hh")
    s = lax.axis_index("st")
    half = num_states // 2
    nsrc = nz * 2
    zr = num_states // nz
    per_group = lanes // 128
    chunk = 64
    first_core = s == 0

    def rcopy(src, dst, ss, rs, dev):
        return pltpu.make_async_remote_copy(
            src_ref=src, dst_ref=dst, send_sem=ss, recv_sem=rs,
            device_id=dev, device_id_type=MESH)

    partner = {"hh": z, "per": x, "st": 1 - s}
    across = {"hh": z, "per": 1 - x, "st": 1 - s}
    beside_core = {"hh": z, "per": 1 - x, "st": s}
    mine = lax.rem(z, 2)
    other = 1 - mine
    pair = {"hh": z + 1 - 2 * mine, "per": x, "st": 1 - s}

    def half_of(pz, px, ps):
        return lax.rem(pz + px + ps, 2)

    peers = []
    for zt in range(nz):
        for dx in range(2):
            px = x if dx == 0 else 1 - x
            dev = {"hh": zt, "per": px, "st": s}
            beside = (z == zt) & (dx == 1)
            aside = beside | (zt != z)
            sends = aside & ((z > 0) | (zt < 2))
            hears = aside & ((zt > 0) | (z < 2))
            peers.append(((px, half_of(zt, px, s)), dev, sends, hears))
    out_degree = jnp.where(z == 0, 5, nsrc + 1) + 1 + jnp.where(z == 1, 1, 0)

    loads = [pltpu.make_async_copy(src, dst, in_sem.at[i]) for i, (src, dst) in enumerate([
        (earn_h, earn), (begin_h, begin), (length_h, length),
        (init_h, params.at[0]), (mean_h, params.at[1]), (sd_h, params.at[2])])]
    for c in loads:
        c.start()
    barrier = pltpu.get_barrier_semaphore()
    for _, dev, _, hears in peers:
        @pl.when(hears)
        def _():
            pl.semaphore_signal(barrier, inc=1, device_id=dev, device_id_type=MESH)
    for dev in [partner, across, pair]:
        pl.semaphore_signal(barrier, inc=1, device_id=dev, device_id_type=MESH)

    @pl.when(z == 2)
    def _():
        pl.semaphore_signal(barrier, inc=1, device_id={"hh": 1, "per": x, "st": 1 - s}, device_id_type=MESH)
    local = []
    for i in range(own_t):
        c = pltpu.make_async_copy(logits.at[i], lg.at[i], lr_sem.at[i])
        c.start()
        local.append(c)

    low = lax.broadcasted_iota(jnp.int32, (8, 128), 1) < 64

    for c in loads[:3]:
        c.wait()
    cnt = count[0].astype(F32)
    about = jnp.concatenate(
        [begin[...].astype(F32), length[...].astype(F32), jnp.full((2, 128), 1.0, F32) * cnt], axis=0)
    about_turned = pltpu.roll(about, 64, 1)
    for h in range(2):
        e = [earn[h * half_t:(h + 1) * half_t, b * 128:(b + 1) * 128] for b in range(3)]
        turned = [pltpu.roll(v, 64, 1) for v in e]
        pack[h, 0, :, 0:128] = jnp.where(low, e[0], turned[1])
        pack[h, 0, :, 128:256] = jnp.where(low, e[2], about_turned)
        pack[h, 1, :, 0:128] = jnp.where(low, turned[0], e[1])
        pack[h, 1, :, 128:256] = jnp.where(low, turned[2], about)

    zrow = pl.ds(pl.multiple_of(z * zr, zr), zr)

    def make_probs(i):
        l = own_t * s + i
        ext = exts[...]
        eye = jnp.where(lax.broadcasted_iota(jnp.int32, (num_states, num_states), 0)
                        == lax.broadcasted_iota(jnp.int32, (num_states, num_states), 1), 1.0, 0.0).astype(BF)
        r = jnp.exp(lg[i].astype(F32))
        p = (r * (1.0 / jnp.sum(r, axis=1, keepdims=True))).astype(BF)
        mats[0, l, 0:EXT] = ext
        mats[1, l, 0:EXT] = ext
        mats[0, l, EXT:] = p
        mats[1, l, EXT:] = dot_nt(eye, p).astype(BF)
        rz = jnp.exp(lg[i, zrow, :].astype(F32))
        prb[l] = rz / jnp.sum(rz, axis=1, keepdims=True)

    def own_work():
        for c in loads[3:]:
            c.wait()
        mean = params[1]
        log_sd = params[2]
        raised_first = jnp.exp(params[0])
        first = raised_first / jnp.sum(raised_first, axis=1, keepdims=True)
        slope = jnp.exp(-log_sd) * ((0.5 * LOG2E) ** 0.5)
        for i, v in enumerate([slope, slope * mean, log_sd * (-LOG2E), first]):
            cols[i] = jnp.broadcast_to(v, (128, num_states)).T
        ext_row = lax.broadcasted_iota(jnp.int32, (EXT, num_states), 0)
        exts[...] = jnp.where(ext_row == 0, 1.0, jnp.where(
            ext_row == 1, jnp.broadcast_to(first, (EXT, num_states)), 0.0)).astype(BF)
        for c in local:
            c.wait()

        @pl.loop(0, own_t)
        def _(i):
            make_probs(i)

    own_span = pl.ds(own_t * s, own_t)
    near = []
    for i in range(own_t):
        at = (1 - x, own_t * s + i)
        near.append(rcopy(mats.at[at], mats.at[at], ls_sem.at[i], lr_sem.at[own_t + i], partner))
    rest = [rcopy(mats.at[x, own_span], mats.at[x, own_span], ls_sem.at[own_t], lr_sem.at[2 * own_t], partner),
            rcopy(prb.at[own_span], prb.at[own_span], ls_sem.at[own_t + 1], lr_sem.at[2 * own_t + 1], partner)]

    @pl.when(z < nz - 2)
    def _():
        own_work()

    pl.semaphore_wait(barrier, out_degree)

    @pl.when(z < nz - 2)
    def _():
        for c in near:
            c.start()

    me_src = z * 2 + x
    for n, (px, dev, sends, _) in enumerate(peers):
        @pl.when(sends)
        def _():
            rcopy(pack.at[px], got.at[me_src], hs_sem.at[n], hr_sem.at[me_src], dev).start()
    pltpu.make_async_copy(pack.at[x, half_of(z, x, s)], got.at[me_src], hr_sem.at[me_src]).start()

    @pl.when(z >= nz - 2)
    def _():
        own_work()
        for c in near:
            c.start()

    for c in rest:
        c.start()

    climbs = z == 1

    def climb(d, zt):
        return rcopy(got.at[d], got.at[d], up_sem.at[d * nz + zt], hr_sem.at[d], {"hh": zt, "per": x, "st": s if zt % 2 else 1 - s})

    tiles = groups * per_group
    high_bit = jnp.where(low, 0.0, 1.0)
    base = jnp.zeros((8, 128), F32)
    xs = [jnp.zeros((8, 128), F32) for _ in range(tiles)]
    whens = [jnp.zeros((8, 128), F32) for _ in range(tiles)]
    for d in range(nsrc):
        rcopy(pack.at[0, 0], got.at[d], hs_sem.at[0], hr_sem.at[d], across).wait_recv()
        if d < 2:
            @pl.when(climbs)
            def _():
                for zt in range(nz - 1, 1, -1):
                    climb(d, zt).start()
        t0, t1 = got[d, :, 0:128], got[d, :, 128:256]
        r0, r1 = pltpu.roll(t0, 64, 1), pltpu.roll(t1, 64, 1)
        held = [jnp.where(low, t0, r0), jnp.where(low, r0, t0), jnp.where(low, t1, r1)]
        about = jnp.where(low, r1, t1)
        live = jnp.broadcast_to(about[6:7], (8, 128))
        for b in range(3):
            spot = jnp.where(live > float(b), base + float(b), -2.0) - high_bit
            when = about if b == 0 else pltpu.roll(about, 8 - b, 0)
            for m in range(tiles):
                hit = spot == float(2 * m)
                xs[m] = jnp.where(hit, held[b], xs[m])
                whens[m] = jnp.where(hit, when, whens[m])
        base = base + live
    years_own = jnp.zeros((1, 1), F32)
    for m in range(tiles):
        g, c = m // per_group, m % per_group
        people[g, c] = xs[m]
        begins, lasts = whens[m][0:1], whens[m][3:4]
        span[0, g, c:c + 1, :] = begins
        span[1, g, c:c + 1, :] = begins + lasts
        years_own = years_own + jnp.sum(lasts, axis=1, keepdims=True)
    ybox[0] = jnp.broadcast_to(years_own, (8, 128))
    yc = rcopy(ybox.at[0], ybox.at[1], y_sem.at[0], y_sem.at[1], partner)
    yc.start()

    for c in near:
        c.wait_recv()

    cells = [(m, pl.ds(m * 128, 128), m * 128, r, pl.ds(r, chunk))
             for m in range(per_group) for r in range(0, num_states, chunk)]

    def row(ref, l, g):
        return [ref[l, g, m:m + 1, :] for m in range(per_group)]

    def put_row(ref, l, g, vals):
        for m in range(per_group):
            ref[l, g, m:m + 1, :] = vals[m]

    def ext_row_of(raw, i):
        return [raw[i:i + 1, m * 128:(m + 1) * 128] for m in range(per_group)]

    def piece(raw, c0, r):
        return raw[EXT + r:EXT + r + chunk, c0:c0 + 128]

    def moving(t, g):
        return [(t > a) & (t < b) for a, b in zip(row(span, 0, g), row(span, 1, g))]

    def fill_emission(l, g):
        xrow = [people[g, m, pl.ds(l, 1), :] for m in range(per_group)]
        for m, cc, c0, r, rr in cells:
            off = cols[0, rr, :] * xrow[m] - cols[1, rr, :]
            emem[l, g, rr, cc] = jnp.exp2(cols[2, rr, :] - off * off)

    def forward_step(l, t, g, raw, inv):
        fresh = [t <= a for a in row(span, 0, g)]
        for m, cc, c0, r, rr in cells:
            moved = jnp.where(fresh[m], cols[3, rr, :], piece(raw, c0, r) * inv[m])
            alph[l + 1, g, rr, cc] = (moved * emem[l, g, rr, cc]).astype(BF)

    def part_rows(k):
        return pl.ds(k * (num_states // parts), num_states // parts)

    def cross(k):
        return rcopy(alph.at[half_t, mine, part_rows(k)], alph.at[0, mine, part_rows(k)],
                     xs_sem.at[k], xr_sem.at[k], across)

    def onward(k, g):
        return rcopy(alph.at[0, g, part_rows(k)], alph.at[0, g, part_rows(k)], fs_sem.at[k], fr_sem.at[k], pair)

    def beside(k):
        return rcopy(alph.at[half_t, other, part_rows(k)], alph.at[0, other, part_rows(k)], fs_sem.at[k], fr_sem.at[k], across)

    def send_cross():
        for k in range(parts):
            cross(k).start()

    def pass_on():
        for c in rest:
            c.wait_recv()
        for k in range(parts):
            cross(k).wait_recv()
            if k < parts // 2:
                onward(k, mine).start()

    def take_other():
        for k in range(parts):
            onward(k, other).wait_recv()

    def junction(g):
        q = []
        for m in range(per_group):
            acc = jnp.zeros((chunk, 128), F32)
            for r in range(0, num_states, chunk):
                rr, cc = pl.ds(r, chunk), pl.ds(m * 128, 128)
                acc = acc + alph[half_t, g, rr, cc].astype(F32) * alph[0, g, rr, cc].astype(F32)
            q.append(jnp.sum(acc, axis=0, keepdims=True))
        return q

    def counts_copy(l):
        return rcopy(cacc.at[l], crecv.at[l], cs_sem.at[l], cr_sem.at[l], partner)

    def add_counts(l, v, last):
        if last:
            cacc[l] = cacc[l] + v
            counts_copy(l).start()
        else:
            cacc[l] = v

    def send_ll(logs):
        llbox[x * 2 + s] = jnp.broadcast_to(
            jnp.sum(jnp.sum(logs, axis=0, keepdims=True), axis=1, keepdims=True), (8, 128))
        at = x * 2 + s
        for j, dev in enumerate([partner, across, beside_core]):
            rcopy(llbox.at[at], llbox.at[at], lls_sem.at[j], llr_sem.at[j], dev).start()

    def finish(order):
        yc.wait()
        years = ybox[0, 0:1, 0:1] + ybox[1, 0:1, 0:1]
        factor = float(num_states * num_states * nt) / years
        at = x * 2 + s
        for j, dev in enumerate([partner, across, beside_core]):
            rcopy(llbox.at[at], llbox.at[at], lls_sem.at[j], llr_sem.at[j], dev).wait()
        ll = (llbox[0, 0:1, :] + llbox[1, 0:1, :]) + (llbox[2, 0:1, :] + llbox[3, 0:1, :])
        llout[...] = ll / years
        order = list(order)
        for n, l in enumerate(order):
            if n == 0:
                for k in order[:-2]:
                    counts_copy(k).wait()
            if n >= len(order) - 2:
                counts_copy(l).wait()
            w = prb[l] * (cacc[l] + crecv[l])
            total = jnp.sum(w, axis=1, keepdims=True)
            w_own = jnp.where(first_core, w[:, :half], w[:, half:])
            p_own = jnp.where(first_core, prb[l, :, :half], prb[l, :, half:])
            out[l] = factor * (w_own - p_own * total)

    @pl.when(x == 0)
    def _early():
        def first_pass(g):
            fill_emission(0, g)
            for m, cc, c0, r, rr in cells:
                alph[1, g, rr, cc] = (cols[3, rr, :] * emem[0, g, rr, cc]).astype(BF)

            @pl.loop(1, half_t)
            def _(l):
                raw = dot(mats[1, l], alph[l, g])
                fill_emission(l, g)
                sums = ext_row_of(raw, 0)
                put_row(srow, l - 1, g, sums)
                forward_step(l, l.astype(F32), g, raw, [1.0 / v for v in sums])

        first_pass(mine)
        send_cross()
        first_pass(other)
        for k in range(parts // 2, parts):
            beside(k).start()
        logs = jnp.zeros((per_group, 128), F32)
        for g in range(groups):
            put_row(srow, half_t - 1, g, ext_row_of(dot(exts[...], alph[half_t, g]), 0))
            for l in range(half_t):
                seen = (float(l) >= span[0, g]) & (float(l) < span[1, g])
                if l == half_t - 1:
                    seen = seen & (span[1, g] == float(half_t))
                logs = logs + jnp.where(seen, jnp.log(srow[l, g]), 0.0)
        irow[...] = 1.0 / srow[...]
        send_ll(logs)

        def put_u(l, t, g, get):
            on = moving(t + 1.0, g)
            gain = [jnp.where(a, b, 0.0) for a, b in zip(moving(t, g), row(irow, l - 1, g))]
            inv_s = row(irow, l, g)
            for m, cc, c0, r, rr in cells:
                y = jnp.where(on[m], get(m, cc, c0, r, rr), inv_s[m])
                back_u[l, g, rr, cc] = (emem[l, g, rr, cc] * y * gain[m]).astype(BF)

        def second_pass(g, last):
            inv_q = [1.0 / v for v in junction(g)]
            put_u(half_t - 1, float(half_t - 1), g,
                  lambda m, cc, c0, r, rr: alph[0, g, rr, cc].astype(F32) * inv_q[m])

            def counts(l):
                add_counts(l, dot_nt(alph[l, g, zrow, :], back_u[l, g]), last)

            def step(l, t, ready):
                raw = dot(mats[0, l], back_u[l, g])
                if ready:
                    counts(l + 1)
                put_u(l - 1, t - 1.0, g, lambda m, cc, c0, r, rr: piece(raw, c0, r))

            step(half_t - 1, half_t - 1.0, False)

            @pl.loop(0, half_t - 3)
            def _(k):
                l = half_t - 2 - k
                step(l, l.astype(F32), True)

            counts(2)
            counts(1)

        pass_on()
        second_pass(mine, False)
        take_other()
        second_pass(other, True)
        out[0] = jnp.zeros(out.shape[1:], F32)
        finish(range(half_t - 1, 0, -1))

    @pl.when(x == 1)
    def _late():
        top = half_t - 1

        def first_pass(g):
            fill_emission(top, g)
            for m, cc, c0, r, rr in cells:
                back_u[top, g, rr, cc] = emem[top, g, rr, cc].astype(BF)

            def back_step(l, t, put):
                raw = dot(mats[0, l], back_u[l, g])
                sums = ext_row_of(raw, 0)
                put_row(srow, l, g, sums)
                put_row(yrow, l, g, ext_row_of(raw, 1))
                inv = [1.0 / v for v in sums]
                on = moving(t, g)
                for m, cc, c0, r, rr in cells:
                    put(rr, cc, jnp.where(on[m], piece(raw, c0, r) * inv[m], 1.0))

            @pl.loop(0, top)
            def _(k):
                l = top - k
                fill_emission(l - 1, g)

                def put(rr, cc, v):
                    back_u[l - 1, g, rr, cc] = (v * emem[l - 1, g, rr, cc]).astype(BF)

                back_step(l, (l + half_t).astype(F32), put)

            def put(rr, cc, v):
                alph[half_t, g, rr, cc] = v.astype(BF)

            back_step(0, float(half_t), put)

        first_pass(mine)
        send_cross()
        first_pass(other)
        for k in range(parts // 2, parts):
            beside(k).start()
        logs = jnp.zeros((per_group, 128), F32)
        for g in range(groups):
            for l in range(half_t):
                t = float(l + half_t)
                on = (t > span[0, g]) & (t < span[1, g])
                logs = logs + jnp.where(on, jnp.log(srow[l, g]), 0.0)
                logs = logs + jnp.where(span[0, g] == t, jnp.log(yrow[l, g]), 0.0)

        def join(g):
            q = junction(g)
            put_row(span, 2, g, q)
            put_row(span, 3, g, q)
            t = float(half_t)
            return jnp.where((t > span[0, g]) & (t < span[1, g]), jnp.log(span[2, g]), 0.0)

        def second_pass(g, last):
            def weigh(l, t, sums):
                inv = [1.0 / v for v in sums]
                on = moving(t, g)
                for m in range(per_group):
                    cc = pl.ds(m * 128, 128)
                    d = jnp.where(span[0, g, m:m + 1, :] == t - 1.0, span[3, g, m:m + 1, :], span[2, g, m:m + 1, :])
                    d = d * inv[m] * srow[l, g, m:m + 1, :]
                    span[2, g, m:m + 1, :] = d
                    span[3, g, m:m + 1, :] = yrow[l, g, m:m + 1, :]
                    w = jnp.where(on[m], 1.0 / d, 0.0)
                    weighed[l, :, cc] = (alph[l, g, zrow, cc].astype(F32) * inv[m] * w).astype(BF)
                return inv

            def counts(l):
                add_counts(l, dot_nt(weighed[l], back_u[l, g]), last)

            def step(l, t, ready):
                raw = dot(mats[1, l], alph[l, g])
                if ready:
                    counts(l - 1)
                inv = weigh(l, t, ext_row_of(raw, 0))
                forward_step(l, t, g, raw, inv)

            step(0, float(half_t), False)

            @pl.loop(1, top)
            def _(l):
                step(l, (l + half_t).astype(F32), True)

            sums = ext_row_of(dot(exts[...], alph[top, g]), 0)
            counts(top - 1)
            weigh(top, float(top + half_t), sums)
            counts(top)

        pass_on()
        logs = logs + join(mine)
        second_pass(mine, False)
        take_other()
        send_ll(logs + join(other))
        second_pass(other, True)
        finish(range(half_t))

    for n, (px, dev, sends, _) in enumerate(peers):
        @pl.when(sends)
        def _():
            rcopy(pack.at[px], got.at[me_src], hs_sem.at[n], hr_sem.at[me_src], dev).wait_send()
    for d in range(2):
        @pl.when(climbs)
        def _():
            for zt in range(2, nz):
                climb(d, zt).wait_send()
    for c in near + rest:
        c.wait_send()
    for k in range(parts):
        cross(k).wait_send()
        (onward(k, mine) if k < parts // 2 else beside(k)).wait_send()


def write_out(grad, ll, out, llout):
    out[...] = grad[...]
    llout[...] = ll[0, 0:1]


def fused_device(
    earnings, starts, lengths, block_count, trans_logits, init_logits, state_mean, log_sd
):
    num_states = init_logits.shape[0]
    nt = earnings.shape[1]
    slot_rows = earnings.shape[0]
    cap = slot_rows // HB
    nz = lax.axis_size("hh")
    nsrc = nz * 2
    own_t = trans_logits.shape[0]
    half_t = nt // 2
    half = num_states // 2
    zr = num_states // nz
    lanes = 256
    groups = nsrc * HB // 2 // lanes
    wide = groups * lanes
    parts = 4
    cfg = (nz, nt, half_t, own_t, num_states, groups, lanes, parts)
    V = pltpu.VMEM
    D = pltpu.SemaphoreType.DMA
    vm = pl.BlockSpec(memory_space=pltpu.VMEM)
    sm = pl.BlockSpec(memory_space=pltpu.SMEM)
    hbm = pl.BlockSpec(memory_space=pltpu.HBM)
    pinned = lambda v: pltpu.with_memory_space_constraint(v, pltpu.HBM)
    held = lambda v: pltpu.with_memory_space_constraint(v, pltpu.VMEM)
    rows_of = V((half_t, groups, lanes // 128, 128), F32)
    grad, ll = pl.pallas_call(
        functools.partial(fused_kernel, cfg),
        out_shape=(pltpu.VMEM((half_t, zr, half), F32), pltpu.VMEM((1, 128), F32)),
        in_specs=[hbm, hbm, hbm, sm, hbm, hbm, hbm, hbm],
        out_specs=(vm, vm),
        scratch_shapes=[
            V((nt, slot_rows), F32), V((cap, HB), jnp.int32), V((cap, HB), jnp.int32), V((3, 1, num_states), F32),
            V((2, 2, 8, 256), F32),
            V((nsrc, 8, 256), F32),
            V((groups, lanes // 128, half_t, 128), F32),
            V((4, groups, lanes // 128, 128), F32),
            V((own_t, num_states, num_states), BF),
            V((2, half_t, EXT + num_states, num_states), BF),
            V((4, num_states, 128), F32),
            V((EXT, num_states), BF),
            V((half_t + 1, groups, num_states, lanes), BF),
            V((half_t, groups, num_states, lanes), BF),
            V((half_t, groups, num_states, lanes), F32),
            rows_of, rows_of, rows_of,
            V((half_t, zr, lanes), BF),
            V((half_t, zr, num_states), F32),
            V((half_t, zr, num_states), F32),
            V((half_t, zr, num_states), F32),
            V((4, 8, 128), F32),
            V((2, 8, 128), F32),
            D((6,)), D((nsrc,)), D((nsrc,)), D((2 * own_t + 2,)), D((own_t + 2,)),
            D((parts,)), D((parts,)), D((parts,)), D((parts,)), D((half_t,)), D((half_t,)),
            D((3,)), D((3,)), D((2,)), D((2 * nz,)),
        ],
        compiler_params=pltpu.CompilerParams(
            collective_id=0, has_side_effects=True, vmem_limit_bytes=40 * 1024 * 1024),
        name="chain",
    )(pinned(earnings.T), pinned(starts.reshape(cap, HB)), pinned(lengths.reshape(cap, HB)), block_count,
      pinned(trans_logits), pinned(init_logits[None]), pinned(state_mean[None]), pinned(log_sd[None]))
    return pl.pallas_call(
        write_out,
        out_shape=(jax.ShapeDtypeStruct(grad.shape, F32), jax.ShapeDtypeStruct((1,), F32)),
        in_specs=[vm, vm],
        out_specs=(vm, vm),
        name="write_out",
    )(held(grad), held(ll))


def solution(mesh):
    fits = mesh.shape["per"] == 2 and mesh.shape["st"] == 2 and mesh.shape["hh"] == 4
    body = fused_device if fits else per_device
    placed = (
        P(("hh", "per"), None),
        P(("hh", "per")),
        P(("hh", "per")),
        P(("hh", "per")),
        P(("grp", "per", "st"), None, None),
        P("grp"),
        P("grp"),
        P("grp"),
    )
    return jax.shard_map(
        body,
        mesh=mesh,
        in_specs=placed,
        out_specs=(P(("grp", "per"), "hh", "st"), P("grp")),
        check_vma=False,
    )
```

```python
import functools

import jax
import jax.numpy as jnp
from jax import lax
from jax.sharding import PartitionSpec as P
from jax.experimental import pallas as pl
from jax.experimental.pallas import tpu as pltpu

HB = 128


top_precision = lax.Precision.HIGHEST


def emission(column, state_mean, log_sd):
    z_score = (column[:, None] - state_mean[None, :]) / jnp.exp(log_sd)[None, :]
    return jnp.exp(-0.5 * z_score * z_score - log_sd[None, :])


def per_device(
    earnings, starts, lengths, block_count, trans_logits, init_logits, state_mean, log_sd
):
    num_states = init_logits.shape[0]
    num_periods = earnings.shape[1]
    slot_rows = earnings.shape[0]
    group_size = lax.axis_size(("hh", "per"))
    core_count = lax.axis_size("st")
    half_states = num_states // core_count
    lead_state = lax.axis_index("st") * half_states
    whole_logits = lax.all_gather(trans_logits, ("per", "st"), axis=0, tiled=True)
    raised = jnp.exp(whole_logits.astype(jnp.float32))
    trans_probs = raised / jnp.sum(raised, axis=2, keepdims=True)
    raised_first = jnp.exp(init_logits)
    first_probs = raised_first / jnp.sum(raised_first)
    source_rows = slot_rows // group_size
    count_out = jnp.broadcast_to(block_count.reshape(1, 1), (1, group_size))
    got_earn, got_start, got_len, got_count = (
        lax.all_to_all(
            earnings.reshape(source_rows, group_size, num_periods),
            ("hh", "per"),
            split_axis=1,
            concat_axis=1,
            tiled=True,
        ),
        lax.all_to_all(
            starts.reshape(source_rows, group_size),
            ("hh", "per"),
            split_axis=1,
            concat_axis=1,
            tiled=True,
        ),
        lax.all_to_all(
            lengths.reshape(source_rows, group_size),
            ("hh", "per"),
            split_axis=1,
            concat_axis=1,
            tiled=True,
        ),
        lax.all_to_all(count_out, ("hh", "per"), split_axis=1, concat_axis=1, tiled=True),
    )
    per_source = got_count[0] * (HB // group_size)
    source_order = jnp.arange(group_size, dtype=jnp.int32)
    up_to = source_order[None, :] <= source_order[:, None]
    ends_at = jnp.sum(jnp.where(up_to, per_source[None, :], 0), axis=1)
    target_ids = jnp.arange(HB, dtype=jnp.int32)
    before_mask = ends_at[None, :] <= target_ids[:, None]
    source_ids = jnp.sum(before_mask.astype(jnp.int32), axis=1)
    begins_at = jnp.sum(jnp.where(before_mask, per_source[None, :], 0), axis=1)
    pick_ids = (target_ids - begins_at) * group_size + source_ids
    rows_earn = jnp.take(got_earn.reshape(source_rows * group_size, num_periods), pick_ids, axis=0)
    rows_start = jnp.take(got_start.reshape(source_rows * group_size), pick_ids)
    rows_len = jnp.take(got_len.reshape(source_rows * group_size), pick_ids)
    row_live = jnp.ones((HB,), dtype=bool)
    years_local = jnp.sum(jnp.where(row_live, rows_len, 0)).astype(jnp.float32)
    row_total_count = rows_earn.shape[0]
    columns = rows_earn.T
    period_ids = jnp.arange(num_periods, dtype=jnp.int32)

    def observed(step_now):
        return row_live & (step_now >= rows_start) & (step_now < rows_start + rows_len)

    def forward(prev_alpha, inputs):
        matrix, column, step_now = inputs
        fresh_start = (step_now <= rows_start)[:, None]
        moved_mass = jnp.dot(
            prev_alpha, matrix, precision=top_precision, preferred_element_type=jnp.float32
        )
        joint_mass = jnp.where(fresh_start, first_probs[None, :], moved_mass) * emission(
            column, state_mean, log_sd
        )
        seen_now = observed(step_now)
        scale_now = jnp.where(seen_now, jnp.sum(joint_mass, axis=1), 1.0)
        new_alpha = jnp.where(seen_now[:, None], joint_mass / scale_now[:, None], prev_alpha)
        return (new_alpha, (new_alpha, scale_now))

    start_alpha = jnp.broadcast_to(first_probs[None, :], (row_total_count, num_states))
    _, (alphas, scales) = lax.scan(forward, start_alpha, (trans_probs, columns, period_ids))

    def carry_of(back_now, column, scale_now, step_now):
        seen_now = observed(step_now)
        return jnp.where(
            seen_now[:, None],
            emission(column, state_mean, log_sd) * back_now / scale_now[:, None],
            0.0,
        )

    def backward(carry_now, inputs):
        matrix, alpha_prev, column_prev, scale_prev, step_now = inputs
        moving = row_live & (step_now > rows_start) & (step_now < rows_start + rows_len)
        weights = jnp.where(moving[:, None], alpha_prev, 0.0)
        own_carry = lax.dynamic_slice_in_dim(carry_now, lead_state, half_states, 1)
        grad_term = lax.dot_general(
            weights,
            own_carry,
            (((0,), (0,)), ((), ())),
            precision=top_precision,
            preferred_element_type=jnp.float32,
        )
        pulled = lax.dot_general(
            carry_now,
            matrix,
            (((1,), (1,)), ((), ())),
            precision=top_precision,
            preferred_element_type=jnp.float32,
        )
        back_now = jnp.where(moving[:, None], pulled, 1.0)
        return (carry_of(back_now, column_prev, scale_prev, step_now - 1), grad_term)

    ones_back = jnp.ones((row_total_count, num_states), jnp.float32)
    last_carry = carry_of(
        ones_back, columns[num_periods - 1], scales[num_periods - 1], num_periods - 1
    )
    _, grad_terms = lax.scan(
        backward,
        last_carry,
        (trans_probs[1:], alphas[:-1], columns[:-1], scales[:-1], period_ids[1:]),
        reverse=True,
    )
    zero_first = jnp.zeros((1,) + grad_terms.shape[1:], jnp.float32)
    partial_counts = jnp.concatenate([zero_first, grad_terms], axis=0)
    loglik_local = jnp.sum(jnp.log(scales))
    summed = lax.psum_scatter(partial_counts, "hh", scatter_dimension=1, tiled=True)
    summed = lax.psum_scatter(summed, "per", scatter_dimension=0, tiled=True)
    loglik_share = loglik_local / core_count
    years_share = years_local / core_count
    period_block = summed.shape[0]
    row_block_size = summed.shape[1]
    local_probs = lax.dynamic_slice(
        trans_probs,
        (lax.axis_index("per") * period_block, lax.axis_index("hh") * row_block_size, lead_state),
        (period_block, row_block_size, half_states),
    )
    weighted = local_probs * summed
    row_total, loglik_core, years_core = lax.psum(
        (jnp.sum(weighted, axis=2), loglik_share, years_share), "st"
    )
    loglik_all, years_all = lax.psum((loglik_core, years_core), ("hh", "per"))
    factor = float(num_states * num_states * num_periods) / years_all
    trans_grad = factor * (weighted - local_probs * row_total[:, :, None])
    mean_loglik = jnp.reshape(loglik_all / years_all, (1,))
    return (trans_grad, mean_loglik)


F32 = jnp.float32
BF = jnp.bfloat16
MESH = pl.DeviceIdType.MESH
EXT = 16
LOG2E = 1.4426950408889634
NT_DIMS = (((1,), (1,)), ((), ()))


def dot(p, q):
    return jnp.dot(p, q, preferred_element_type=F32)


def dot_nt(p, q):
    return lax.dot_general(p, q, NT_DIMS, preferred_element_type=F32)


def fused_kernel(cfg, earn_h, begin_h, length_h, count, logits, init_h, mean_h, sd_h, out, llout,
                 earn, begin, length, params, pack, got, people, span, lg, mats, cols, exts, alph, back_u, emem,
                 srow, irow, yrow, weighed, cacc, crecv, prb, llbox, ybox,
                 in_sem, hs_sem, hr_sem, lr_sem, ls_sem, xs_sem, xr_sem, fs_sem, fr_sem, cs_sem, cr_sem,
                 lls_sem, llr_sem, y_sem, up_sem):
    nz, nt, half_t, own_t, num_states, groups, lanes, parts = cfg
    x = lax.axis_index("per")
    z = lax.axis_index("hh")
    s = lax.axis_index("st")
    half = num_states // 2
    nsrc = nz * 2
    zr = num_states // nz
    per_group = lanes // 128
    chunk = 16
    first_core = s == 0

    def rcopy(src, dst, ss, rs, dev):
        return pltpu.make_async_remote_copy(
            src_ref=src, dst_ref=dst, send_sem=ss, recv_sem=rs,
            device_id=dev, device_id_type=MESH)

    partner = {"hh": z, "per": x, "st": 1 - s}
    across = {"hh": z, "per": 1 - x, "st": 1 - s}
    beside_core = {"hh": z, "per": 1 - x, "st": s}
    mine = lax.rem(z, 2)
    other = 1 - mine
    pair = {"hh": z + 1 - 2 * mine, "per": x, "st": 1 - s}

    def half_of(pz, px, ps):
        return lax.rem(pz + px + ps, 2)

    peers = []
    for zt in range(nz):
        for dx in range(2):
            px = x if dx == 0 else 1 - x
            dev = {"hh": zt, "per": px, "st": s}
            beside = (z == zt) & (dx == 1)
            aside = beside | (zt != z)
            sends = aside & ((z > 0) | (zt < 2))
            hears = aside & ((zt > 0) | (z < 2))
            peers.append(((px, half_of(zt, px, s)), dev, sends, hears))
    out_degree = jnp.where(z == 0, 5, nsrc + 1) + 1 + jnp.where(z == 1, 1, 0)

    loads = [pltpu.make_async_copy(src, dst, in_sem.at[i]) for i, (src, dst) in enumerate([
        (earn_h, earn), (begin_h, begin), (length_h, length),
        (init_h, params.at[0]), (mean_h, params.at[1]), (sd_h, params.at[2])])]
    for c in loads[:3]:
        c.start()
    barrier = pltpu.get_barrier_semaphore()
    for _, dev, _, hears in peers:
        @pl.when(hears)
        def _():
            pl.semaphore_signal(barrier, inc=1, device_id=dev, device_id_type=MESH)
    for dev in [partner, across, pair]:
        pl.semaphore_signal(barrier, inc=1, device_id=dev, device_id_type=MESH)

    @pl.when(z == 2)
    def _():
        pl.semaphore_signal(barrier, inc=1, device_id={"hh": 1, "per": x, "st": 1 - s}, device_id_type=MESH)
    for c in loads[3:]:
        c.start()
    local = []
    for i in range(own_t):
        c = pltpu.make_async_copy(logits.at[i], lg.at[i], lr_sem.at[i])
        c.start()
        local.append(c)

    low = lax.broadcasted_iota(jnp.int32, (8, 128), 1) < 64

    for c in loads[:3]:
        c.wait()
    cnt = count[0].astype(F32)
    about = jnp.concatenate(
        [begin[...].astype(F32), length[...].astype(F32), jnp.full((2, 128), 1.0, F32) * cnt], axis=0)
    about_turned = pltpu.roll(about, 64, 1)
    for h in range(2):
        e = [earn[h * half_t:(h + 1) * half_t, b * 128:(b + 1) * 128] for b in range(3)]
        turned = [pltpu.roll(v, 64, 1) for v in e]
        pack[h, 0, :, 0:128] = jnp.where(low, e[0], turned[1])
        pack[h, 0, :, 128:256] = jnp.where(low, e[2], about_turned)
        pack[h, 1, :, 0:128] = jnp.where(low, turned[0], e[1])
        pack[h, 1, :, 128:256] = jnp.where(low, turned[2], about)

    zrow = pl.ds(pl.multiple_of(z * zr, zr), zr)

    def make_probs(i):
        l = own_t * s + i
        ext = exts[...]
        eye = jnp.where(lax.broadcasted_iota(jnp.int32, (num_states, num_states), 0)
                        == lax.broadcasted_iota(jnp.int32, (num_states, num_states), 1), 1.0, 0.0).astype(BF)
        r = jnp.exp(lg[i].astype(F32))
        p = (r * (1.0 / jnp.sum(r, axis=1, keepdims=True))).astype(BF)
        mats[0, l, 0:EXT] = ext
        mats[1, l, 0:EXT] = ext
        mats[0, l, EXT:] = p
        mats[1, l, EXT:] = dot_nt(eye, p).astype(BF)
        rz = jnp.exp(lg[i, zrow, :].astype(F32))
        prb[l] = rz / jnp.sum(rz, axis=1, keepdims=True)

    def own_work():
        for c in loads[3:]:
            c.wait()
        mean = params[1]
        log_sd = params[2]
        raised_first = jnp.exp(params[0])
        first = raised_first / jnp.sum(raised_first, axis=1, keepdims=True)
        slope = jnp.exp(-log_sd) * ((0.5 * LOG2E) ** 0.5)
        for i, v in enumerate([slope, slope * mean, log_sd * (-LOG2E), first]):
            cols[i] = jnp.broadcast_to(v, (128, num_states)).T
        ext_row = lax.broadcasted_iota(jnp.int32, (EXT, num_states), 0)
        exts[...] = jnp.where(ext_row == 0, 1.0, jnp.where(
            ext_row == 1, jnp.broadcast_to(first, (EXT, num_states)), 0.0)).astype(BF)
        for c in local:
            c.wait()

        @pl.loop(0, own_t)
        def _(i):
            make_probs(i)

    own_span = pl.ds(own_t * s, own_t)
    near = []
    for i in range(own_t):
        at = (1 - x, own_t * s + i)
        near.append(rcopy(mats.at[at], mats.at[at], ls_sem.at[i], lr_sem.at[own_t + i], partner))
    rest = [rcopy(mats.at[x, own_span], mats.at[x, own_span], ls_sem.at[own_t], lr_sem.at[2 * own_t], partner),
            rcopy(prb.at[own_span], prb.at[own_span], ls_sem.at[own_t + 1], lr_sem.at[2 * own_t + 1], partner)]

    @pl.when(z < nz - 2)
    def _():
        own_work()

    pl.semaphore_wait(barrier, out_degree)

    @pl.when(z < nz - 2)
    def _():
        for c in near:
            c.start()

    me_src = z * 2 + x
    for n, (px, dev, sends, _) in enumerate(peers):
        @pl.when(sends)
        def _():
            rcopy(pack.at[px], got.at[me_src], hs_sem.at[n], hr_sem.at[me_src], dev).start()
    pltpu.make_async_copy(pack.at[x, half_of(z, x, s)], got.at[me_src], hr_sem.at[me_src]).start()

    @pl.when(z >= nz - 2)
    def _():
        own_work()
        for c in near:
            c.start()

    for c in rest:
        c.start()

    climbs = z == 1

    def climb(d, zt):
        return rcopy(got.at[d], got.at[d], up_sem.at[d * nz + zt], hr_sem.at[d], {"hh": zt, "per": x, "st": s if zt % 2 else 1 - s})

    tiles = groups * per_group
    high_bit = jnp.where(low, 0.0, 1.0)
    base = jnp.zeros((8, 128), F32)
    xs = [jnp.zeros((8, 128), F32) for _ in range(tiles)]
    whens = [jnp.zeros((8, 128), F32) for _ in range(tiles)]
    for d in range(nsrc):
        rcopy(pack.at[0, 0], got.at[d], hs_sem.at[0], hr_sem.at[d], across).wait_recv()
        if d < 2:
            @pl.when(climbs)
            def _():
                for zt in range(nz - 1, 1, -1):
                    climb(d, zt).start()
        t0, t1 = got[d, :, 0:128], got[d, :, 128:256]
        r0, r1 = pltpu.roll(t0, 64, 1), pltpu.roll(t1, 64, 1)
        held = [jnp.where(low, t0, r0), jnp.where(low, r0, t0), jnp.where(low, t1, r1)]
        about = jnp.where(low, r1, t1)
        live = jnp.broadcast_to(about[6:7], (8, 128))
        for b in range(3):
            spot = jnp.where(live > float(b), base + float(b), -2.0) - high_bit
            when = about if b == 0 else pltpu.roll(about, 8 - b, 0)
            for m in range(tiles):
                hit = spot == float(2 * m)
                xs[m] = jnp.where(hit, held[b], xs[m])
                whens[m] = jnp.where(hit, when, whens[m])
        base = base + live
    years_own = jnp.zeros((1, 1), F32)
    for m in range(tiles):
        g, c = m // per_group, m % per_group
        people[g, c] = xs[m]
        begins, lasts = whens[m][0:1], whens[m][3:4]
        span[0, g, c:c + 1, :] = begins
        span[1, g, c:c + 1, :] = begins + lasts
        years_own = years_own + jnp.sum(lasts, axis=1, keepdims=True)
    ybox[0] = jnp.broadcast_to(years_own, (8, 128))
    yc = rcopy(ybox.at[0], ybox.at[1], y_sem.at[0], y_sem.at[1], partner)
    yc.start()

    for c in near:
        c.wait_recv()

    cells = [(m, pl.ds(m * 128, 128), m * 128, r, pl.ds(r, chunk))
             for r in range(0, num_states, chunk) for m in range(per_group)]

    def row(ref, l, g):
        return [ref[l, g, m:m + 1, :] for m in range(per_group)]

    def put_row(ref, l, g, vals):
        for m in range(per_group):
            ref[l, g, m:m + 1, :] = vals[m]

    def ext_row_of(raw, i):
        return [raw[i:i + 1, m * 128:(m + 1) * 128] for m in range(per_group)]

    def piece(raw, c0, r):
        return raw[EXT + r:EXT + r + chunk, c0:c0 + 128]

    def moving(t, g):
        return [(t > a) & (t < b) for a, b in zip(row(span, 0, g), row(span, 1, g))]

    def fill_emission(l, g):
        xrow = [people[g, m, pl.ds(l, 1), :] for m in range(per_group)]
        for m, cc, c0, r, rr in cells:
            off = cols[0, rr, :] * xrow[m] - cols[1, rr, :]
            emem[l, g, rr, cc] = jnp.exp2(cols[2, rr, :] - off * off)

    def forward_step(l, t, g, raw, inv):
        fresh = [t <= a for a in row(span, 0, g)]
        for m, cc, c0, r, rr in cells:
            moved = jnp.where(fresh[m], cols[3, rr, :], piece(raw, c0, r) * inv[m])
            alph[l + 1, g, rr, cc] = (moved * emem[l, g, rr, cc]).astype(BF)

    def part_rows(k):
        return pl.ds(k * (num_states // parts), num_states // parts)

    def cross(k):
        return rcopy(alph.at[half_t, mine, part_rows(k)], alph.at[0, mine, part_rows(k)],
                     xs_sem.at[k], xr_sem.at[k], across)

    def onward(k, g):
        return rcopy(alph.at[0, g, part_rows(k)], alph.at[0, g, part_rows(k)], fs_sem.at[k], fr_sem.at[k], pair)

    def beside(k):
        return rcopy(alph.at[half_t, other, part_rows(k)], alph.at[0, other, part_rows(k)], fs_sem.at[k], fr_sem.at[k], across)

    def send_cross():
        for k in range(parts):
            cross(k).start()

    def pass_on():
        for c in rest:
            c.wait_recv()
        for k in range(parts):
            cross(k).wait_recv()
            if k < parts // 2:
                onward(k, mine).start()

    def take_other():
        for k in range(parts):
            onward(k, other).wait_recv()

    def junction(g):
        q = []
        for m in range(per_group):
            acc = jnp.zeros((chunk, 128), F32)
            for r in range(0, num_states, chunk):
                rr, cc = pl.ds(r, chunk), pl.ds(m * 128, 128)
                acc = acc + alph[half_t, g, rr, cc].astype(F32) * alph[0, g, rr, cc].astype(F32)
            q.append(jnp.sum(acc, axis=0, keepdims=True))
        return q

    def counts_copy(l):
        return rcopy(cacc.at[l], crecv.at[l], cs_sem.at[l], cr_sem.at[l], partner)

    def add_counts(l, v, last):
        if last:
            cacc[l] = cacc[l] + v
            counts_copy(l).start()
        else:
            cacc[l] = v

    def send_ll(logs):
        llbox[x * 2 + s] = jnp.broadcast_to(
            jnp.sum(jnp.sum(logs, axis=0, keepdims=True), axis=1, keepdims=True), (8, 128))
        at = x * 2 + s
        for j, dev in enumerate([partner, across, beside_core]):
            rcopy(llbox.at[at], llbox.at[at], lls_sem.at[j], llr_sem.at[j], dev).start()

    def finish(order):
        yc.wait()
        years = ybox[0, 0:1, 0:1] + ybox[1, 0:1, 0:1]
        factor = float(num_states * num_states * nt) / years
        at = x * 2 + s
        for j, dev in enumerate([partner, across, beside_core]):
            rcopy(llbox.at[at], llbox.at[at], lls_sem.at[j], llr_sem.at[j], dev).wait()
        ll = (llbox[0, 0:1, :] + llbox[1, 0:1, :]) + (llbox[2, 0:1, :] + llbox[3, 0:1, :])
        llout[...] = ll / years
        order = list(order)
        for n, l in enumerate(order):
            if n == 0:
                for k in order[:-2]:
                    counts_copy(k).wait()
            if n >= len(order) - 2:
                counts_copy(l).wait()
            w = prb[l] * (cacc[l] + crecv[l])
            total = jnp.sum(w, axis=1, keepdims=True)
            w_own = jnp.where(first_core, w[:, :half], w[:, half:])
            p_own = jnp.where(first_core, prb[l, :, :half], prb[l, :, half:])
            out[l] = factor * (w_own - p_own * total)

    @pl.when(x == 0)
    def _early():
        def first_pass(g):
            fill_emission(0, g)
            for m, cc, c0, r, rr in cells:
                alph[1, g, rr, cc] = (cols[3, rr, :] * emem[0, g, rr, cc]).astype(BF)

            @pl.loop(1, half_t)
            def _(l):
                raw = dot(mats[1, l], alph[l, g])
                fill_emission(l, g)
                sums = ext_row_of(raw, 0)
                put_row(srow, l - 1, g, sums)
                forward_step(l, l.astype(F32), g, raw, [1.0 / v for v in sums])

        first_pass(mine)
        send_cross()
        first_pass(other)
        for k in range(parts // 2, parts):
            beside(k).start()
        logs = jnp.zeros((per_group, 128), F32)
        for g in range(groups):
            put_row(srow, half_t - 1, g, ext_row_of(dot(exts[...], alph[half_t, g]), 0))
            for l in range(half_t):
                seen = (float(l) >= span[0, g]) & (float(l) < span[1, g])
                if l == half_t - 1:
                    seen = seen & (span[1, g] == float(half_t))
                logs = logs + jnp.where(seen, jnp.log(srow[l, g]), 0.0)
        irow[...] = 1.0 / srow[...]
        send_ll(logs)

        def put_u(l, t, g, get):
            on = moving(t + 1.0, g)
            gain = [jnp.where(a, b, 0.0) for a, b in zip(moving(t, g), row(irow, l - 1, g))]
            inv_s = row(irow, l, g)
            for m, cc, c0, r, rr in cells:
                y = jnp.where(on[m], get(m, cc, c0, r, rr), inv_s[m])
                back_u[l, g, rr, cc] = (emem[l, g, rr, cc] * y * gain[m]).astype(BF)

        def second_pass(g, last):
            inv_q = [1.0 / v for v in junction(g)]
            put_u(half_t - 1, float(half_t - 1), g,
                  lambda m, cc, c0, r, rr: alph[0, g, rr, cc].astype(F32) * inv_q[m])

            def counts(l):
                add_counts(l, dot_nt(alph[l, g, zrow, :], back_u[l, g]), last)

            def step(l, t, ready):
                raw = dot(mats[0, l], back_u[l, g])
                if ready:
                    counts(l + 1)
                put_u(l - 1, t - 1.0, g, lambda m, cc, c0, r, rr: piece(raw, c0, r))

            step(half_t - 1, half_t - 1.0, False)

            @pl.loop(0, half_t - 3)
            def _(k):
                l = half_t - 2 - k
                step(l, l.astype(F32), True)

            counts(2)
            counts(1)

        pass_on()
        second_pass(mine, False)
        take_other()
        second_pass(other, True)
        out[0] = jnp.zeros(out.shape[1:], F32)
        finish(range(half_t - 1, 0, -1))

    @pl.when(x == 1)
    def _late():
        top = half_t - 1

        def first_pass(g):
            fill_emission(top, g)
            for m, cc, c0, r, rr in cells:
                back_u[top, g, rr, cc] = emem[top, g, rr, cc].astype(BF)

            def back_step(l, t, put):
                raw = dot(mats[0, l], back_u[l, g])
                sums = ext_row_of(raw, 0)
                put_row(srow, l, g, sums)
                put_row(yrow, l, g, ext_row_of(raw, 1))
                inv = [1.0 / v for v in sums]
                on = moving(t, g)
                for m, cc, c0, r, rr in cells:
                    put(rr, cc, jnp.where(on[m], piece(raw, c0, r) * inv[m], 1.0))

            @pl.loop(0, top)
            def _(k):
                l = top - k
                fill_emission(l - 1, g)

                def put(rr, cc, v):
                    back_u[l - 1, g, rr, cc] = (v * emem[l - 1, g, rr, cc]).astype(BF)

                back_step(l, (l + half_t).astype(F32), put)

            def put(rr, cc, v):
                alph[half_t, g, rr, cc] = v.astype(BF)

            back_step(0, float(half_t), put)

        first_pass(mine)
        send_cross()
        first_pass(other)
        for k in range(parts // 2, parts):
            beside(k).start()
        logs = jnp.zeros((per_group, 128), F32)
        for g in range(groups):
            for l in range(half_t):
                t = float(l + half_t)
                on = (t > span[0, g]) & (t < span[1, g])
                logs = logs + jnp.where(on, jnp.log(srow[l, g]), 0.0)
                logs = logs + jnp.where(span[0, g] == t, jnp.log(yrow[l, g]), 0.0)

        def join(g):
            q = junction(g)
            put_row(span, 2, g, q)
            put_row(span, 3, g, q)
            t = float(half_t)
            return jnp.where((t > span[0, g]) & (t < span[1, g]), jnp.log(span[2, g]), 0.0)

        def second_pass(g, last):
            def weigh(l, t, sums):
                inv = [1.0 / v for v in sums]
                on = moving(t, g)
                for m in range(per_group):
                    cc = pl.ds(m * 128, 128)
                    d = jnp.where(span[0, g, m:m + 1, :] == t - 1.0, span[3, g, m:m + 1, :], span[2, g, m:m + 1, :])
                    d = d * inv[m] * srow[l, g, m:m + 1, :]
                    span[2, g, m:m + 1, :] = d
                    span[3, g, m:m + 1, :] = yrow[l, g, m:m + 1, :]
                    w = jnp.where(on[m], 1.0 / d, 0.0)
                    weighed[l, :, cc] = (alph[l, g, zrow, cc].astype(F32) * inv[m] * w).astype(BF)
                return inv

            def counts(l):
                add_counts(l, dot_nt(weighed[l], back_u[l, g]), last)

            def step(l, t, ready):
                raw = dot(mats[1, l], alph[l, g])
                if ready:
                    counts(l - 1)
                inv = weigh(l, t, ext_row_of(raw, 0))
                forward_step(l, t, g, raw, inv)

            step(0, float(half_t), False)

            @pl.loop(1, top)
            def _(l):
                step(l, (l + half_t).astype(F32), True)

            sums = ext_row_of(dot(exts[...], alph[top, g]), 0)
            counts(top - 1)
            weigh(top, float(top + half_t), sums)
            counts(top)

        pass_on()
        logs = logs + join(mine)
        second_pass(mine, False)
        take_other()
        send_ll(logs + join(other))
        second_pass(other, True)
        finish(range(half_t))

    for n, (px, dev, sends, _) in enumerate(peers):
        @pl.when(sends)
        def _():
            rcopy(pack.at[px], got.at[me_src], hs_sem.at[n], hr_sem.at[me_src], dev).wait_send()
    for d in range(2):
        @pl.when(climbs)
        def _():
            for zt in range(2, nz):
                climb(d, zt).wait_send()
    for c in near + rest:
        c.wait_send()
    for k in range(parts):
        cross(k).wait_send()
        (onward(k, mine) if k < parts // 2 else beside(k)).wait_send()


def write_out(grad, ll, out, llout):
    out[...] = grad[...]
    llout[...] = ll[0, 0:1]


def fused_device(
    earnings, starts, lengths, block_count, trans_logits, init_logits, state_mean, log_sd
):
    num_states = init_logits.shape[0]
    nt = earnings.shape[1]
    slot_rows = earnings.shape[0]
    cap = slot_rows // HB
    nz = lax.axis_size("hh")
    nsrc = nz * 2
    own_t = trans_logits.shape[0]
    half_t = nt // 2
    half = num_states // 2
    zr = num_states // nz
    lanes = 256
    groups = nsrc * HB // 2 // lanes
    wide = groups * lanes
    parts = 4
    cfg = (nz, nt, half_t, own_t, num_states, groups, lanes, parts)
    V = pltpu.VMEM
    D = pltpu.SemaphoreType.DMA
    vm = pl.BlockSpec(memory_space=pltpu.VMEM)
    sm = pl.BlockSpec(memory_space=pltpu.SMEM)
    hbm = pl.BlockSpec(memory_space=pltpu.HBM)
    pinned = lambda v: pltpu.with_memory_space_constraint(v, pltpu.HBM)
    held = lambda v: pltpu.with_memory_space_constraint(v, pltpu.VMEM)
    rows_of = V((half_t, groups, lanes // 128, 128), F32)
    grad, ll = pl.pallas_call(
        functools.partial(fused_kernel, cfg),
        out_shape=(pltpu.VMEM((half_t, zr, half), F32), pltpu.VMEM((1, 128), F32)),
        in_specs=[hbm, hbm, hbm, sm, hbm, hbm, hbm, hbm],
        out_specs=(vm, vm),
        scratch_shapes=[
            V((nt, slot_rows), F32), V((cap, HB), jnp.int32), V((cap, HB), jnp.int32), V((3, 1, num_states), F32),
            V((2, 2, 8, 256), F32),
            V((nsrc, 8, 256), F32),
            V((groups, lanes // 128, half_t, 128), F32),
            V((4, groups, lanes // 128, 128), F32),
            V((own_t, num_states, num_states), BF),
            V((2, half_t, EXT + num_states, num_states), BF),
            V((4, num_states, 128), F32),
            V((EXT, num_states), BF),
            V((half_t + 1, groups, num_states, lanes), BF),
            V((half_t, groups, num_states, lanes), BF),
            V((half_t, groups, num_states, lanes), F32),
            rows_of, rows_of, rows_of,
            V((half_t, zr, lanes), BF),
            V((half_t, zr, num_states), F32),
            V((half_t, zr, num_states), F32),
            V((half_t, zr, num_states), F32),
            V((4, 8, 128), F32),
            V((2, 8, 128), F32),
            D((6,)), D((nsrc,)), D((nsrc,)), D((2 * own_t + 2,)), D((own_t + 2,)),
            D((parts,)), D((parts,)), D((parts,)), D((parts,)), D((half_t,)), D((half_t,)),
            D((3,)), D((3,)), D((2,)), D((2 * nz,)),
        ],
        compiler_params=pltpu.CompilerParams(
            collective_id=0, has_side_effects=True, vmem_limit_bytes=40 * 1024 * 1024),
        name="chain",
    )(pinned(earnings.T), pinned(starts.reshape(cap, HB)), pinned(lengths.reshape(cap, HB)), block_count,
      pinned(trans_logits), pinned(init_logits[None]), pinned(state_mean[None]), pinned(log_sd[None]))
    return pl.pallas_call(
        write_out,
        out_shape=(jax.ShapeDtypeStruct(grad.shape, F32), jax.ShapeDtypeStruct((1,), F32)),
        in_specs=[vm, vm],
        out_specs=(vm, vm),
        name="write_out",
    )(held(grad), held(ll))


def solution(mesh):
    fits = mesh.shape["per"] == 2 and mesh.shape["st"] == 2 and mesh.shape["hh"] == 4
    body = fused_device if fits else per_device
    placed = (
        P(("hh", "per"), None),
        P(("hh", "per")),
        P(("hh", "per")),
        P(("hh", "per")),
        P(("grp", "per", "st"), None, None),
        P("grp"),
        P("grp"),
        P("grp"),
    )
    return jax.shard_map(
        body,
        mesh=mesh,
        in_specs=placed,
        out_specs=(P(("grp", "per"), "hh", "st"), P("grp")),
        check_vma=False,
    )
```

```python
import functools

import jax
import jax.numpy as jnp
from jax import lax
from jax.sharding import PartitionSpec as P
from jax.experimental import pallas as pl
from jax.experimental.pallas import tpu as pltpu

HB = 128


top_precision = lax.Precision.HIGHEST


def emission(column, state_mean, log_sd):
    z_score = (column[:, None] - state_mean[None, :]) / jnp.exp(log_sd)[None, :]
    return jnp.exp(-0.5 * z_score * z_score - log_sd[None, :])


def per_device(
    earnings, starts, lengths, block_count, trans_logits, init_logits, state_mean, log_sd
):
    num_states = init_logits.shape[0]
    num_periods = earnings.shape[1]
    slot_rows = earnings.shape[0]
    group_size = lax.axis_size(("hh", "per"))
    core_count = lax.axis_size("st")
    half_states = num_states // core_count
    lead_state = lax.axis_index("st") * half_states
    whole_logits = lax.all_gather(trans_logits, ("per", "st"), axis=0, tiled=True)
    raised = jnp.exp(whole_logits.astype(jnp.float32))
    trans_probs = raised / jnp.sum(raised, axis=2, keepdims=True)
    raised_first = jnp.exp(init_logits)
    first_probs = raised_first / jnp.sum(raised_first)
    source_rows = slot_rows // group_size
    count_out = jnp.broadcast_to(block_count.reshape(1, 1), (1, group_size))
    got_earn, got_start, got_len, got_count = (
        lax.all_to_all(
            earnings.reshape(source_rows, group_size, num_periods),
            ("hh", "per"),
            split_axis=1,
            concat_axis=1,
            tiled=True,
        ),
        lax.all_to_all(
            starts.reshape(source_rows, group_size),
            ("hh", "per"),
            split_axis=1,
            concat_axis=1,
            tiled=True,
        ),
        lax.all_to_all(
            lengths.reshape(source_rows, group_size),
            ("hh", "per"),
            split_axis=1,
            concat_axis=1,
            tiled=True,
        ),
        lax.all_to_all(count_out, ("hh", "per"), split_axis=1, concat_axis=1, tiled=True),
    )
    per_source = got_count[0] * (HB // group_size)
    source_order = jnp.arange(group_size, dtype=jnp.int32)
    up_to = source_order[None, :] <= source_order[:, None]
    ends_at = jnp.sum(jnp.where(up_to, per_source[None, :], 0), axis=1)
    target_ids = jnp.arange(HB, dtype=jnp.int32)
    before_mask = ends_at[None, :] <= target_ids[:, None]
    source_ids = jnp.sum(before_mask.astype(jnp.int32), axis=1)
    begins_at = jnp.sum(jnp.where(before_mask, per_source[None, :], 0), axis=1)
    pick_ids = (target_ids - begins_at) * group_size + source_ids
    rows_earn = jnp.take(got_earn.reshape(source_rows * group_size, num_periods), pick_ids, axis=0)
    rows_start = jnp.take(got_start.reshape(source_rows * group_size), pick_ids)
    rows_len = jnp.take(got_len.reshape(source_rows * group_size), pick_ids)
    row_live = jnp.ones((HB,), dtype=bool)
    years_local = jnp.sum(jnp.where(row_live, rows_len, 0)).astype(jnp.float32)
    row_total_count = rows_earn.shape[0]
    columns = rows_earn.T
    period_ids = jnp.arange(num_periods, dtype=jnp.int32)

    def observed(step_now):
        return row_live & (step_now >= rows_start) & (step_now < rows_start + rows_len)

    def forward(prev_alpha, inputs):
        matrix, column, step_now = inputs
        fresh_start = (step_now <= rows_start)[:, None]
        moved_mass = jnp.dot(
            prev_alpha, matrix, precision=top_precision, preferred_element_type=jnp.float32
        )
        joint_mass = jnp.where(fresh_start, first_probs[None, :], moved_mass) * emission(
            column, state_mean, log_sd
        )
        seen_now = observed(step_now)
        scale_now = jnp.where(seen_now, jnp.sum(joint_mass, axis=1), 1.0)
        new_alpha = jnp.where(seen_now[:, None], joint_mass / scale_now[:, None], prev_alpha)
        return (new_alpha, (new_alpha, scale_now))

    start_alpha = jnp.broadcast_to(first_probs[None, :], (row_total_count, num_states))
    _, (alphas, scales) = lax.scan(forward, start_alpha, (trans_probs, columns, period_ids))

    def carry_of(back_now, column, scale_now, step_now):
        seen_now = observed(step_now)
        return jnp.where(
            seen_now[:, None],
            emission(column, state_mean, log_sd) * back_now / scale_now[:, None],
            0.0,
        )

    def backward(carry_now, inputs):
        matrix, alpha_prev, column_prev, scale_prev, step_now = inputs
        moving = row_live & (step_now > rows_start) & (step_now < rows_start + rows_len)
        weights = jnp.where(moving[:, None], alpha_prev, 0.0)
        own_carry = lax.dynamic_slice_in_dim(carry_now, lead_state, half_states, 1)
        grad_term = lax.dot_general(
            weights,
            own_carry,
            (((0,), (0,)), ((), ())),
            precision=top_precision,
            preferred_element_type=jnp.float32,
        )
        pulled = lax.dot_general(
            carry_now,
            matrix,
            (((1,), (1,)), ((), ())),
            precision=top_precision,
            preferred_element_type=jnp.float32,
        )
        back_now = jnp.where(moving[:, None], pulled, 1.0)
        return (carry_of(back_now, column_prev, scale_prev, step_now - 1), grad_term)

    ones_back = jnp.ones((row_total_count, num_states), jnp.float32)
    last_carry = carry_of(
        ones_back, columns[num_periods - 1], scales[num_periods - 1], num_periods - 1
    )
    _, grad_terms = lax.scan(
        backward,
        last_carry,
        (trans_probs[1:], alphas[:-1], columns[:-1], scales[:-1], period_ids[1:]),
        reverse=True,
    )
    zero_first = jnp.zeros((1,) + grad_terms.shape[1:], jnp.float32)
    partial_counts = jnp.concatenate([zero_first, grad_terms], axis=0)
    loglik_local = jnp.sum(jnp.log(scales))
    summed = lax.psum_scatter(partial_counts, "hh", scatter_dimension=1, tiled=True)
    summed = lax.psum_scatter(summed, "per", scatter_dimension=0, tiled=True)
    loglik_share = loglik_local / core_count
    years_share = years_local / core_count
    period_block = summed.shape[0]
    row_block_size = summed.shape[1]
    local_probs = lax.dynamic_slice(
        trans_probs,
        (lax.axis_index("per") * period_block, lax.axis_index("hh") * row_block_size, lead_state),
        (period_block, row_block_size, half_states),
    )
    weighted = local_probs * summed
    row_total, loglik_core, years_core = lax.psum(
        (jnp.sum(weighted, axis=2), loglik_share, years_share), "st"
    )
    loglik_all, years_all = lax.psum((loglik_core, years_core), ("hh", "per"))
    factor = float(num_states * num_states * num_periods) / years_all
    trans_grad = factor * (weighted - local_probs * row_total[:, :, None])
    mean_loglik = jnp.reshape(loglik_all / years_all, (1,))
    return (trans_grad, mean_loglik)


F32 = jnp.float32
BF = jnp.bfloat16
MESH = pl.DeviceIdType.MESH
EXT = 16
LOG2E = 1.4426950408889634
NT_DIMS = (((1,), (1,)), ((), ()))


def dot(p, q):
    return jnp.dot(p, q, preferred_element_type=F32)


def dot_nt(p, q):
    return lax.dot_general(p, q, NT_DIMS, preferred_element_type=F32)


def fused_kernel(cfg, earn_h, begin_h, length_h, count, logits, init_h, mean_h, sd_h, out, llout,
                 earn, begin, length, params, pack, got, people, span, lg, mats, cols, exts, alph, back_u, emem,
                 srow, irow, yrow, weighed, cacc, crecv, prb, llbox, ybox,
                 in_sem, hs_sem, hr_sem, lr_sem, ls_sem, xs_sem, xr_sem, fs_sem, fr_sem, cs_sem, cr_sem,
                 lls_sem, llr_sem, y_sem, up_sem):
    nz, nt, half_t, own_t, num_states, groups, lanes, parts = cfg
    x = lax.axis_index("per")
    z = lax.axis_index("hh")
    s = lax.axis_index("st")
    half = num_states // 2
    nsrc = nz * 2
    zr = num_states // nz
    per_group = lanes // 128
    chunk = 16
    first_core = s == 0

    def rcopy(src, dst, ss, rs, dev):
        return pltpu.make_async_remote_copy(
            src_ref=src, dst_ref=dst, send_sem=ss, recv_sem=rs,
            device_id=dev, device_id_type=MESH)

    partner = {"hh": z, "per": x, "st": 1 - s}
    across = {"hh": z, "per": 1 - x, "st": 1 - s}
    beside_core = {"hh": z, "per": 1 - x, "st": s}
    mine = lax.rem(z, 2)
    other = 1 - mine
    pair = {"hh": z + 1 - 2 * mine, "per": x, "st": 1 - s}

    def half_of(pz, px, ps):
        return lax.rem(pz + px + ps, 2)

    peers = []
    for zt in range(nz):
        for dx in range(2):
            px = x if dx == 0 else 1 - x
            dev = {"hh": zt, "per": px, "st": s}
            beside = (z == zt) & (dx == 1)
            aside = beside | (zt != z)
            sends = aside & ((z > 0) | (zt < 2))
            hears = aside & ((zt > 0) | (z < 2))
            peers.append(((px, half_of(zt, px, s)), dev, sends, hears))
    out_degree = jnp.where(z == 0, 5, nsrc + 1) + 1 + jnp.where(z == 1, 1, 0)

    loads = [pltpu.make_async_copy(src, dst, in_sem.at[i]) for i, (src, dst) in enumerate([
        (earn_h, earn), (begin_h, begin), (length_h, length),
        (init_h, params.at[0]), (mean_h, params.at[1]), (sd_h, params.at[2])])]
    for c in loads[:3]:
        c.start()
    barrier = pltpu.get_barrier_semaphore()
    for _, dev, _, hears in peers:
        @pl.when(hears)
        def _():
            pl.semaphore_signal(barrier, inc=1, device_id=dev, device_id_type=MESH)
    for dev in [partner, across, pair]:
        pl.semaphore_signal(barrier, inc=1, device_id=dev, device_id_type=MESH)

    @pl.when(z == 2)
    def _():
        pl.semaphore_signal(barrier, inc=1, device_id={"hh": 1, "per": x, "st": 1 - s}, device_id_type=MESH)
    for c in loads[3:]:
        c.start()
    local = []
    for i in range(own_t):
        c = pltpu.make_async_copy(logits.at[i], lg.at[i], lr_sem.at[i])
        c.start()
        local.append(c)

    low = lax.broadcasted_iota(jnp.int32, (8, 128), 1) < 64

    for c in loads[:3]:
        c.wait()
    cnt = count[0].astype(F32)
    about = jnp.concatenate(
        [begin[...].astype(F32), length[...].astype(F32), jnp.full((2, 128), 1.0, F32) * cnt], axis=0)
    about_turned = pltpu.roll(about, 64, 1)
    for h in range(2):
        e = [earn[h * half_t:(h + 1) * half_t, b * 128:(b + 1) * 128] for b in range(3)]
        turned = [pltpu.roll(v, 64, 1) for v in e]
        pack[h, 0, :, 0:128] = jnp.where(low, e[0], turned[1])
        pack[h, 0, :, 128:256] = jnp.where(low, e[2], about_turned)
        pack[h, 1, :, 0:128] = jnp.where(low, turned[0], e[1])
        pack[h, 1, :, 128:256] = jnp.where(low, turned[2], about)

    zrow = pl.ds(pl.multiple_of(z * zr, zr), zr)

    def make_probs(i):
        l = own_t * s + i
        ext = exts[...]
        eye = jnp.where(lax.broadcasted_iota(jnp.int32, (num_states, num_states), 0)
                        == lax.broadcasted_iota(jnp.int32, (num_states, num_states), 1), 1.0, 0.0).astype(BF)
        r = jnp.exp(lg[i].astype(F32))
        p = (r * (1.0 / jnp.sum(r, axis=1, keepdims=True))).astype(BF)
        mats[0, l, 0:EXT] = ext
        mats[1, l, 0:EXT] = ext
        mats[0, l, EXT:] = p
        mats[1, l, EXT:] = dot_nt(eye, p).astype(BF)
        rz = jnp.exp(lg[i, zrow, :].astype(F32))
        prb[l] = rz / jnp.sum(rz, axis=1, keepdims=True)

    def own_work():
        for c in loads[3:]:
            c.wait()
        mean = params[1]
        log_sd = params[2]
        raised_first = jnp.exp(params[0])
        first = raised_first / jnp.sum(raised_first, axis=1, keepdims=True)
        slope = jnp.exp(-log_sd) * ((0.5 * LOG2E) ** 0.5)
        for i, v in enumerate([slope, slope * mean, log_sd * (-LOG2E), first]):
            cols[i] = jnp.broadcast_to(v, (128, num_states)).T
        ext_row = lax.broadcasted_iota(jnp.int32, (EXT, num_states), 0)
        exts[...] = jnp.where(ext_row == 0, 1.0, jnp.where(
            ext_row == 1, jnp.broadcast_to(first, (EXT, num_states)), 0.0)).astype(BF)
        for c in local:
            c.wait()

        @pl.loop(0, own_t)
        def _(i):
            make_probs(i)

    own_span = pl.ds(own_t * s, own_t)
    near = []
    for i in range(own_t):
        at = (1 - x, own_t * s + i)
        near.append(rcopy(mats.at[at], mats.at[at], ls_sem.at[i], lr_sem.at[own_t + i], partner))
    rest = [rcopy(mats.at[x, own_span], mats.at[x, own_span], ls_sem.at[own_t], lr_sem.at[2 * own_t], partner),
            rcopy(prb.at[own_span], prb.at[own_span], ls_sem.at[own_t + 1], lr_sem.at[2 * own_t + 1], partner)]

    @pl.when(z < nz - 2)
    def _():
        own_work()

    pl.semaphore_wait(barrier, out_degree)

    @pl.when(z < nz - 2)
    def _():
        for c in near:
            c.start()

    me_src = z * 2 + x
    for n, (px, dev, sends, _) in enumerate(peers):
        @pl.when(sends)
        def _():
            rcopy(pack.at[px], got.at[me_src], hs_sem.at[n], hr_sem.at[me_src], dev).start()
    pltpu.make_async_copy(pack.at[x, half_of(z, x, s)], got.at[me_src], hr_sem.at[me_src]).start()

    @pl.when(z >= nz - 2)
    def _():
        own_work()
        for c in near:
            c.start()

    for c in rest:
        c.start()

    climbs = z == 1

    def climb(d, zt):
        return rcopy(got.at[d], got.at[d], up_sem.at[d * nz + zt], hr_sem.at[d], {"hh": zt, "per": x, "st": s if zt % 2 else 1 - s})

    tiles = groups * per_group
    high_bit = jnp.where(low, 0.0, 1.0)
    base = jnp.zeros((8, 128), F32)
    xs = [jnp.zeros((8, 128), F32) for _ in range(tiles)]
    whens = [jnp.zeros((8, 128), F32) for _ in range(tiles)]
    for d in range(nsrc):
        rcopy(pack.at[0, 0], got.at[d], hs_sem.at[0], hr_sem.at[d], across).wait_recv()
        if d < 2:
            @pl.when(climbs)
            def _():
                for zt in range(nz - 1, 1, -1):
                    climb(d, zt).start()
        t0, t1 = got[d, :, 0:128], got[d, :, 128:256]
        r0, r1 = pltpu.roll(t0, 64, 1), pltpu.roll(t1, 64, 1)
        held = [jnp.where(low, t0, r0), jnp.where(low, r0, t0), jnp.where(low, t1, r1)]
        about = jnp.where(low, r1, t1)
        live = jnp.broadcast_to(about[6:7], (8, 128))
        for b in range(3):
            spot = jnp.where(live > float(b), base + float(b), -2.0) - high_bit
            when = about if b == 0 else pltpu.roll(about, 8 - b, 0)
            for m in range(tiles):
                hit = spot == float(2 * m)
                xs[m] = jnp.where(hit, held[b], xs[m])
                whens[m] = jnp.where(hit, when, whens[m])
        base = base + live
    years_own = jnp.zeros((1, 1), F32)
    for m in range(tiles):
        g, c = m // per_group, m % per_group
        people[g, c] = xs[m]
        begins, lasts = whens[m][0:1], whens[m][3:4]
        span[0, g, c:c + 1, :] = begins
        span[1, g, c:c + 1, :] = begins + lasts
        years_own = years_own + jnp.sum(lasts, axis=1, keepdims=True)
    ybox[0] = jnp.broadcast_to(years_own, (8, 128))
    yc = rcopy(ybox.at[0], ybox.at[1], y_sem.at[0], y_sem.at[1], partner)
    yc.start()

    for c in near:
        c.wait_recv()

    cells = [(m, pl.ds(m * 128, 128), m * 128, r, pl.ds(r, chunk))
             for r in range(0, num_states, chunk) for m in range(per_group)]

    def row(ref, l, g):
        return [ref[l, g, m:m + 1, :] for m in range(per_group)]

    def put_row(ref, l, g, vals):
        for m in range(per_group):
            ref[l, g, m:m + 1, :] = vals[m]

    def ext_row_of(raw, i):
        return [raw[i:i + 1, m * 128:(m + 1) * 128] for m in range(per_group)]

    def piece(raw, c0, r):
        return raw[EXT + r:EXT + r + chunk, c0:c0 + 128]

    def moving(t, g):
        return [(t > a) & (t < b) for a, b in zip(row(span, 0, g), row(span, 1, g))]

    def fill_emission(l, g):
        xrow = [people[g, m, pl.ds(l, 1), :] for m in range(per_group)]
        for m, cc, c0, r, rr in cells:
            off = cols[0, rr, :] * xrow[m] - cols[1, rr, :]
            emem[l, g, rr, cc] = jnp.exp2(cols[2, rr, :] - off * off)

    def forward_step(l, t, g, raw, inv):
        fresh = [t <= a for a in row(span, 0, g)]
        for m, cc, c0, r, rr in cells:
            moved = jnp.where(fresh[m], cols[3, rr, :], piece(raw, c0, r) * inv[m])
            alph[l + 1, g, rr, cc] = (moved * emem[l, g, rr, cc]).astype(BF)

    def part_rows(k):
        return pl.ds(k * (num_states // parts), num_states // parts)

    def cross(k):
        return rcopy(alph.at[half_t, mine, part_rows(k)], alph.at[0, mine, part_rows(k)],
                     xs_sem.at[k], xr_sem.at[k], across)

    def onward(k, g):
        return rcopy(alph.at[0, g, part_rows(k)], alph.at[0, g, part_rows(k)], fs_sem.at[k], fr_sem.at[k], pair)

    def beside(k):
        return rcopy(alph.at[half_t, other, part_rows(k)], alph.at[0, other, part_rows(k)], fs_sem.at[k], fr_sem.at[k], across)

    def send_cross():
        for k in range(parts):
            cross(k).start()

    def pass_on():
        for c in rest:
            c.wait_recv()
        for k in range(parts):
            cross(k).wait_recv()
            if k < parts // 2:
                onward(k, mine).start()

    def take_other():
        for k in range(parts):
            onward(k, other).wait_recv()

    def junction(g):
        q = []
        for m in range(per_group):
            acc = jnp.zeros((chunk, 128), F32)
            for r in range(0, num_states, chunk):
                rr, cc = pl.ds(r, chunk), pl.ds(m * 128, 128)
                acc = acc + alph[half_t, g, rr, cc].astype(F32) * alph[0, g, rr, cc].astype(F32)
            q.append(jnp.sum(acc, axis=0, keepdims=True))
        return q

    def counts_copy(l):
        return rcopy(cacc.at[l], crecv.at[l], cs_sem.at[l], cr_sem.at[l], partner)

    def add_counts(l, v, last):
        if last:
            cacc[l] = cacc[l] + v
            counts_copy(l).start()
        else:
            cacc[l] = v

    def send_ll(logs):
        llbox[x * 2 + s] = jnp.broadcast_to(
            jnp.sum(jnp.sum(logs, axis=0, keepdims=True), axis=1, keepdims=True), (8, 128))
        at = x * 2 + s
        for j, dev in enumerate([partner, across, beside_core]):
            rcopy(llbox.at[at], llbox.at[at], lls_sem.at[j], llr_sem.at[j], dev).start()

    def finish(order):
        yc.wait()
        years = ybox[0, 0:1, 0:1] + ybox[1, 0:1, 0:1]
        factor = float(num_states * num_states * nt) / years
        at = x * 2 + s
        for j, dev in enumerate([partner, across, beside_core]):
            rcopy(llbox.at[at], llbox.at[at], lls_sem.at[j], llr_sem.at[j], dev).wait()
        ll = (llbox[0, 0:1, :] + llbox[1, 0:1, :]) + (llbox[2, 0:1, :] + llbox[3, 0:1, :])
        llout[...] = ll / years
        order = list(order)
        for n, l in enumerate(order):
            if n == 0:
                for k in order[:-1]:
                    counts_copy(k).wait()
            if n >= len(order) - 1:
                counts_copy(l).wait()
            w = prb[l] * (cacc[l] + crecv[l])
            total = jnp.sum(w, axis=1, keepdims=True)
            w_own = jnp.where(first_core, w[:, :half], w[:, half:])
            p_own = jnp.where(first_core, prb[l, :, :half], prb[l, :, half:])
            out[l] = factor * (w_own - p_own * total)

    @pl.when(x == 0)
    def _early():
        def first_pass(g):
            fill_emission(0, g)
            for m, cc, c0, r, rr in cells:
                alph[1, g, rr, cc] = (cols[3, rr, :] * emem[0, g, rr, cc]).astype(BF)

            @pl.loop(1, half_t)
            def _(l):
                raw = dot(mats[1, l], alph[l, g])
                fill_emission(l, g)
                sums = ext_row_of(raw, 0)
                put_row(srow, l - 1, g, sums)
                forward_step(l, l.astype(F32), g, raw, [1.0 / v for v in sums])

        first_pass(mine)
        send_cross()
        first_pass(other)
        for k in range(parts // 2, parts):
            beside(k).start()
        logs = jnp.zeros((per_group, 128), F32)
        for g in range(groups):
            put_row(srow, half_t - 1, g, ext_row_of(dot(exts[...], alph[half_t, g]), 0))
            for l in range(half_t):
                seen = (float(l) >= span[0, g]) & (float(l) < span[1, g])
                if l == half_t - 1:
                    seen = seen & (span[1, g] == float(half_t))
                logs = logs + jnp.where(seen, jnp.log(srow[l, g]), 0.0)
        irow[...] = 1.0 / srow[...]
        send_ll(logs)

        def put_u(l, t, g, get):
            on = moving(t + 1.0, g)
            gain = [jnp.where(a, b, 0.0) for a, b in zip(moving(t, g), row(irow, l - 1, g))]
            inv_s = row(irow, l, g)
            for m, cc, c0, r, rr in cells:
                y = jnp.where(on[m], get(m, cc, c0, r, rr), inv_s[m])
                back_u[l, g, rr, cc] = (emem[l, g, rr, cc] * y * gain[m]).astype(BF)

        def second_pass(g, last):
            inv_q = [1.0 / v for v in junction(g)]
            put_u(half_t - 1, float(half_t - 1), g,
                  lambda m, cc, c0, r, rr: alph[0, g, rr, cc].astype(F32) * inv_q[m])

            def counts(l):
                add_counts(l, dot_nt(alph[l, g, zrow, :], back_u[l, g]), last)

            def step(l, t, ready):
                raw = dot(mats[0, l], back_u[l, g])
                if ready:
                    counts(l + 1)
                put_u(l - 1, t - 1.0, g, lambda m, cc, c0, r, rr: piece(raw, c0, r))

            step(half_t - 1, half_t - 1.0, False)

            @pl.loop(0, half_t - 3)
            def _(k):
                l = half_t - 2 - k
                step(l, l.astype(F32), True)

            counts(2)
            counts(1)

        pass_on()
        second_pass(mine, False)
        take_other()
        second_pass(other, True)
        out[0] = jnp.zeros(out.shape[1:], F32)
        finish(range(half_t - 1, 0, -1))

    @pl.when(x == 1)
    def _late():
        top = half_t - 1

        def first_pass(g):
            fill_emission(top, g)
            for m, cc, c0, r, rr in cells:
                back_u[top, g, rr, cc] = emem[top, g, rr, cc].astype(BF)

            def back_step(l, t, put):
                raw = dot(mats[0, l], back_u[l, g])
                sums = ext_row_of(raw, 0)
                put_row(srow, l, g, sums)
                put_row(yrow, l, g, ext_row_of(raw, 1))
                inv = [1.0 / v for v in sums]
                on = moving(t, g)
                for m, cc, c0, r, rr in cells:
                    put(rr, cc, jnp.where(on[m], piece(raw, c0, r) * inv[m], 1.0))

            @pl.loop(0, top)
            def _(k):
                l = top - k
                fill_emission(l - 1, g)

                def put(rr, cc, v):
                    back_u[l - 1, g, rr, cc] = (v * emem[l - 1, g, rr, cc]).astype(BF)

                back_step(l, (l + half_t).astype(F32), put)

            def put(rr, cc, v):
                alph[half_t, g, rr, cc] = v.astype(BF)

            back_step(0, float(half_t), put)

        first_pass(mine)
        send_cross()
        first_pass(other)
        for k in range(parts // 2, parts):
            beside(k).start()
        logs = jnp.zeros((per_group, 128), F32)
        for g in range(groups):
            for l in range(half_t):
                t = float(l + half_t)
                on = (t > span[0, g]) & (t < span[1, g])
                logs = logs + jnp.where(on, jnp.log(srow[l, g]), 0.0)
                logs = logs + jnp.where(span[0, g] == t, jnp.log(yrow[l, g]), 0.0)

        def join(g):
            q = junction(g)
            put_row(span, 2, g, q)
            put_row(span, 3, g, q)
            t = float(half_t)
            return jnp.where((t > span[0, g]) & (t < span[1, g]), jnp.log(span[2, g]), 0.0)

        def second_pass(g, last):
            def weigh(l, t, sums):
                inv = [1.0 / v for v in sums]
                on = moving(t, g)
                for m in range(per_group):
                    cc = pl.ds(m * 128, 128)
                    d = jnp.where(span[0, g, m:m + 1, :] == t - 1.0, span[3, g, m:m + 1, :], span[2, g, m:m + 1, :])
                    d = d * inv[m] * srow[l, g, m:m + 1, :]
                    span[2, g, m:m + 1, :] = d
                    span[3, g, m:m + 1, :] = yrow[l, g, m:m + 1, :]
                    w = jnp.where(on[m], 1.0 / d, 0.0)
                    weighed[l, :, cc] = (alph[l, g, zrow, cc].astype(F32) * inv[m] * w).astype(BF)
                return inv

            def counts(l):
                add_counts(l, dot_nt(weighed[l], back_u[l, g]), last)

            def step(l, t, ready):
                raw = dot(mats[1, l], alph[l, g])
                if ready:
                    counts(l - 1)
                inv = weigh(l, t, ext_row_of(raw, 0))
                forward_step(l, t, g, raw, inv)

            step(0, float(half_t), False)

            @pl.loop(1, top)
            def _(l):
                step(l, (l + half_t).astype(F32), True)

            sums = ext_row_of(dot(exts[...], alph[top, g]), 0)
            counts(top - 1)
            weigh(top, float(top + half_t), sums)
            counts(top)

        pass_on()
        logs = logs + join(mine)
        second_pass(mine, False)
        take_other()
        send_ll(logs + join(other))
        second_pass(other, True)
        finish(range(half_t))

    for n, (px, dev, sends, _) in enumerate(peers):
        @pl.when(sends)
        def _():
            rcopy(pack.at[px], got.at[me_src], hs_sem.at[n], hr_sem.at[me_src], dev).wait_send()
    for d in range(2):
        @pl.when(climbs)
        def _():
            for zt in range(2, nz):
                climb(d, zt).wait_send()
    for c in near + rest:
        c.wait_send()
    for k in range(parts):
        cross(k).wait_send()
        (onward(k, mine) if k < parts // 2 else beside(k)).wait_send()


def write_out(grad, ll, out, llout):
    out[...] = grad[...]
    llout[...] = ll[0, 0:1]


def fused_device(
    earnings, starts, lengths, block_count, trans_logits, init_logits, state_mean, log_sd
):
    num_states = init_logits.shape[0]
    nt = earnings.shape[1]
    slot_rows = earnings.shape[0]
    cap = slot_rows // HB
    nz = lax.axis_size("hh")
    nsrc = nz * 2
    own_t = trans_logits.shape[0]
    half_t = nt // 2
    half = num_states // 2
    zr = num_states // nz
    lanes = 256
    groups = nsrc * HB // 2 // lanes
    wide = groups * lanes
    parts = 4
    cfg = (nz, nt, half_t, own_t, num_states, groups, lanes, parts)
    V = pltpu.VMEM
    D = pltpu.SemaphoreType.DMA
    vm = pl.BlockSpec(memory_space=pltpu.VMEM)
    sm = pl.BlockSpec(memory_space=pltpu.SMEM)
    hbm = pl.BlockSpec(memory_space=pltpu.HBM)
    pinned = lambda v: pltpu.with_memory_space_constraint(v, pltpu.HBM)
    held = lambda v: pltpu.with_memory_space_constraint(v, pltpu.VMEM)
    rows_of = V((half_t, groups, lanes // 128, 128), F32)
    grad, ll = pl.pallas_call(
        functools.partial(fused_kernel, cfg),
        out_shape=(pltpu.VMEM((half_t, zr, half), F32), pltpu.VMEM((1, 128), F32)),
        in_specs=[hbm, hbm, hbm, sm, hbm, hbm, hbm, hbm],
        out_specs=(vm, vm),
        scratch_shapes=[
            V((nt, slot_rows), F32), V((cap, HB), jnp.int32), V((cap, HB), jnp.int32), V((3, 1, num_states), F32),
            V((2, 2, 8, 256), F32),
            V((nsrc, 8, 256), F32),
            V((groups, lanes // 128, half_t, 128), F32),
            V((4, groups, lanes // 128, 128), F32),
            V((own_t, num_states, num_states), BF),
            V((2, half_t, EXT + num_states, num_states), BF),
            V((4, num_states, 128), F32),
            V((EXT, num_states), BF),
            V((half_t + 1, groups, num_states, lanes), BF),
            V((half_t, groups, num_states, lanes), BF),
            V((half_t, groups, num_states, lanes), F32),
            rows_of, rows_of, rows_of,
            V((half_t, zr, lanes), BF),
            V((half_t, zr, num_states), F32),
            V((half_t, zr, num_states), F32),
            V((half_t, zr, num_states), F32),
            V((4, 8, 128), F32),
            V((2, 8, 128), F32),
            D((6,)), D((nsrc,)), D((nsrc,)), D((2 * own_t + 2,)), D((own_t + 2,)),
            D((parts,)), D((parts,)), D((parts,)), D((parts,)), D((half_t,)), D((half_t,)),
            D((3,)), D((3,)), D((2,)), D((2 * nz,)),
        ],
        compiler_params=pltpu.CompilerParams(
            collective_id=0, has_side_effects=True, vmem_limit_bytes=40 * 1024 * 1024),
        name="chain",
    )(pinned(earnings.T), pinned(starts.reshape(cap, HB)), pinned(lengths.reshape(cap, HB)), block_count,
      pinned(trans_logits), pinned(init_logits[None]), pinned(state_mean[None]), pinned(log_sd[None]))
    return pl.pallas_call(
        write_out,
        out_shape=(jax.ShapeDtypeStruct(grad.shape, F32), jax.ShapeDtypeStruct((1,), F32)),
        in_specs=[vm, vm],
        out_specs=(vm, vm),
        name="write_out",
    )(held(grad), held(ll))


def solution(mesh):
    fits = mesh.shape["per"] == 2 and mesh.shape["st"] == 2 and mesh.shape["hh"] == 4
    body = fused_device if fits else per_device
    placed = (
        P(("hh", "per"), None),
        P(("hh", "per")),
        P(("hh", "per")),
        P(("hh", "per")),
        P(("grp", "per", "st"), None, None),
        P("grp"),
        P("grp"),
        P("grp"),
    )
    return jax.shard_map(
        body,
        mesh=mesh,
        in_specs=placed,
        out_specs=(P(("grp", "per"), "hh", "st"), P("grp")),
        check_vma=False,
    )
```
